256 devices in a mesh: lat: 8 (over x_hi, y), lon: 32 (over z, x_lo, core).
Axes of the slice: x: 4 (x_hi: 2, x_lo: 2; x = x_hi * 2 + x_lo), y: 4, z: 8, core: 2. Of those that a mesh axis runs over, the one named last changes fastest.
Arguments:
- state_field: bfloat16 [16, 2880, 512], P('lat', 'lon'), may hold values from -32 to 32
- cotangent: bfloat16 [16, 2880, 512], P('lat', 'lon'), may hold values from -6 to 6
- key_bias: bfloat16 [16, 2880, 16], P('lat', 'lon'), may hold values from -3 to 250
- input_gain: float32 [512], replicated, may hold values from 0.1 to 1.9
- expand_weight: bfloat16 [512, 2048], replicated, may hold values from -0.25 to 0.25
- depth_weight: bfloat16 [3, 3, 2048], replicated, may hold values from -2 to 2
- shrink_weight: bfloat16 [2048, 512], replicated, may hold values from -0.125 to 0.125
- attention_gain: float32 [512], replicated, may hold values from 0.1 to 1.9
- attention_in: bfloat16 [512, 1536], replicated, may hold values from -0.25 to 0.25
- attention_out: bfloat16 [512, 512], replicated, may hold values from -0.25 to 0.25
Outputs:
- output_field: bfloat16 [16, 2880, 512], P('lat', 'lon')
- input_grad: bfloat16 [16, 2880, 512], P('lat', 'lon')
- expand_grad: float32 [512, 2048], P('lat', 'lon')
- shrink_grad: float32 [2048, 512], P('lat', 'lon')
- attention_in_grad: float32 [512, 1536], P('lat', 'lon')
- attention_out_grad: float32 [512, 512], P('lat', 'lon')
- depth_grad: float32 [3, 3, 2048], replicated
- input_gain_grad: float32 [512], replicated
- attention_gain_grad: float32 [512], replicated
The draws below stay inside these ranges and needn't reach their ends.
All inputs are finite; a program needn't handle non-finite values.
Results may differ from the reference program's by a relative error of at most 0.035.
Values may be sent and summed in bfloat16 or wider, within the bound.
A program may use at most 128 MiB of HBM per device.

```python
import math
import jax
import jax.numpy as jnp
from jax import lax

ROWS_DEV = 2
C = 512
HEADS = 16
HEAD_DIM = 32
WIDE = 2048
LAT = 16
LON = 2880


def draw_state_field(key, part):
    base_key, channel_key, cell_key = jax.random.split(key, 3)
    grid_shape = (LAT, LON, C)
    base_values = jnp.clip(jax.random.normal(base_key, grid_shape, jnp.float32), -3.5, 3.5)
    lower_log = math.log(0.3)
    upper_log = math.log(3.0)
    channel_scale = jnp.exp(jax.random.uniform(channel_key, (1, 1, C), jnp.float32, lower_log, upper_log))
    cell_scale = jnp.exp(jax.random.uniform(cell_key, (LAT, LON, 1), jnp.float32, lower_log, upper_log))
    return (base_values * channel_scale * cell_scale).astype(jnp.bfloat16)


def draw_key_bias(key, part):
    base_key = jax.random.fold_in(key, 0)
    base_values = jax.random.uniform(base_key, (LAT, LON, HEADS), jnp.float32, -3.0, 3.0)
    return base_values.astype(jnp.bfloat16)


def shard_levels(rng, shape, cuts, low, high):
    loudness = 1.0
    for dim, blocks in cuts:
        steps = jax.random.uniform(jax.random.fold_in(jax.random.fold_in(rng, 6), dim), (blocks,), jnp.float32, low / len(cuts), high / len(cuts))
        loudness = loudness * jnp.repeat(jnp.exp(steps), shape[dim] // blocks).reshape((-1,) + (1,) * (len(shape) - 1 - dim))
    return loudness


def normal_values(stream_key, shape, scale, limit, shards=(), kind=jnp.bfloat16):
    values = scale * jax.random.normal(stream_key, shape, jnp.float32)
    if shards:
        values = values * shard_levels(stream_key, shape, shards, -0.22, 0.18)
    return jnp.clip(values, -limit, limit).astype(kind)


def setup_inputs(seed: int = 0) -> dict:
    streams_of = jax.random.split(jax.random.key(seed), 11)
    return {
        "state_field": draw_state_field(jax.random.fold_in(streams_of[10], 71), 0),
        "cotangent": normal_values(streams_of[1], (LAT, LON, C), 1.0, 6.0, ((0, 8), (1, 32))),
        "key_bias": draw_key_bias(jax.random.fold_in(streams_of[10], 71), 0),
        "input_gain": jnp.clip(1.0 + 0.18 * jax.random.normal(streams_of[3], (C,), jnp.float32), 0.1, 1.9),
        "expand_weight": normal_values(streams_of[4], (C, WIDE), C ** -0.5, 0.25),
        "depth_weight": normal_values(streams_of[5], (3, 3, WIDE), 9 ** -0.5, 2.0),
        "shrink_weight": normal_values(streams_of[6], (WIDE, C), WIDE ** -0.5, 0.125),
        "attention_gain": jnp.clip(1.0 + 0.18 * jax.random.normal(streams_of[7], (C,), jnp.float32), 0.1, 1.9),
        "attention_in": normal_values(streams_of[8], (C, 3 * C), C ** -0.5, 0.25),
        "attention_out": normal_values(streams_of[9], (C, C), C ** -0.5, 0.25),
    }


EPSILON = 1e-06

def inverse_rms(values):
    return lax.rsqrt(lax.optimization_barrier(jnp.mean(values * values, axis=-1, keepdims=True)) + EPSILON)

def silu_slope(values):
    sigmoid = jax.nn.sigmoid(values)
    return sigmoid * (1.0 + values * (1.0 - sigmoid))

def rounded(values):
    return lax.optimization_barrier(values.astype(jnp.bfloat16)).astype(jnp.float32)

def wrap_longitude(values):
    return jnp.concatenate([values[:, -1:], values, values[:, :1]], axis=1)

def depthwise_sum(padded, weights, row_count, lon_count):
    total = jnp.zeros((row_count, lon_count, padded.shape[2]), jnp.float32)
    for lat_step in range(3):
        for lon_step in range(3):
            total = total + weights[lat_step, lon_step].astype(jnp.float32) * padded[lat_step:lat_step + row_count, lon_step:lon_step + lon_count].astype(jnp.float32)
    return total

def transposed_sum(padded, weights, row_count, lon_count):
    total = jnp.zeros((row_count, lon_count, padded.shape[2]), jnp.float32)
    for lat_step in range(3):
        for lon_step in range(3):
            total = total + weights[lat_step, lon_step].astype(jnp.float32) * padded[2 - lat_step:2 - lat_step + row_count, 2 - lon_step:2 - lon_step + lon_count].astype(jnp.float32)
    return total

def norm_back(back_normed, state, inverse, gain):
    scaled = back_normed * gain
    return inverse * scaled - inverse * inverse * inverse * state * lax.optimization_barrier(jnp.mean(scaled * state, axis=-1, keepdims=True))

def reference(state_field, cotangent, key_bias, input_gain, expand_weight, depth_weight, shrink_weight, attention_gain, attention_in, attention_out):
    norm_factor = 1.0 / math.sqrt(LAT * LON)
    score_scale = 1.0 / math.sqrt(HEAD_DIM)
    band_count = LAT // ROWS_DEV
    state_float = state_field.astype(jnp.float32)
    inverse_first = inverse_rms(state_float)
    normed = (state_float * inverse_first * input_gain).astype(jnp.bfloat16)
    normed_pad = jnp.pad(normed, ((2, 2), (0, 0), (0, 0)))
    band_ids = jnp.arange(band_count, dtype=jnp.int32)

    def band_forward(band):
        start_row = band * ROWS_DEV
        block_rows = lax.dynamic_slice_in_dim(normed_pad, start_row + 1, ROWS_DEV + 2, 0)
        activated = jax.nn.silu(jnp.dot(block_rows, expand_weight, preferred_element_type=jnp.float32)).astype(jnp.bfloat16)
        convolved = depthwise_sum(wrap_longitude(activated), depth_weight, ROWS_DEV, LON)
        mixed = jax.nn.silu(convolved).astype(jnp.bfloat16)
        own_rows = lax.dynamic_slice_in_dim(state_float, start_row, ROWS_DEV, 0)
        return (own_rows + jnp.dot(mixed, shrink_weight, preferred_element_type=jnp.float32)).astype(jnp.bfloat16)
    inner_state = lax.map(band_forward, band_ids).reshape(LAT, LON, C)

    def row_step(carry, operands):
        in_total, out_total, gain_total = carry
        inner_row, back_row, bias_row = operands
        inner_float = inner_row.astype(jnp.float32)
        inverse_second = inverse_rms(inner_float)
        normed_second = (inner_float * inverse_second * attention_gain).astype(jnp.bfloat16)
        projected = rounded(jnp.dot(normed_second, attention_in, preferred_element_type=jnp.float32))
        queries = projected[:, :C].reshape(LON, HEADS, HEAD_DIM)
        keys_all = projected[:, C:2 * C].reshape(LON, HEADS, HEAD_DIM)
        values_all = projected[:, 2 * C:].reshape(LON, HEADS, HEAD_DIM)
        bias_float = bias_row.astype(jnp.float32).T[:, None, :]
        scores = jnp.einsum('qhd,khd->hqk', queries, keys_all) * score_scale + bias_float
        highest = lax.optimization_barrier(jnp.max(scores, axis=-1, keepdims=True))
        exponent = jnp.exp(scores - highest)
        probs_float = exponent / lax.optimization_barrier(jnp.sum(exponent, axis=-1, keepdims=True))
        probs_low = rounded(probs_float)
        heads_field = jnp.einsum('hqk,khd->qhd', probs_low, values_all).reshape(LON, C).astype(jnp.bfloat16)
        output_row = (inner_float + jnp.dot(heads_field, attention_out, preferred_element_type=jnp.float32)).astype(jnp.bfloat16)
        out_total = out_total + jnp.dot(heads_field.T, back_row, preferred_element_type=jnp.float32) * norm_factor
        back_heads = rounded(jnp.dot(back_row, attention_out.T, preferred_element_type=jnp.float32)).reshape(LON, HEADS, HEAD_DIM)
        back_probs = jnp.einsum('qhd,khd->hqk', back_heads, values_all)
        centred = lax.optimization_barrier(jnp.sum(probs_float * back_probs, axis=-1, keepdims=True))
        back_scores = rounded(probs_float * (back_probs - centred))
        back_queries = (jnp.einsum('hqk,khd->qhd', back_scores, keys_all) * score_scale).astype(jnp.bfloat16)
        back_keys = (jnp.einsum('hqk,qhd->khd', back_scores, queries) * score_scale).astype(jnp.bfloat16)
        back_values = jnp.einsum('hqk,qhd->khd', probs_low, back_heads).astype(jnp.bfloat16)
        back_projected = jnp.concatenate([back_queries.reshape(LON, C), back_keys.reshape(LON, C), back_values.reshape(LON, C)], axis=-1)
        in_total = in_total + jnp.dot(normed_second.T, back_projected, preferred_element_type=jnp.float32) * norm_factor
        back_second = jnp.dot(back_projected, attention_in.T, preferred_element_type=jnp.float32)
        gain_total = gain_total + lax.optimization_barrier(jnp.sum(back_second * inner_float * inverse_second, axis=0)) * norm_factor
        back_inner = (back_row.astype(jnp.float32) + norm_back(back_second, inner_float, inverse_second, attention_gain)).astype(jnp.bfloat16)
        return ((in_total, out_total, gain_total), (output_row, back_inner))
    row_start = (jnp.zeros((C, 3 * C), jnp.float32), jnp.zeros((C, C), jnp.float32), jnp.zeros((C,), jnp.float32))
    row_final, row_outputs = lax.scan(row_step, row_start, (inner_state, cotangent, key_bias))
    in_grad, out_grad, gain_two = row_final
    output_field, back_inner = row_outputs
    back_inner_pad = jnp.pad(back_inner, ((1, 1), (0, 0), (0, 0)))

    def band_back(carry, band):
        expand_total, shrink_total, depth_total, gain_total = carry
        start_row = band * ROWS_DEV
        block_rows = lax.dynamic_slice_in_dim(normed_pad, start_row, ROWS_DEV + 4, 0)
        expanded = jnp.dot(block_rows, expand_weight, preferred_element_type=jnp.float32)
        activated = wrap_longitude(jax.nn.silu(expanded).astype(jnp.bfloat16))
        convolved = depthwise_sum(activated, depth_weight, ROWS_DEV + 2, LON)
        mixed = jax.nn.silu(convolved[1:-1]).astype(jnp.bfloat16)
        back_rows = lax.dynamic_slice_in_dim(back_inner_pad, start_row, ROWS_DEV + 2, 0)
        back_convolved = (jnp.dot(back_rows, shrink_weight.T, preferred_element_type=jnp.float32) * silu_slope(convolved)).astype(jnp.bfloat16)
        back_activated = transposed_sum(wrap_longitude(back_convolved), depth_weight, ROWS_DEV, LON)
        centre = back_convolved[1:-1].astype(jnp.float32)
        depth_terms = jnp.stack([jnp.stack([lax.optimization_barrier(jnp.sum(activated[lat_step + 1:lat_step + 1 + ROWS_DEV, lon_step:lon_step + LON].astype(jnp.float32) * centre, axis=(0, 1))) for lon_step in range(3)]) for lat_step in range(3)])
        depth_total = depth_total + depth_terms * norm_factor
        own_back = back_rows[1:-1]
        shrink_total = shrink_total + jnp.dot(mixed.reshape(-1, WIDE).T, own_back.reshape(-1, C), preferred_element_type=jnp.float32) * norm_factor
        back_expanded = (back_activated * silu_slope(expanded[2:-2])).astype(jnp.bfloat16)
        expand_total = expand_total + jnp.dot(block_rows[2:-2].reshape(-1, C).T, back_expanded.reshape(-1, WIDE), preferred_element_type=jnp.float32) * norm_factor
        back_normed = jnp.dot(back_expanded, expand_weight.T, preferred_element_type=jnp.float32)
        own_rows = lax.dynamic_slice_in_dim(state_float, start_row, ROWS_DEV, 0)
        inverse_own = inverse_rms(own_rows)
        gain_total = gain_total + lax.optimization_barrier(jnp.sum(back_normed * own_rows * inverse_own, axis=(0, 1))) * norm_factor
        band_grad = (own_back.astype(jnp.float32) + norm_back(back_normed, own_rows, inverse_own, input_gain)).astype(jnp.bfloat16)
        return ((expand_total, shrink_total, depth_total, gain_total), band_grad)
    band_start = (jnp.zeros((C, WIDE), jnp.float32), jnp.zeros((WIDE, C), jnp.float32), jnp.zeros((3, 3, WIDE), jnp.float32), jnp.zeros((C,), jnp.float32))
    band_final, grad_bands = lax.scan(band_back, band_start, band_ids)
    expand_grad, shrink_grad, depth_grad, gain_one = band_final
    input_grad = grad_bands.reshape(LAT, LON, C)
    return (output_field, input_grad, expand_grad, shrink_grad, in_grad, out_grad, depth_grad, gain_one, gain_two)
```

```python
import functools
import math

import jax
import jax.numpy as jnp
from jax import lax
from jax.experimental import pallas as pl
from jax.experimental.pallas import tpu as pltpu
from jax.sharding import PartitionSpec as P

EPSILON = 1e-06


def with_halo(block, sides, width, periodic):
    for axis, dim in sides:
        count = lax.axis_size(axis)
        forward = [(i, i + 1) for i in range(count - 1)]
        if periodic:
            forward.append((count - 1, 0))
        backward = [(target, source) for source, target in forward]
        low = lax.ppermute(
            lax.slice_in_dim(block, block.shape[dim] - width, None, axis=dim), axis, forward
        )
        high = lax.ppermute(lax.slice_in_dim(block, 0, width, axis=dim), axis, backward)
        block = jnp.concatenate([low, block, high], axis=dim)
    return block


def inverse_rms(values):
    return lax.rsqrt(jnp.mean(values * values, axis=-1, keepdims=True) + EPSILON)


def silu_slope(values):
    sigmoid = jax.nn.sigmoid(values)
    return sigmoid * (1.0 + values * (1.0 - sigmoid))


def depthwise_sum(padded, weights, row_count, lon_count):
    total = jnp.zeros((row_count, lon_count, padded.shape[2]), jnp.float32)
    for lat_step in range(3):
        for lon_step in range(3):
            total = total + weights[lat_step, lon_step].astype(jnp.float32) * padded[
                lat_step : lat_step + row_count, lon_step : lon_step + lon_count
            ].astype(jnp.float32)
    return total


def transposed_sum(padded, weights, row_count, lon_count):
    total = jnp.zeros((row_count, lon_count, padded.shape[2]), jnp.float32)
    for lat_step in range(3):
        for lon_step in range(3):
            total = total + weights[lat_step, lon_step].astype(jnp.float32) * padded[
                2 - lat_step : 2 - lat_step + row_count, 2 - lon_step : 2 - lon_step + lon_count
            ].astype(jnp.float32)
    return total


def times_transpose(values, weights):
    return lax.dot_general(
        values, weights, (((values.ndim - 1,), (1,)), ((), ())), preferred_element_type=jnp.float32
    )


def norm_back(back_normed, state, inverse, gain):
    scaled = back_normed * gain
    return inverse * scaled - inverse * inverse * inverse * state * jnp.mean(
        scaled * state, axis=-1, keepdims=True
    )


CELLS = 96


def attend_kernel(valid, scale, x_ref, out_ref, xt_ref, kaug_ref, vaug_ref, t_ref, pb_ref, acc_ref, qo_ref):
    sources = x_ref.shape[0]
    total = sources * CELLS
    block = 256
    step = 512 if total % 512 == 0 else 256
    log2e = 1.4426950408889634
    to_log2 = scale * log2e
    f32, bf16 = jnp.float32, jnp.bfloat16

    def prepare(index, carry):
        raw = x_ref[index].astype(f32)
        row = lax.broadcasted_iota(jnp.int32, (CELLS, 128), 0)
        lane = lax.broadcasted_iota(jnp.int32, (CELLS, 128), 1)
        bias_row = jnp.broadcast_to(raw[valid : valid + 1, :], (CELLS, 128))
        bias = jnp.sum(jnp.where(row == lane, bias_row, 0.0), axis=1, keepdims=True) * log2e
        bias = jnp.broadcast_to(bias, (CELLS, 128))
        first = bias.astype(bf16).astype(f32)
        second = (bias - first).astype(bf16).astype(f32)
        third = bias - first - second
        first = jnp.where(row < valid, first, -1e30)
        second = jnp.where(row < valid, second, 0.0)
        third = jnp.where(row < valid, third, 0.0)
        cell = jnp.where(row < valid, raw, 0.0)
        key = jnp.where((lane >= 32) & (lane < 64), cell, 0.0)
        value = jnp.where((lane >= 64) & (lane < 96), cell, 0.0)
        keys = pltpu.roll(key, 96, 1) + key + pltpu.roll(key, 32, 1)
        keys = jnp.where(lane == 96, first, keys)
        keys = jnp.where(lane == 97, second, keys)
        keys = jnp.where(lane == 98, third, keys)
        values = pltpu.roll(value, 64, 1) + pltpu.roll(value, 96, 1)
        values = jnp.where((lane >= 64) & (lane < 67), 1.0, values)
        start = pl.multiple_of(index * CELLS, 32)
        kaug_ref[pl.ds(start, CELLS), :] = keys.astype(bf16)
        vaug_ref[pl.ds(start, CELLS), :] = values.astype(bf16)
        qo_ref[pl.ds(start, CELLS), :] = cell
        return carry

    lax.fori_loop(0, sources, prepare, 0)

    def turn(index, carry):
        start = pl.multiple_of(index * block, block)
        xt_ref[:, pl.ds(start, block)] = qo_ref[pl.ds(start, block), :].T.astype(bf16)
        acc_ref[pl.ds(start, block), :] = jnp.zeros((block, 128), f32)
        return carry

    lax.fori_loop(0, total // block, turn, 0)

    def one_block(index, carry):
        start = pl.multiple_of(index * block, block)
        xq = qo_ref[pl.ds(start, block), :]
        xt = xt_ref[:, pl.ds(start, block)].astype(f32)
        query = xt[0:32] * to_log2
        first = query.astype(bf16).astype(f32)
        second = (query - first).astype(bf16).astype(f32)
        third = query - first - second
        qaug = jnp.concatenate([first, second, third, jnp.ones((32, block), f32)], axis=0).astype(bf16)

        def scores(part, highest):
            begin = pl.multiple_of(part * step, step)
            t = jnp.dot(kaug_ref[pl.ds(begin, step), :], qaug, preferred_element_type=f32)
            t_ref[pl.ds(begin, step), :] = t
            return jnp.maximum(highest, jnp.max(t.reshape(step // 8, 8, block), axis=0))

        highest = lax.fori_loop(0, total // step, scores, jnp.full((8, block), -jnp.inf, f32))
        highest = jnp.max(highest, axis=0, keepdims=True)

        def weigh(part, carry):
            norm, heads = carry
            begin = pl.multiple_of(part * step, step)
            p = jnp.exp2(t_ref[pl.ds(begin, step), :] - highest)
            t_ref[pl.ds(begin, step), :] = p
            low = p.astype(bf16)
            pb_ref[pl.ds(begin, step), :] = low
            norm = norm + jnp.sum(p.reshape(step // 8, 8, block), axis=0)
            heads = heads + jnp.dot(
                xt_ref[64:96, pl.ds(begin, step)], low, preferred_element_type=f32
            )
            return norm, heads

        norm, heads = lax.fori_loop(
            0, total // step, weigh, (jnp.zeros((8, block), f32), jnp.zeros((32, block), f32))
        )
        inverse = 1.0 / jnp.sum(norm, axis=0, keepdims=True)
        heads = heads * inverse
        back = xt[96:128]
        centred = jnp.sum(back * heads, axis=0, keepdims=True) * inverse
        back = back * inverse
        back_first = back.astype(bf16).astype(f32)
        back_second = back - back_first
        cen_first = centred.astype(bf16).astype(f32)
        cen_second = (centred - cen_first).astype(bf16).astype(f32)
        cen_third = centred - cen_first - cen_second
        sub = lax.broadcasted_iota(jnp.int32, (64, block), 0)
        cen = jnp.where(sub == 0, cen_first, jnp.where(sub == 1, cen_second, jnp.where(sub == 2, cen_third, 0.0)))
        baug = jnp.concatenate([back_first, back_second, -cen], axis=0).astype(bf16)
        zeros = jnp.zeros((32, block), f32)
        back_cells = jnp.concatenate([zeros, zeros, back_first, zeros], axis=0).T.astype(bf16)
        lane = lax.broadcasted_iota(jnp.int32, (block, 128), 1)
        query_cells = pltpu.roll(jnp.where(lane < 32, xq, 0.0), 32, 1).astype(bf16)

        def grads(part, back_queries):
            begin = pl.multiple_of(part * step, step)
            dp = jnp.dot(vaug_ref[pl.ds(begin, step), :], baug, preferred_element_type=f32)
            ds = (t_ref[pl.ds(begin, step), :] * dp).astype(bf16)
            acc_ref[pl.ds(begin, step), :] += jnp.dot(
                pb_ref[pl.ds(begin, step), :], back_cells, preferred_element_type=f32
            ) + jnp.dot(ds, query_cells, preferred_element_type=f32)
            return back_queries + jnp.dot(
                xt_ref[32:64, pl.ds(begin, step)], ds, preferred_element_type=f32
            )

        back_queries = lax.fori_loop(0, total // step, grads, zeros)
        turned = jnp.concatenate([back_queries * scale, zeros, zeros, heads], axis=0).T
        out_ref[pl.ds(start, block), :] = turned.astype(bf16)
        return carry

    lax.fori_loop(0, total // block, one_block, 0)

    def finish(index, carry):
        start = pl.multiple_of(index * block, block)
        lane = lax.broadcasted_iota(jnp.int32, (block, 128), 1)
        both = acc_ref[pl.ds(start, block), :]
        both = jnp.where(lane < 64, both * scale, both)
        both = jnp.where((lane >= 32) & (lane < 96), both, out_ref[pl.ds(start, block), :].astype(f32))
        out_ref[pl.ds(start, block), :] = both.astype(bf16)
        return carry

    lax.fori_loop(0, total // block, finish, 0)


def attend_items(items, valid, scale):
    sources = items.shape[0]
    total = sources * CELLS
    f32, bf16 = jnp.float32, jnp.bfloat16
    out = pl.pallas_call(
        functools.partial(attend_kernel, valid, scale),
        out_shape=jax.ShapeDtypeStruct((total, 128), bf16),
        in_specs=[pl.BlockSpec(memory_space=pltpu.VMEM)],
        out_specs=pl.BlockSpec(memory_space=pltpu.VMEM),
        scratch_shapes=[
            pltpu.VMEM((128, total), bf16),
            pltpu.VMEM((total, 128), bf16),
            pltpu.VMEM((total, 128), bf16),
            pltpu.VMEM((total, 256), f32),
            pltpu.VMEM((total, 256), bf16),
            pltpu.VMEM((total, 128), f32),
            pltpu.VMEM((total, 128), f32),
        ],
        compiler_params=pltpu.CompilerParams(vmem_limit_bytes=40 * 1024 * 1024),
        name="attend",
    )(items)
    return out.reshape(sources, CELLS, 128)


MESH = pl.DeviceIdType.MESH
SMALL = 80


def reduce_kernel(
    factor,
    normed_ref,
    expand_ref,
    mixed_ref,
    inner_ref,
    second_ref,
    project_ref,
    heads_ref,
    cot_ref,
    small_ref,
    out_ref,
    sums_ref,
    ga,
    gb,
    ra0,
    rb0,
    ra1,
    rb1,
    a1,
    b1,
    ra2,
    rb2,
    ab2,
    rz,
    s0,
    small0,
    smallz,
    smally,
    smallx,
    send_sems,
    recv_sems,
):
    f32, bf16 = jnp.float32, jnp.bfloat16
    lat, lon = lax.axis_index("lat"), lax.axis_index("lon")
    x_hi, y = lat // 4, lat % 4
    z, x_lo, core = lon // 4, (lon // 2) % 2, lon % 2
    x = x_hi * 2 + x_lo

    def place(px, py, pz, pc):
        return ((px // 2) * 4 + py, pz * 4 + (px % 2) * 2 + pc)

    other = 1 - core
    sibling = place(x, y, z, other)
    x_peers = [place((x + d) % 4, y, z, core) for d in range(1, 4)]
    y_peers = [place(x, (y + d) % 4, z, core) for d in range(1, 4)]
    z_peers = [place(x, y, (z + d) % 8, core) for d in range(1, 8)]
    barrier = pltpu.get_barrier_semaphore()
    peers = [sibling] + x_peers + y_peers + z_peers
    for peer in peers:
        pl.semaphore_signal(barrier, inc=1, device_id=peer, device_id_type=MESH)

    def half_lanes(top, bottom):
        lane = lax.broadcasted_iota(jnp.int32, top.shape, 1)
        even = jnp.where(lane < 64, top, pltpu.roll(bottom, 64, 1))
        odd = jnp.where(lane < 64, pltpu.roll(top, 64, 1), bottom)
        return even, odd

    def cross(left, right):
        return (
            lax.dot_general(left, right, (((0,), (0,)), ((), ())), preferred_element_type=f32)
            * factor
        )

    def expand_part(pz, carry):
        columns = pl.ds(pl.multiple_of(pz * 256, 256), 256)
        grad = cross(expand_ref[:, columns], normed_ref[...])
        for sub in range(4):
            plo, pc = sub // 2, sub % 2
            for pair in range(4):
                tile = slice(pair * 128, pair * 128 + 128)
                parts = half_lanes(
                    grad[sub * 64 : sub * 64 + 32, tile], grad[sub * 64 + 32 : sub * 64 + 64, tile]
                )
                for odd in range(2):
                    plat = pair * 2 + odd
                    px, py = (plat // 4) * 2 + plo, plat % 4
                    ga[pc, (px * 4 + py) * 8 + pz, 0:32, :] = parts[odd].astype(bf16)
        return carry

    def other_part(zz, carry):
        columns = pl.ds(pl.multiple_of(zz * 128, 128), 128)
        shrink = cross(inner_ref[:, columns], mixed_ref[...])
        grad_in = cross(
            project_ref[:, pl.ds(pl.multiple_of(zz * 384, 128), 384)], second_ref[...]
        )
        grad_out = cross(cot_ref[:, columns], heads_ref[...])
        for sub in range(8):
            pz, plo, pc = zz * 2 + sub // 4, (sub // 2) % 2, sub % 2
            for plat in range(8):
                px, py = (plat // 4) * 2 + plo, plat % 4
                rows = slice(sub * 16, sub * 16 + 16)
                ga[pc, (px * 4 + py) * 8 + pz, 32:48, :] = shrink[
                    rows, plat * 256 : plat * 256 + 128
                ].astype(bf16)
                gb[pc, (py * 4 + px) * 8 + pz, 0:16, :] = shrink[
                    rows, plat * 256 + 128 : plat * 256 + 256
                ].astype(bf16)
            for pair in range(4):
                tile = slice(pair * 128, pair * 128 + 128)
                top = jnp.concatenate(
                    [grad_in[sub * 48 : sub * 48 + 24, tile], grad_out[sub * 16 : sub * 16 + 8, tile]],
                    axis=0,
                )
                bottom = jnp.concatenate(
                    [
                        grad_in[sub * 48 + 24 : sub * 48 + 48, tile],
                        grad_out[sub * 16 + 8 : sub * 16 + 16, tile],
                    ],
                    axis=0,
                )
                parts = half_lanes(top, bottom)
                for odd in range(2):
                    plat = pair * 2 + odd
                    px, py = (plat // 4) * 2 + plo, plat % 4
                    gb[pc, (py * 4 + px) * 8 + pz, 16:48, :] = parts[odd].astype(bf16)
        return carry

    lax.fori_loop(0, 4, other_part, 0)
    lax.fori_loop(0, 8, expand_part, 0)
    pl.semaphore_wait(barrier, len(peers))

    count = [0]

    def copy(source, target, peer):
        index = count[0]
        count[0] += 1
        made = pltpu.make_async_remote_copy(
            src_ref=source,
            dst_ref=target,
            send_sem=send_sems.at[index],
            recv_sem=recv_sems.at[index],
            device_id=peer,
            device_id_type=MESH,
        )
        made.start()
        return made

    sent = []
    small_core = copy(small_ref.at[other], small0, sibling)
    first_a, first_b = [], []
    for d in (1, 2, 3, 0):
        rows = pl.ds(((x + d) % 4) * 32, 32)
        first_a.append((rows, copy(ga.at[other, rows], ra0.at[rows], sibling)))
        rows = pl.ds(((y + d) % 4) * 32, 32)
        first_b.append((rows, copy(gb.at[other, rows], rb0.at[rows], sibling)))

    small_core.wait_recv()
    s0[...] = small_ref[core] + small0[...]
    smallz[z] = s0[...]
    small_z = [copy(s0, smallz.at[z], peer) for peer in z_peers]

    def add_pair(mine, theirs, base):
        def body(step, carry):
            index = base + step * 4
            mine[core, pl.ds(index, 4)] = (
                mine[core, pl.ds(index, 4)].astype(f32) + theirs[pl.ds(index, 4)].astype(f32)
            ).astype(bf16)
            return carry

        lax.fori_loop(0, 8, body, 0)

    next_a, next_b = [], []
    for order, d in enumerate((1, 2, 3, 0)):
        rows, made = first_a[order]
        made.wait_recv()
        base = ((x + d) % 4) * 32
        add_pair(ga, ra0, base)
        if d:
            next_a.append(copy(ga.at[core, pl.ds(base, 32)], ra1.at[d - 1], x_peers[d - 1]))
        rows, made = first_b[order]
        made.wait_recv()
        base = ((y + d) % 4) * 32
        add_pair(gb, rb0, base)
        if d:
            next_b.append(copy(gb.at[core, pl.ds(base, 32)], rb1.at[d - 1], y_peers[d - 1]))

    def add_four(mine, theirs, total, base, blocks):
        def body(step, carry):
            index = step * 2
            value = mine(base + index).astype(f32)
            for d in range(3):
                value = value + theirs[d, pl.ds(index, 2)].astype(f32)
            total[pl.ds(index, 2)] = value.astype(bf16)
            return carry

        lax.fori_loop(0, blocks // 2, body, 0)

    for made in next_a:
        made.wait_recv()
    add_four(lambda i: ga[core, pl.ds(i, 2)], ra1, a1, x * 32, 32)
    last_a = [
        copy(a1.at[pl.ds(((y + d) % 4) * 8, 8)], ra2.at[d - 1], y_peers[d - 1]) for d in (1, 2, 3)
    ]
    for made in next_b:
        made.wait_recv()
    add_four(lambda i: gb[core, pl.ds(i, 2)], rb1, b1, y * 32, 32)
    last_b = [
        copy(b1.at[pl.ds(((x + d) % 4) * 8, 8)], rb2.at[d - 1], x_peers[d - 1]) for d in (1, 2, 3)
    ]

    for made in small_z:
        made.wait_recv()
    total = smallz[0]
    for index in range(1, 8):
        total = total + smallz[index]
    smally[y] = total
    small_y = [copy(smally.at[y], smally.at[y], peer) for peer in y_peers]

    def finish_pair(mine, theirs, first_row, base):
        def body(step, carry):
            value = mine[base + step].astype(f32)
            for d in range(3):
                value = value + theirs[d, step].astype(f32)
            ab2[step, first_row : first_row + 48, :] = value.astype(bf16)
            return carry

        lax.fori_loop(0, 8, body, 0)

    for made in last_a:
        made.wait_recv()
    finish_pair(a1, ra2, 0, y * 8)
    for made in last_b:
        made.wait_recv()
    finish_pair(b1, rb2, 48, x * 8)
    last = [copy(ab2.at[(z + d) % 8], rz.at[d - 1], z_peers[d - 1]) for d in range(1, 8)]

    for made in small_y:
        made.wait_recv()
    total = (smally[0] + smally[1]) + (smally[2] + smally[3])
    smallx[x] = total
    small_x = [copy(smallx.at[x], smallx.at[x], peer) for peer in x_peers]

    for made in last:
        made.wait_recv()
    value = ab2[z].astype(f32)
    for d in range(7):
        value = value + rz[d].astype(f32)
    out_ref[...] = value

    for made in small_x:
        made.wait_recv()
    s0_final = (smallx[0] + smallx[1]) + (smallx[2] + smallx[3])
    sums_ref[core] = s0_final
    final = copy(sums_ref.at[core], sums_ref.at[core], sibling)
    final.wait_recv()
    everything = (
        [small_core, final]
        + [made for _, made in first_a]
        + [made for _, made in first_b]
        + next_a
        + next_b
        + last_a
        + last_b
        + last
        + small_z
        + small_y
        + small_x
    )
    for made in everything:
        made.wait_send()


def reduce_all(factor, operands, small):
    f32, bf16 = jnp.float32, jnp.bfloat16
    vmem = pl.BlockSpec(memory_space=pltpu.VMEM)
    copies = 1 + 8 + 7 + 6 + 6 + 3 + 7 + 3 + 1
    return pl.pallas_call(
        functools.partial(reduce_kernel, factor),
        out_shape=(
            jax.ShapeDtypeStruct((96, 128), f32),
            jax.ShapeDtypeStruct((2, SMALL, 128), f32),
        ),
        in_specs=[vmem] * 9,
        out_specs=(vmem, vmem),
        scratch_shapes=[
            pltpu.VMEM((2, 128, 48, 128), bf16),
            pltpu.VMEM((2, 128, 48, 128), bf16),
            pltpu.VMEM((128, 48, 128), bf16),
            pltpu.VMEM((128, 48, 128), bf16),
            pltpu.VMEM((3, 32, 48, 128), bf16),
            pltpu.VMEM((3, 32, 48, 128), bf16),
            pltpu.VMEM((32, 48, 128), bf16),
            pltpu.VMEM((32, 48, 128), bf16),
            pltpu.VMEM((3, 8, 48, 128), bf16),
            pltpu.VMEM((3, 8, 48, 128), bf16),
            pltpu.VMEM((8, 96, 128), bf16),
            pltpu.VMEM((7, 96, 128), bf16),
            pltpu.VMEM((SMALL, 128), f32),
            pltpu.VMEM((SMALL, 128), f32),
            pltpu.VMEM((8, SMALL, 128), f32),
            pltpu.VMEM((4, SMALL, 128), f32),
            pltpu.VMEM((4, SMALL, 128), f32),
            pltpu.SemaphoreType.DMA((copies,)),
            pltpu.SemaphoreType.DMA((copies,)),
        ],
        compiler_params=pltpu.CompilerParams(
            vmem_limit_bytes=48 * 1024 * 1024, collective_id=1, has_side_effects=True
        ),
        name="reduce_grads",
    )(*operands, small)


def owner_blocks(block):
    def unfold(part):
        return jnp.concatenate([part[:, :64], part[:, 64:]], axis=0).T

    expand = unfold(block[0:32])
    shrink = jnp.concatenate([block[32:48], block[48:64]], axis=1).T
    grad_in = unfold(block[64:88])
    grad_out = unfold(block[88:96])
    return expand, shrink, grad_in, grad_out


def per_device(
    state_field,
    cotangent,
    key_bias,
    input_gain,
    expand_weight,
    depth_weight,
    shrink_weight,
    attention_gain,
    attention_in,
    attention_out,
):
    row_count, lon_count, channels = state_field.shape
    head_count = key_bias.shape[2]
    head_width = channels // head_count
    norm_factor = 1.0 / math.sqrt(
        row_count * lon_count * lax.axis_size("lat") * lax.axis_size("lon")
    )
    score_scale = 1.0 / math.sqrt(head_width)
    state_float = state_field.astype(jnp.float32)
    inverse_first = inverse_rms(state_float)
    normed = (state_float * inverse_first * input_gain).astype(jnp.bfloat16)
    expanded = jnp.dot(normed, expand_weight, preferred_element_type=jnp.float32)
    activated = jax.nn.silu(expanded).astype(jnp.bfloat16)
    padded = with_halo(activated, (("lon", 1),), 1, True)
    padded = with_halo(padded, (("lat", 0),), 1, False)
    convolved = depthwise_sum(padded, depth_weight, row_count, lon_count)
    mixed = jax.nn.silu(convolved).astype(jnp.bfloat16)
    inner_state = (
        state_float + jnp.dot(mixed, shrink_weight, preferred_element_type=jnp.float32)
    ).astype(jnp.bfloat16)
    inner_float = inner_state.astype(jnp.float32)
    inverse_second = inverse_rms(inner_float)
    normed_second = (inner_float * inverse_second * attention_gain).astype(jnp.bfloat16)
    wide_in = attention_in.reshape(channels, 3, head_count, head_width).transpose(0, 2, 1, 3)
    wide_in = wide_in.reshape(channels, head_count, 3 * head_width)
    wide_in = jnp.pad(wide_in, ((0, 0), (0, 0), (0, head_width)))
    wide_out = attention_out.T.reshape(channels, head_count, head_width)
    wide_out = jnp.pad(wide_out, ((0, 0), (0, 0), (3 * head_width, 0)))
    wide = jnp.concatenate([wide_in, wide_out], axis=0).reshape(2 * channels, -1)
    items = jnp.dot(
        jnp.concatenate([normed_second, cotangent], axis=-1),
        wide,
        preferred_element_type=jnp.float32,
    ).astype(jnp.bfloat16)
    items = items.reshape(row_count, lon_count, head_count, 4 * head_width)
    items = items.transpose(0, 2, 1, 3).reshape(row_count * head_count, lon_count, -1)
    bias_items = key_bias.transpose(0, 2, 1).reshape(row_count * head_count, 1, lon_count)
    bias_items = jnp.pad(bias_items, ((0, 0), (0, 0), (0, 4 * head_width - lon_count)))
    items = jnp.concatenate([items, bias_items], axis=1)
    items = jnp.pad(items, ((0, 0), (0, CELLS - lon_count - 1), (0, 0)))
    items = lax.all_to_all(items, "lon", split_axis=0, concat_axis=0, tiled=True)
    answers = attend_items(items, lon_count, score_scale)
    answers = lax.all_to_all(answers, "lon", split_axis=0, concat_axis=0, tiled=True)
    answers = answers.reshape(row_count, head_count, CELLS, 4, head_width)[:, :, :lon_count]
    answers = answers.transpose(0, 2, 3, 1, 4).reshape(row_count, lon_count, 4 * channels)
    back_projected = answers[..., : 3 * channels]
    heads_field = answers[..., 3 * channels :]
    output_field = (
        inner_float + jnp.dot(heads_field, attention_out, preferred_element_type=jnp.float32)
    ).astype(jnp.bfloat16)
    back_second = times_transpose(back_projected, attention_in)
    gain_two = jnp.sum(back_second * inner_float * inverse_second, axis=(0, 1)) * norm_factor
    back_inner = (
        cotangent.astype(jnp.float32)
        + norm_back(back_second, inner_float, inverse_second, attention_gain)
    ).astype(jnp.bfloat16)
    back_convolved = (times_transpose(back_inner, shrink_weight) * silu_slope(convolved)).astype(
        jnp.bfloat16
    )
    back_pad = with_halo(back_convolved, (("lon", 1),), 1, True)
    back_pad = with_halo(back_pad, (("lat", 0),), 1, False)
    back_activated = transposed_sum(back_pad, depth_weight, row_count, lon_count)
    back_conv_float = back_convolved.astype(jnp.float32)
    depth_local = (
        jnp.stack(
            [
                jnp.stack(
                    [
                        jnp.sum(
                            padded[
                                lat_step : lat_step + row_count, lon_step : lon_step + lon_count
                            ].astype(jnp.float32)
                            * back_conv_float,
                            axis=(0, 1),
                        )
                        for lon_step in range(3)
                    ]
                )
                for lat_step in range(3)
            ]
        )
        * norm_factor
    )
    back_expanded = (back_activated * silu_slope(expanded)).astype(jnp.bfloat16)
    back_normed = times_transpose(back_expanded, expand_weight)
    gain_one = jnp.sum(back_normed * state_float * inverse_first, axis=(0, 1)) * norm_factor
    input_grad = (
        back_inner.astype(jnp.float32)
        + norm_back(back_normed, state_float, inverse_first, input_gain)
    ).astype(jnp.bfloat16)
    wide_count = depth_local.shape[2]
    small = jnp.concatenate([depth_local.reshape(-1), gain_one, gain_two])
    small = jnp.pad(small, (0, 2 * SMALL * 128 - small.shape[0])).reshape(2, SMALL, 128)

    def flat(values):
        values = jnp.pad(values, ((0, 0), (0, CELLS - lon_count), (0, 0)))
        return values.reshape(row_count * CELLS, values.shape[2])

    block, sums = reduce_all(
        norm_factor,
        [
            flat(values)
            for values in (
                normed,
                back_expanded,
                mixed,
                back_inner,
                normed_second,
                back_projected,
                heads_field,
                cotangent,
            )
        ],
        small,
    )
    results = owner_blocks(block)
    sums = sums.reshape(-1)
    depth_grad = sums[: 9 * wide_count].reshape(3, 3, wide_count)
    input_gain_grad = sums[9 * wide_count : 9 * wide_count + channels]
    attention_gain_grad = sums[9 * wide_count + channels : 9 * wide_count + 2 * channels]
    return (
        output_field,
        input_grad,
        results[0],
        results[1],
        results[2],
        results[3],
        depth_grad,
        input_gain_grad,
        attention_gain_grad,
    )


def solution(mesh):
    placed = (
        P("lat", "lon", None),
        P("lat", "lon", None),
        P("lat", "lon", None),
        P(),
        P(),
        P(),
        P(),
        P(),
        P(),
        P(),
    )
    return jax.shard_map(
        per_device,
        mesh=mesh,
        in_specs=placed,
        out_specs=(
            P("lat", "lon", None),
            P("lat", "lon", None),
            P("lat", "lon"),
            P("lat", "lon"),
            P("lat", "lon"),
            P("lat", "lon"),
            P(),
            P(),
            P(),
        ),
        check_vma=False,
    )
```

```python
import functools
import math

import jax
import jax.numpy as jnp
from jax import lax
from jax.experimental import pallas as pl
from jax.experimental.pallas import tpu as pltpu
from jax.sharding import PartitionSpec as P

EPSILON = 1e-06


def with_halo(block, sides, width, periodic):
    for axis, dim in sides:
        count = lax.axis_size(axis)
        forward = [(i, i + 1) for i in range(count - 1)]
        if periodic:
            forward.append((count - 1, 0))
        backward = [(target, source) for source, target in forward]
        low = lax.ppermute(
            lax.slice_in_dim(block, block.shape[dim] - width, None, axis=dim), axis, forward
        )
        high = lax.ppermute(lax.slice_in_dim(block, 0, width, axis=dim), axis, backward)
        block = jnp.concatenate([low, block, high], axis=dim)
    return block


def inverse_rms(values):
    return lax.rsqrt(jnp.mean(values * values, axis=-1, keepdims=True) + EPSILON)


def silu_slope(values):
    sigmoid = jax.nn.sigmoid(values)
    return sigmoid * (1.0 + values * (1.0 - sigmoid))


def depthwise_sum(padded, weights, row_count, lon_count):
    total = jnp.zeros((row_count, lon_count, padded.shape[2]), jnp.float32)
    for lat_step in range(3):
        for lon_step in range(3):
            total = total + weights[lat_step, lon_step].astype(jnp.float32) * padded[
                lat_step : lat_step + row_count, lon_step : lon_step + lon_count
            ].astype(jnp.float32)
    return total


def transposed_sum(padded, weights, row_count, lon_count):
    total = jnp.zeros((row_count, lon_count, padded.shape[2]), jnp.float32)
    for lat_step in range(3):
        for lon_step in range(3):
            total = total + weights[lat_step, lon_step].astype(jnp.float32) * padded[
                2 - lat_step : 2 - lat_step + row_count, 2 - lon_step : 2 - lon_step + lon_count
            ].astype(jnp.float32)
    return total


def times_transpose(values, weights):
    return lax.dot_general(
        values, weights, (((values.ndim - 1,), (1,)), ((), ())), preferred_element_type=jnp.float32
    )


def norm_back(back_normed, state, inverse, gain):
    scaled = back_normed * gain
    return inverse * scaled - inverse * inverse * inverse * state * jnp.mean(
        scaled * state, axis=-1, keepdims=True
    )


CELLS = 96
MESH = pl.DeviceIdType.MESH


def attend_kernel(
    valid,
    scale,
    items_ref,
    near_ref,
    last_ref,
    x_ref,
    near_send,
    last_send,
    xt_ref,
    kaug_ref,
    vaug_ref,
    t_ref,
    pb_ref,
    acc_ref,
    cell_ref,
    in_send,
    in_recv,
    near_send_sem,
    near_recv_sem,
    last_send_sem,
    last_recv_sem,
):
    sources = items_ref.shape[0]
    total = sources * CELLS
    block = t_ref.shape[1]
    group = block // CELLS
    log2e = 1.4426950408889634
    to_log2 = scale * log2e
    f32, bf16 = jnp.float32, jnp.bfloat16
    lat, lon = lax.axis_index("lat"), lax.axis_index("lon")
    z, low = lon // 4, lon % 4

    def partner(k, sign):
        ring, side = k // 4, 3 - k % 4
        half = (ring + 1) // 2
        shift = 4 + (1 - 2 * (ring % 2)) * half
        x_lo, core = low // 2, low % 2
        x_lo = x_lo + (side // 2) * (1 - 2 * x_lo)
        core = core + (side % 2) * (1 - 2 * core)
        return ((z + sign * shift + 8) % 8) * 4 + x_lo * 2 + core

    barrier = pltpu.get_barrier_semaphore()

    def greet(k, carry):
        pl.semaphore_signal(
            barrier, inc=1, device_id=(lat, partner(k, 1)), device_id_type=MESH
        )
        return carry

    lax.fori_loop(0, sources - 1, greet, 0)
    pl.semaphore_wait(barrier, sources - 1)

    def incoming(k, slot):
        to = partner(k, 1)
        return pltpu.make_async_remote_copy(
            src_ref=items_ref.at[to],
            dst_ref=x_ref.at[slot],
            send_sem=in_send.at[k],
            recv_sem=in_recv.at[k],
            device_id=(lat, to),
            device_id_type=MESH,
        )

    def push(k, carry):
        incoming(k, lon).start()
        return carry

    lax.fori_loop(0, sources - 1, push, 0)
    x_ref[lon] = items_ref[lon]

    def prepare(index):
        raw = x_ref[index].astype(f32)
        row = lax.broadcasted_iota(jnp.int32, (CELLS, 128), 0)
        lane = lax.broadcasted_iota(jnp.int32, (CELLS, 128), 1)
        bias_row = jnp.broadcast_to(raw[valid : valid + 1, :], (CELLS, 128))
        bias = jnp.sum(jnp.where(row == lane, bias_row, 0.0), axis=1, keepdims=True) * log2e
        bias = jnp.broadcast_to(bias, (CELLS, 128))
        first = bias.astype(bf16).astype(f32)
        second = (bias - first).astype(bf16).astype(f32)
        third = bias - first - second
        first = jnp.where(row < valid, first, -1e30)
        second = jnp.where(row < valid, second, 0.0)
        third = jnp.where(row < valid, third, 0.0)
        cell = jnp.where(row < valid, raw, 0.0)
        key = jnp.where((lane >= 32) & (lane < 64), cell, 0.0)
        value = jnp.where((lane >= 64) & (lane < 96), cell, 0.0)
        keys = pltpu.roll(key, 96, 1) + key + pltpu.roll(key, 32, 1)
        keys = jnp.where(lane == 96, first, keys)
        keys = jnp.where(lane == 97, second, keys)
        keys = jnp.where(lane == 98, third, keys)
        values = pltpu.roll(value, 64, 1) + pltpu.roll(value, 96, 1)
        values = jnp.where((lane >= 64) & (lane < 67), 1.0, values)
        start = pl.multiple_of(index * CELLS, 32)
        kaug_ref[pl.ds(start, CELLS), :] = keys.astype(bf16)
        vaug_ref[pl.ds(start, CELLS), :] = values.astype(bf16)
        cell_ref[pl.ds(start, CELLS), :] = cell

    prepare(lon)

    def arrive(k, carry):
        source = partner(k, -1)
        incoming(k, source).wait_recv()
        prepare(source)
        return carry

    lax.fori_loop(0, sources - 1, arrive, 0)

    def turn(index, carry):
        start = pl.multiple_of(index * block, block)
        xt_ref[:, pl.ds(start, block)] = cell_ref[pl.ds(start, block), :].T.astype(bf16)
        acc_ref[:, pl.ds(start, block)] = jnp.zeros((64, block), f32)
        return carry

    lax.fori_loop(0, total // block, turn, 0)

    def packed(cells):
        return (cells[:48] + pltpu.roll(cells[48:], 64, 1)).astype(bf16)

    def nearby(source, slot):
        return pltpu.make_async_remote_copy(
            src_ref=near_send.at[source],
            dst_ref=near_ref.at[slot],
            send_sem=near_send_sem.at[source],
            recv_sem=near_recv_sem.at[slot],
            device_id=(lat, source),
            device_id_type=MESH,
        )

    def one_block(turn_index, carry):
        index = (turn_index + lon // group) % (sources // group)
        start = pl.multiple_of(index * block, block)
        xt = xt_ref[:, pl.ds(start, block)].astype(f32)
        query = xt[0:32] * to_log2
        first = query.astype(bf16).astype(f32)
        second = (query - first).astype(bf16).astype(f32)
        third = query - first - second
        qaug = jnp.concatenate(
            [first, second, third, jnp.ones((32, block), f32)], axis=0
        ).astype(bf16)
        t = jnp.dot(kaug_ref[...], qaug, preferred_element_type=f32)
        t_ref[...] = t
        highest = jnp.max(jnp.max(t.reshape(total // 8, 8, block), axis=0), axis=0, keepdims=True)
        p = jnp.exp2(t_ref[...] - highest)
        t_ref[...] = p
        low_p = p.astype(bf16)
        pb_ref[...] = low_p
        norm = jnp.sum(p.reshape(total // 8, 8, block), axis=0)
        heads = jnp.dot(xt_ref[64:96, :], low_p, preferred_element_type=f32)
        inverse = 1.0 / jnp.sum(norm, axis=0, keepdims=True)
        heads = heads * inverse
        back = xt[96:128]
        centred = jnp.sum(back * heads, axis=0, keepdims=True) * inverse
        back = back * inverse
        back_first = back.astype(bf16).astype(f32)
        back_second = back - back_first
        cen_first = centred.astype(bf16).astype(f32)
        cen_second = (centred - cen_first).astype(bf16).astype(f32)
        cen_third = centred - cen_first - cen_second
        sub = lax.broadcasted_iota(jnp.int32, (64, block), 0)
        cen = jnp.where(
            sub == 0,
            cen_first,
            jnp.where(sub == 1, cen_second, jnp.where(sub == 2, cen_third, 0.0)),
        )
        baug = jnp.concatenate([back_first, back_second, -cen], axis=0).astype(bf16)
        nt = (((1,), (1,)), ((), ()))
        dp = jnp.dot(vaug_ref[...], baug, preferred_element_type=f32)
        ds = (t_ref[...] * dp).astype(bf16)
        acc_ref[32:64, :] += lax.dot_general(
            back_first.astype(bf16), pb_ref[...], nt, preferred_element_type=f32
        )
        acc_ref[0:32, :] += lax.dot_general(
            xt_ref[0:32, pl.ds(start, block)], ds, nt, preferred_element_type=f32
        )
        back_queries = jnp.dot(xt_ref[32:64, :], ds, preferred_element_type=f32)
        zeros = jnp.zeros((64, block), f32)
        done = jnp.concatenate([back_queries * scale, heads, zeros], axis=0).T
        for part in range(group):
            source = index * group + part
            near_send[source] = packed(done[part * CELLS : part * CELLS + CELLS])

            @pl.when(source != lon)
            def _():
                nearby(source, lon).start()

        return carry

    lax.fori_loop(0, total // block, one_block, 0)
    near_ref[lon] = near_send[lon]

    def finish(index, carry):
        start = pl.multiple_of(index * block, block)
        both = acc_ref[:, pl.ds(start, block)]
        zeros = jnp.zeros((64, block), f32)
        both = jnp.concatenate([both[0:32] * scale, both[32:64], zeros], axis=0)
        cell_ref[pl.ds(start, block), :] = both.T
        return carry

    lax.fori_loop(0, total // block, finish, 0)

    def final(k, to, slot):
        return pltpu.make_async_remote_copy(
            src_ref=last_send.at[to],
            dst_ref=last_ref.at[slot],
            send_sem=last_send_sem.at[k],
            recv_sem=last_recv_sem.at[k],
            device_id=(lat, to),
            device_id_type=MESH,
        )

    def pack_last(source):
        start = pl.multiple_of(source * CELLS, 32)
        last_send[source] = packed(cell_ref[pl.ds(start, CELLS), :])

    def leave(k, carry):
        to = partner(k, 1)
        pack_last(to)
        final(k, to, lon).start()
        return carry

    lax.fori_loop(0, sources - 1, leave, 0)
    pack_last(lon)
    last_ref[lon] = last_send[lon]

    def settle(k, carry):
        to, source = partner(k, 1), partner(k, -1)
        incoming(k, lon).wait_send()
        nearby(to, lon).wait_send()
        nearby(source, source).wait_recv()
        made = final(k, to, source)
        made.wait_send()
        made.wait_recv()
        return carry

    lax.fori_loop(0, sources - 1, settle, 0)


def attend_items(items, valid, scale):
    sources = items.shape[0]
    total = sources * CELLS
    block = 768
    f32, bf16 = jnp.float32, jnp.bfloat16
    vmem = pl.BlockSpec(memory_space=pltpu.VMEM)
    answer = jax.ShapeDtypeStruct((sources, 48, 128), bf16)
    return pl.pallas_call(
        functools.partial(attend_kernel, valid, scale),
        out_shape=(answer, answer),
        in_specs=[vmem],
        out_specs=(vmem, vmem),
        scratch_shapes=[
            pltpu.VMEM((sources, CELLS, 128), bf16),
            pltpu.VMEM((sources, 48, 128), bf16),
            pltpu.VMEM((sources, 48, 128), bf16),
            pltpu.VMEM((128, total), bf16),
            pltpu.VMEM((total, 128), bf16),
            pltpu.VMEM((total, 128), bf16),
            pltpu.VMEM((total, block), f32),
            pltpu.VMEM((total, block), bf16),
            pltpu.VMEM((64, total), f32),
            pltpu.VMEM((total, 128), f32),
        ]
        + [pltpu.SemaphoreType.DMA((sources,))] * 6,
        compiler_params=pltpu.CompilerParams(
            vmem_limit_bytes=48 * 1024 * 1024, collective_id=2, has_side_effects=True
        ),
        name="attend",
    )(items)


SMALL = 80


def reduce_kernel(
    factor,
    normed_ref,
    expand_ref,
    mixed_ref,
    inner_ref,
    second_ref,
    project_ref,
    heads_ref,
    cot_ref,
    small_ref,
    out_ref,
    sums_ref,
    ga,
    gb,
    ra0,
    rb0,
    ra1,
    rb1,
    a1,
    b1,
    ra2,
    rb2,
    ab2,
    rz,
    s0,
    small0,
    smallz,
    smally,
    smallx,
    send_sems,
    recv_sems,
):
    f32, bf16 = jnp.float32, jnp.bfloat16
    lat, lon = lax.axis_index("lat"), lax.axis_index("lon")
    x_hi, y = lat // 4, lat % 4
    z, x_lo, core = lon // 4, (lon // 2) % 2, lon % 2
    x = x_hi * 2 + x_lo

    def place(px, py, pz, pc):
        return ((px // 2) * 4 + py, pz * 4 + (px % 2) * 2 + pc)

    other = 1 - core
    sibling = place(x, y, z, other)
    x_peers = [place((x + d) % 4, y, z, core) for d in range(1, 4)]
    y_peers = [place(x, (y + d) % 4, z, core) for d in range(1, 4)]
    z_peers = [place(x, y, (z + d) % 8, core) for d in range(1, 8)]
    barrier = pltpu.get_barrier_semaphore()
    peers = [sibling] + x_peers + y_peers + z_peers
    for peer in peers:
        pl.semaphore_signal(barrier, inc=1, device_id=peer, device_id_type=MESH)

    def half_lanes(top, bottom):
        lane = lax.broadcasted_iota(jnp.int32, top.shape, 1)
        even = jnp.where(lane < 64, top, pltpu.roll(bottom, 64, 1))
        odd = jnp.where(lane < 64, pltpu.roll(top, 64, 1), bottom)
        return even, odd

    def cross(left, right):
        return (
            lax.dot_general(left, right, (((0,), (0,)), ((), ())), preferred_element_type=f32)
            * factor
        )

    def expand_part(pz, carry):
        columns = pl.ds(pl.multiple_of(pz * 256, 256), 256)
        grad = cross(expand_ref[:, columns], normed_ref[...])
        for sub in range(4):
            plo, pc = sub // 2, sub % 2
            for pair in range(4):
                tile = slice(pair * 128, pair * 128 + 128)
                parts = half_lanes(
                    grad[sub * 64 : sub * 64 + 32, tile], grad[sub * 64 + 32 : sub * 64 + 64, tile]
                )
                for odd in range(2):
                    plat = pair * 2 + odd
                    px, py = (plat // 4) * 2 + plo, plat % 4
                    ga[pc, (px * 4 + py) * 8 + pz, 0:32, :] = parts[odd].astype(bf16)
        return carry

    def other_part(zz, carry):
        columns = pl.ds(pl.multiple_of(zz * 128, 128), 128)
        shrink = cross(inner_ref[:, columns], mixed_ref[...])
        grad_in = cross(
            project_ref[:, pl.ds(pl.multiple_of(zz * 384, 128), 384)], second_ref[...]
        )
        grad_out = cross(cot_ref[:, columns], heads_ref[...])
        for sub in range(8):
            pz, plo, pc = zz * 2 + sub // 4, (sub // 2) % 2, sub % 2
            for plat in range(8):
                px, py = (plat // 4) * 2 + plo, plat % 4
                rows = slice(sub * 16, sub * 16 + 16)
                ga[pc, (px * 4 + py) * 8 + pz, 32:48, :] = shrink[
                    rows, plat * 256 : plat * 256 + 128
                ].astype(bf16)
                gb[pc, (py * 4 + px) * 8 + pz, 0:16, :] = shrink[
                    rows, plat * 256 + 128 : plat * 256 + 256
                ].astype(bf16)
            for pair in range(4):
                tile = slice(pair * 128, pair * 128 + 128)
                top = jnp.concatenate(
                    [grad_in[sub * 48 : sub * 48 + 24, tile], grad_out[sub * 16 : sub * 16 + 8, tile]],
                    axis=0,
                )
                bottom = jnp.concatenate(
                    [
                        grad_in[sub * 48 + 24 : sub * 48 + 48, tile],
                        grad_out[sub * 16 + 8 : sub * 16 + 16, tile],
                    ],
                    axis=0,
                )
                parts = half_lanes(top, bottom)
                for odd in range(2):
                    plat = pair * 2 + odd
                    px, py = (plat // 4) * 2 + plo, plat % 4
                    gb[pc, (py * 4 + px) * 8 + pz, 16:48, :] = parts[odd].astype(bf16)
        return carry

    lax.fori_loop(0, 4, other_part, 0)
    lax.fori_loop(0, 8, expand_part, 0)
    pl.semaphore_wait(barrier, len(peers))

    count = [0]

    def copy(source, target, peer):
        index = count[0]
        count[0] += 1
        made = pltpu.make_async_remote_copy(
            src_ref=source,
            dst_ref=target,
            send_sem=send_sems.at[index],
            recv_sem=recv_sems.at[index],
            device_id=peer,
            device_id_type=MESH,
        )
        made.start()
        return made

    sent = []
    small_core = copy(small_ref.at[other], small0, sibling)
    first_a, first_b = [], []
    for d in (1, 2, 3, 0):
        rows = pl.ds(((x + d) % 4) * 32, 32)
        first_a.append((rows, copy(ga.at[other, rows], ra0.at[rows], sibling)))
        rows = pl.ds(((y + d) % 4) * 32, 32)
        first_b.append((rows, copy(gb.at[other, rows], rb0.at[rows], sibling)))

    small_core.wait_recv()
    s0[...] = small_ref[core] + small0[...]
    smallz[z] = s0[...]
    small_z = [copy(s0, smallz.at[z], peer) for peer in z_peers]

    def add_pair(mine, theirs, base):
        def body(step, carry):
            index = base + step * 4
            mine[core, pl.ds(index, 4)] = (
                mine[core, pl.ds(index, 4)].astype(f32) + theirs[pl.ds(index, 4)].astype(f32)
            ).astype(bf16)
            return carry

        lax.fori_loop(0, 8, body, 0)

    next_a, next_b = [], []
    for order, d in enumerate((1, 2, 3, 0)):
        rows, made = first_a[order]
        made.wait_recv()
        base = ((x + d) % 4) * 32
        add_pair(ga, ra0, base)
        if d:
            next_a.append(copy(ga.at[core, pl.ds(base, 32)], ra1.at[d - 1], x_peers[d - 1]))
        rows, made = first_b[order]
        made.wait_recv()
        base = ((y + d) % 4) * 32
        add_pair(gb, rb0, base)
        if d:
            next_b.append(copy(gb.at[core, pl.ds(base, 32)], rb1.at[d - 1], y_peers[d - 1]))

    def add_four(mine, theirs, total, base, blocks):
        def body(step, carry):
            index = step * 2
            value = mine(base + index).astype(f32)
            for d in range(3):
                value = value + theirs[d, pl.ds(index, 2)].astype(f32)
            total[pl.ds(index, 2)] = value.astype(bf16)
            return carry

        lax.fori_loop(0, blocks // 2, body, 0)

    for made in next_a:
        made.wait_recv()
    add_four(lambda i: ga[core, pl.ds(i, 2)], ra1, a1, x * 32, 32)
    last_a = [
        copy(a1.at[pl.ds(((y + d) % 4) * 8, 8)], ra2.at[d - 1], y_peers[d - 1]) for d in (1, 2, 3)
    ]
    for made in next_b:
        made.wait_recv()
    add_four(lambda i: gb[core, pl.ds(i, 2)], rb1, b1, y * 32, 32)
    last_b = [
        copy(b1.at[pl.ds(((x + d) % 4) * 8, 8)], rb2.at[d - 1], x_peers[d - 1]) for d in (1, 2, 3)
    ]

    for made in small_z:
        made.wait_recv()
    total = smallz[0]
    for index in range(1, 8):
        total = total + smallz[index]
    smally[y] = total
    small_y = [copy(smally.at[y], smally.at[y], peer) for peer in y_peers]

    def finish_pair(mine, theirs, first_row, base):
        def body(step, carry):
            value = mine[base + step].astype(f32)
            for d in range(3):
                value = value + theirs[d, step].astype(f32)
            ab2[step, first_row : first_row + 48, :] = value.astype(bf16)
            return carry

        lax.fori_loop(0, 8, body, 0)

    for made in last_a:
        made.wait_recv()
    finish_pair(a1, ra2, 0, y * 8)
    for made in last_b:
        made.wait_recv()
    finish_pair(b1, rb2, 48, x * 8)
    last = [copy(ab2.at[(z + d) % 8], rz.at[d - 1], z_peers[d - 1]) for d in range(1, 8)]

    for made in small_y:
        made.wait_recv()
    total = (smally[0] + smally[1]) + (smally[2] + smally[3])
    smallx[x] = total
    small_x = [copy(smallx.at[x], smallx.at[x], peer) for peer in x_peers]

    for made in last:
        made.wait_recv()
    value = ab2[z].astype(f32)
    for d in range(7):
        value = value + rz[d].astype(f32)
    out_ref[...] = value

    for made in small_x:
        made.wait_recv()
    s0_final = (smallx[0] + smallx[1]) + (smallx[2] + smallx[3])
    sums_ref[core] = s0_final
    final = copy(sums_ref.at[core], sums_ref.at[core], sibling)
    final.wait_recv()
    everything = (
        [small_core, final]
        + [made for _, made in first_a]
        + [made for _, made in first_b]
        + next_a
        + next_b
        + last_a
        + last_b
        + last
        + small_z
        + small_y
        + small_x
    )
    for made in everything:
        made.wait_send()


def reduce_all(factor, operands, small):
    f32, bf16 = jnp.float32, jnp.bfloat16
    vmem = pl.BlockSpec(memory_space=pltpu.VMEM)
    copies = 1 + 8 + 7 + 6 + 6 + 3 + 7 + 3 + 1
    return pl.pallas_call(
        functools.partial(reduce_kernel, factor),
        out_shape=(
            jax.ShapeDtypeStruct((96, 128), f32),
            jax.ShapeDtypeStruct((2, SMALL, 128), f32),
        ),
        in_specs=[vmem] * 9,
        out_specs=(vmem, vmem),
        scratch_shapes=[
            pltpu.VMEM((2, 128, 48, 128), bf16),
            pltpu.VMEM((2, 128, 48, 128), bf16),
            pltpu.VMEM((128, 48, 128), bf16),
            pltpu.VMEM((128, 48, 128), bf16),
            pltpu.VMEM((3, 32, 48, 128), bf16),
            pltpu.VMEM((3, 32, 48, 128), bf16),
            pltpu.VMEM((32, 48, 128), bf16),
            pltpu.VMEM((32, 48, 128), bf16),
            pltpu.VMEM((3, 8, 48, 128), bf16),
            pltpu.VMEM((3, 8, 48, 128), bf16),
            pltpu.VMEM((8, 96, 128), bf16),
            pltpu.VMEM((7, 96, 128), bf16),
            pltpu.VMEM((SMALL, 128), f32),
            pltpu.VMEM((SMALL, 128), f32),
            pltpu.VMEM((8, SMALL, 128), f32),
            pltpu.VMEM((4, SMALL, 128), f32),
            pltpu.VMEM((4, SMALL, 128), f32),
            pltpu.SemaphoreType.DMA((copies,)),
            pltpu.SemaphoreType.DMA((copies,)),
        ],
        compiler_params=pltpu.CompilerParams(
            vmem_limit_bytes=48 * 1024 * 1024, collective_id=1, has_side_effects=True
        ),
        name="reduce_grads",
    )(*operands, small)


def owner_blocks(block):
    def unfold(part):
        return jnp.concatenate([part[:, :64], part[:, 64:]], axis=0).T

    expand = unfold(block[0:32])
    shrink = jnp.concatenate([block[32:48], block[48:64]], axis=1).T
    grad_in = unfold(block[64:88])
    grad_out = unfold(block[88:96])
    return expand, shrink, grad_in, grad_out


def per_device(
    state_field,
    cotangent,
    key_bias,
    input_gain,
    expand_weight,
    depth_weight,
    shrink_weight,
    attention_gain,
    attention_in,
    attention_out,
):
    row_count, lon_count, channels = state_field.shape
    head_count = key_bias.shape[2]
    head_width = channels // head_count
    norm_factor = 1.0 / math.sqrt(
        row_count * lon_count * lax.axis_size("lat") * lax.axis_size("lon")
    )
    score_scale = 1.0 / math.sqrt(head_width)
    state_float = state_field.astype(jnp.float32)
    inverse_first = inverse_rms(state_float)
    normed = (state_float * inverse_first * input_gain).astype(jnp.bfloat16)
    expanded = jnp.dot(normed, expand_weight, preferred_element_type=jnp.float32)
    activated = jax.nn.silu(expanded).astype(jnp.bfloat16)
    padded = with_halo(activated, (("lon", 1),), 1, True)
    padded = with_halo(padded, (("lat", 0),), 1, False)
    convolved = depthwise_sum(padded, depth_weight, row_count, lon_count)
    mixed = jax.nn.silu(convolved).astype(jnp.bfloat16)
    inner_state = (
        state_float + jnp.dot(mixed, shrink_weight, preferred_element_type=jnp.float32)
    ).astype(jnp.bfloat16)
    inner_float = inner_state.astype(jnp.float32)
    inverse_second = inverse_rms(inner_float)
    normed_second = (inner_float * inverse_second * attention_gain).astype(jnp.bfloat16)
    wide_in = attention_in.reshape(channels, 3, head_count, head_width).transpose(0, 2, 1, 3)
    wide_in = wide_in.reshape(channels, head_count, 3 * head_width)
    wide_in = jnp.pad(wide_in, ((0, 0), (0, 0), (0, head_width)))
    wide_out = attention_out.T.reshape(channels, head_count, head_width)
    wide_out = jnp.pad(wide_out, ((0, 0), (0, 0), (3 * head_width, 0)))
    wide = jnp.concatenate([wide_in, wide_out], axis=0).reshape(2 * channels, -1)
    items = jnp.dot(
        jnp.concatenate([normed_second, cotangent], axis=-1),
        wide,
        preferred_element_type=jnp.float32,
    ).astype(jnp.bfloat16)
    items = items.reshape(row_count, lon_count, head_count, 4 * head_width)
    items = items.transpose(0, 2, 1, 3).reshape(row_count * head_count, lon_count, -1)
    bias_items = key_bias.transpose(0, 2, 1).reshape(row_count * head_count, 1, lon_count)
    bias_items = jnp.pad(bias_items, ((0, 0), (0, 0), (0, 4 * head_width - lon_count)))
    items = jnp.concatenate([items, bias_items], axis=1)
    items = jnp.pad(items, ((0, 0), (0, CELLS - lon_count - 1), (0, 0)))
    near, last = attend_items(items, lon_count, score_scale)

    def unpack(parts):
        parts = parts.reshape(row_count, head_count, CELLS // 2, 2, 2, head_width)
        parts = parts.transpose(4, 0, 3, 2, 1, 5).reshape(2, row_count, CELLS, channels)
        return parts[0, :, :lon_count], parts[1, :, :lon_count]

    back_queries, heads_field = unpack(near)
    back_keys, back_values = unpack(last)
    back_projected = jnp.concatenate([back_queries, back_keys, back_values], axis=-1)
    output_field = (
        inner_float + jnp.dot(heads_field, attention_out, preferred_element_type=jnp.float32)
    ).astype(jnp.bfloat16)
    back_second = times_transpose(back_projected, attention_in)
    gain_two = jnp.sum(back_second * inner_float * inverse_second, axis=(0, 1)) * norm_factor
    back_inner = (
        cotangent.astype(jnp.float32)
        + norm_back(back_second, inner_float, inverse_second, attention_gain)
    ).astype(jnp.bfloat16)
    back_convolved = (times_transpose(back_inner, shrink_weight) * silu_slope(convolved)).astype(
        jnp.bfloat16
    )
    back_pad = with_halo(back_convolved, (("lon", 1),), 1, True)
    back_pad = with_halo(back_pad, (("lat", 0),), 1, False)
    back_activated = transposed_sum(back_pad, depth_weight, row_count, lon_count)
    back_conv_float = back_convolved.astype(jnp.float32)
    depth_local = (
        jnp.stack(
            [
                jnp.stack(
                    [
                        jnp.sum(
                            padded[
                                lat_step : lat_step + row_count, lon_step : lon_step + lon_count
                            ].astype(jnp.float32)
                            * back_conv_float,
                            axis=(0, 1),
                        )
                        for lon_step in range(3)
                    ]
                )
                for lat_step in range(3)
            ]
        )
        * norm_factor
    )
    back_expanded = (back_activated * silu_slope(expanded)).astype(jnp.bfloat16)
    back_normed = times_transpose(back_expanded, expand_weight)
    gain_one = jnp.sum(back_normed * state_float * inverse_first, axis=(0, 1)) * norm_factor
    input_grad = (
        back_inner.astype(jnp.float32)
        + norm_back(back_normed, state_float, inverse_first, input_gain)
    ).astype(jnp.bfloat16)
    wide_count = depth_local.shape[2]
    small = jnp.concatenate([depth_local.reshape(-1), gain_one, gain_two])
    small = jnp.pad(small, (0, 2 * SMALL * 128 - small.shape[0])).reshape(2, SMALL, 128)

    def flat(values):
        values = jnp.pad(values, ((0, 0), (0, CELLS - lon_count), (0, 0)))
        return values.reshape(row_count * CELLS, values.shape[2])

    block, sums = reduce_all(
        norm_factor,
        [
            flat(values)
            for values in (
                normed,
                back_expanded,
                mixed,
                back_inner,
                normed_second,
                back_projected,
                heads_field,
                cotangent,
            )
        ],
        small,
    )
    results = owner_blocks(block)
    sums = sums.reshape(-1)
    depth_grad = sums[: 9 * wide_count].reshape(3, 3, wide_count)
    input_gain_grad = sums[9 * wide_count : 9 * wide_count + channels]
    attention_gain_grad = sums[9 * wide_count + channels : 9 * wide_count + 2 * channels]
    return (
        output_field,
        input_grad,
        results[0],
        results[1],
        results[2],
        results[3],
        depth_grad,
        input_gain_grad,
        attention_gain_grad,
    )


def solution(mesh):
    placed = (
        P("lat", "lon", None),
        P("lat", "lon", None),
        P("lat", "lon", None),
        P(),
        P(),
        P(),
        P(),
        P(),
        P(),
        P(),
    )
    return jax.shard_map(
        per_device,
        mesh=mesh,
        in_specs=placed,
        out_specs=(
            P("lat", "lon", None),
            P("lat", "lon", None),
            P("lat", "lon"),
            P("lat", "lon"),
            P("lat", "lon"),
            P("lat", "lon"),
            P(),
            P(),
            P(),
        ),
        check_vma=False,
    )
```

```python
import functools
import math

import jax
import jax.numpy as jnp
from jax import lax
from jax.experimental import pallas as pl
from jax.experimental.pallas import tpu as pltpu
from jax.sharding import PartitionSpec as P

EPSILON = 1e-06
CELLS = 96
MESH = pl.DeviceIdType.MESH


CHUNK = 256


def silu_parts(values):
    sigmoid = 1.0 / (1.0 + jnp.exp(-values))
    return values * sigmoid, sigmoid * (1.0 + values * (1.0 - sigmoid))


def halo_copies(rows, edges, row_slots, edge_slots, sends, recvs):
    lat, lon = lax.axis_index("lat"), lax.axis_index("lon")
    bands, sectors = lax.axis_size("lat"), lax.axis_size("lon")
    west, east = (lon + sectors - 1) % sectors, (lon + 1) % sectors

    def made(source, target, index, peer):
        return pltpu.make_async_remote_copy(
            src_ref=source,
            dst_ref=target,
            send_sem=sends.at[index],
            recv_sem=recvs.at[index],
            device_id=peer,
            device_id_type=MESH,
        )

    north, south = lat > 0, lat < bands - 1
    copies = [
        (north, south, made(rows.at[0], row_slots.at[1], 0, (lat - 1, lon))),
        (south, north, made(rows.at[1], row_slots.at[0], 1, (lat + 1, lon))),
    ]
    for side, column in ((0, west), (1, east)):
        for slot in range(3):
            step = 1 - slot
            sends_it = (None, south, north)[step]
            gets_it = (None, north, south)[step]
            copies.append(
                (
                    sends_it,
                    gets_it,
                    made(
                        edges.at[side],
                        edge_slots.at[side, slot],
                        2 + side * 3 + slot,
                        (lat + step, column),
                    ),
                )
            )
    return copies


def guarded(condition, action):
    if condition is None:
        action()
    else:
        pl.when(condition)(action)


def halo_start(copies):
    for sends_it, _, made in copies:
        guarded(sends_it, made.start)


def halo_arrive(copies):
    for _, gets_it, made in copies:
        guarded(gets_it, made.wait_recv)


def halo_leave(copies):
    for sends_it, _, made in copies:
        guarded(sends_it, made.wait_send)


def halo_greet(barrier):
    lat, lon = lax.axis_index("lat"), lax.axis_index("lon")
    bands, sectors = lax.axis_size("lat"), lax.axis_size("lon")
    west, east = (lon + sectors - 1) % sectors, (lon + 1) % sectors

    def signal(row, column):
        pl.semaphore_signal(barrier, inc=1, device_id=(row, column), device_id_type=MESH)

    signal(lat, west)
    signal(lat, east)

    @pl.when(lat > 0)
    def _():
        for column in (west, lon, east):
            signal(lat - 1, column)

    @pl.when(lat < bands - 1)
    def _():
        for column in (west, lon, east):
            signal(lat + 1, column)

    north, south = (lat + bands - 1) // bands, (2 * bands - 2 - lat) // bands
    return 2 + 3 * north + 3 * south


def edge_pair(top, bottom, last):
    sub = lax.broadcasted_iota(jnp.int32, (8, top.shape[1]), 0)
    west = jnp.where(sub == 0, top[0:1], bottom[0:1])
    east = jnp.where(sub == 0, top[last : last + 1], bottom[last : last + 1])
    return west, east


def halo_row(index, base, edge_slots, valid, lanes=slice(None)):
    slot, row = ((0, 1), (1, 0), (1, 1), (2, 0))[index]
    place = lax.broadcasted_iota(jnp.int32, base.shape, 0)
    east = edge_slots[0, slot, row : row + 1, lanes]
    west = edge_slots[1, slot, row : row + 1, lanes]
    value = jnp.where(place == valid, east, jnp.where(place == CELLS - 1, west, base))
    lat, bands = lax.axis_index("lat"), lax.axis_size("lat")
    if index == 0:
        value = jnp.where(lat > 0, value, 0.0)
    if index == 3:
        value = jnp.where(lat < bands - 1, value, 0.0)
    return value


def inside(shape, valid):
    return lax.broadcasted_iota(jnp.int32, shape, 0) < valid


def inverse_rms(values):
    return lax.rsqrt(jnp.mean(values * values, axis=-1, keepdims=True) + EPSILON)


def nt_dot(left, right):
    return lax.dot_general(
        left, right, (((1,), (1,)), ((), ())), preferred_element_type=jnp.float32
    )


def forward_kernel(
    state_ref,
    cot_ref,
    bias_ref,
    first_gain,
    expand_ref,
    depth_ref,
    shrink_ref,
    second_gain,
    in_ref,
    out_ref,
    items_ref,
    act_ref,
    slope_ref,
    slope_expanded_ref,
    mixed_ref,
    normed_ref,
    inner_ref,
    second_ref,
    slope_edges,
    rows,
    edges,
    row_slots,
    edge_slots,
    wide_normed,
    total_ref,
    project_ref,
    cot_pad,
    sends,
    recvs,
):
    f32, bf16 = jnp.float32, jnp.bfloat16
    valid = state_ref.shape[1]
    barrier = pltpu.get_barrier_semaphore()
    greetings = halo_greet(barrier)
    rows[...] = jnp.zeros(rows.shape, bf16)
    cot_pad[...] = jnp.zeros(cot_pad.shape, bf16)
    for i in range(2):
        rows[i, 0:valid, :] = state_ref[i]
        cot_pad[i * CELLS : i * CELLS + valid, :] = cot_ref[i]
    west, east = edge_pair(rows[0].astype(f32), rows[1].astype(f32), valid - 1)
    edges[0] = west
    edges[1] = east
    pl.semaphore_wait(barrier, greetings)
    copies = halo_copies(rows, edges, row_slots, edge_slots, sends, recvs)
    halo_start(copies)
    project_ref[:, 1536:2048] = nt_dot(cot_pad[...], out_ref[...]).astype(bf16)
    total_ref[...] = jnp.zeros(total_ref.shape, f32)
    halo_arrive(copies)
    for r in range(4):
        base = rows[r - 1] if r in (1, 2) else row_slots[r // 3]
        value = halo_row(r, base.astype(f32), edge_slots, valid)
        value = (value * inverse_rms(value) * first_gain[...]).astype(bf16)
        wide_normed[r * CELLS : r * CELLS + CELLS, :] = value
        if r in (1, 2):
            keep = inside(value.shape, valid)
            own = jnp.where(keep, value.astype(f32), 0.0).astype(bf16)
            normed_ref[(r - 1) * CELLS : r * CELLS, :] = own

    def chunk(index, carry):
        lanes = pl.ds(pl.multiple_of(index * CHUNK, CHUNK), CHUNK)
        expanded = jnp.dot(wide_normed[...], expand_ref[:, lanes], preferred_element_type=f32)
        activated, slope = silu_parts(expanded)
        activated = activated.astype(bf16)
        slope_expanded_ref[:, lanes] = slope[CELLS : 3 * CELLS].astype(bf16)
        planes = []
        for r in range(4):
            plane = activated[r * CELLS : r * CELLS + CELLS]
            act_ref[r, :, lanes] = plane
            planes.append(plane.astype(f32))
        mixes, slopes = [], []
        for i in range(2):
            sums = []
            for b in range(3):
                part = depth_ref[b : b + 1, lanes] * planes[i]
                for a in (1, 2):
                    part = part + depth_ref[a * 3 + b : a * 3 + b + 1, lanes] * planes[i + a]
                sums.append(part)
            convolved = pltpu.roll(sums[0], 1, 0) + sums[1] + pltpu.roll(sums[2], CELLS - 1, 0)
            mixed, slope = silu_parts(convolved)
            keep = inside(mixed.shape, valid)
            mixes.append(jnp.where(keep, mixed, 0.0).astype(bf16))
            slope = jnp.where(keep, slope, 0.0)
            slope_ref[i, :, lanes] = slope.astype(bf16)
            slopes.append(slope)
        west, east = edge_pair(slopes[0], slopes[1], valid - 1)
        slope_edges[0, :, lanes] = west
        slope_edges[1, :, lanes] = east
        mixed = jnp.concatenate(mixes, axis=0)
        mixed_ref[:, lanes] = mixed
        total_ref[...] += jnp.dot(
            mixed,
            shrink_ref[pl.ds(pl.multiple_of(index * CHUNK, CHUNK), CHUNK), :],
            preferred_element_type=f32,
        )
        return carry

    lax.fori_loop(0, expand_ref.shape[1] // CHUNK, chunk, 0)
    for i in range(2):
        inner = (rows[i].astype(f32) + total_ref[i * CELLS : i * CELLS + CELLS, :]).astype(bf16)
        inner_ref[i * CELLS : i * CELLS + CELLS, :] = inner
        inner = inner.astype(f32)
        second = (inner * inverse_rms(inner) * second_gain[...]).astype(bf16)
        second_ref[i * CELLS : i * CELLS + CELLS, :] = second
    project_ref[:, 0:1536] = jnp.dot(
        second_ref[...], in_ref[...], preferred_element_type=f32
    ).astype(bf16)
    lane = lax.broadcasted_iota(jnp.int32, (CELLS, 128), 1)
    row = lax.broadcasted_iota(jnp.int32, (CELLS, 128), 0)
    for i in range(2):
        for tile in range(4):
            parts = [
                project_ref[
                    i * CELLS : i * CELLS + CELLS, part * 512 + tile * 128 : part * 512 + tile * 128 + 128
                ].astype(f32)
                for part in range(4)
            ]
            for u in range(4):
                item = i * 16 + tile * 4 + u
                moved = [
                    value if part == u else pltpu.roll(value, ((part - u) * 32) % 128, 1)
                    for part, value in enumerate(parts)
                ]
                value = jnp.where(
                    lane < 64,
                    jnp.where(lane < 32, moved[0], moved[1]),
                    jnp.where(lane < 96, moved[2], moved[3]),
                )
                value = jnp.where(row == valid, bias_ref[item : item + 1, :], value)
                items_ref[item] = value.astype(bf16)
    halo_leave(copies)


def forward_pass(state, cotangent, bias, first_gain, expand, depth, shrink, second_gain, weight_in, weight_out):
    f32, bf16 = jnp.float32, jnp.bfloat16
    vmem = pl.BlockSpec(memory_space=pltpu.VMEM)
    cells, wide, channels = 2 * CELLS, expand.shape[1], expand.shape[0]
    shaped = jax.ShapeDtypeStruct
    return pl.pallas_call(
        forward_kernel,
        out_shape=(
            shaped((32, CELLS, 128), bf16),
            shaped((4, CELLS, wide), bf16),
            shaped((2, CELLS, wide), bf16),
            shaped((cells, wide), bf16),
            shaped((cells, wide), bf16),
            shaped((cells, channels), bf16),
            shaped((cells, channels), bf16),
            shaped((cells, channels), bf16),
            shaped((2, 8, wide), f32),
        ),
        in_specs=[vmem] * 10,
        out_specs=(vmem,) * 9,
        scratch_shapes=[
            pltpu.VMEM((2, CELLS, channels), bf16),
            pltpu.VMEM((2, 8, channels), f32),
            pltpu.VMEM((2, CELLS, channels), bf16),
            pltpu.VMEM((2, 3, 8, channels), f32),
            pltpu.VMEM((4 * CELLS, channels), bf16),
            pltpu.VMEM((cells, channels), f32),
            pltpu.VMEM((cells, 4 * channels), bf16),
            pltpu.VMEM((cells, channels), bf16),
            pltpu.SemaphoreType.DMA((8,)),
            pltpu.SemaphoreType.DMA((8,)),
        ],
        compiler_params=pltpu.CompilerParams(
            vmem_limit_bytes=40 * 1024 * 1024, collective_id=3, has_side_effects=True
        ),
        name="forward",
    )(state, cotangent, bias, first_gain, expand, depth, shrink, second_gain, weight_in, weight_out)


def attend_kernel(
    valid,
    scale,
    items_ref,
    slope_ref,
    slope_edges,
    near_ref,
    last_ref,
    slope_rows,
    slope_sides,
    x_ref,
    near_send,
    last_send,
    xt_ref,
    kaug_ref,
    vaug_ref,
    t_ref,
    pb_ref,
    acc_ref,
    cell_ref,
    in_send,
    in_recv,
    near_send_sem,
    near_recv_sem,
    last_send_sem,
    last_recv_sem,
    halo_sends,
    halo_recvs,
):
    sources = items_ref.shape[0]
    total = sources * CELLS
    block = t_ref.shape[1]
    group = block // CELLS
    log2e = 1.4426950408889634
    to_log2 = scale * log2e
    f32, bf16 = jnp.float32, jnp.bfloat16
    lat, lon = lax.axis_index("lat"), lax.axis_index("lon")
    z, low = lon // 4, lon % 4

    def partner(k, sign):
        ring, side = k // 4, 3 - k % 4
        half = (ring + 1) // 2
        shift = 4 + (1 - 2 * (ring % 2)) * half
        x_lo, core = low // 2, low % 2
        x_lo = x_lo + (side // 2) * (1 - 2 * x_lo)
        core = core + (side % 2) * (1 - 2 * core)
        return ((z + sign * shift + 8) % 8) * 4 + x_lo * 2 + core

    barrier = pltpu.get_barrier_semaphore()

    def greet(k, carry):
        pl.semaphore_signal(
            barrier, inc=1, device_id=(lat, partner(k, 1)), device_id_type=MESH
        )
        return carry

    lax.fori_loop(0, sources - 1, greet, 0)
    greetings = halo_greet(barrier)
    pl.semaphore_wait(barrier, greetings + sources - 1)

    def incoming(k, slot):
        to = partner(k, 1)
        return pltpu.make_async_remote_copy(
            src_ref=items_ref.at[to],
            dst_ref=x_ref.at[slot],
            send_sem=in_send.at[k],
            recv_sem=in_recv.at[k],
            device_id=(lat, to),
            device_id_type=MESH,
        )

    def push(k, carry):
        incoming(k, lon).start()
        return carry

    lax.fori_loop(0, sources - 1, push, 0)
    halo = halo_copies(slope_ref, slope_edges, slope_rows, slope_sides, halo_sends, halo_recvs)
    halo_start(halo)
    x_ref[lon] = items_ref[lon]

    def prepare(index):
        raw = x_ref[index].astype(f32)
        row = lax.broadcasted_iota(jnp.int32, (CELLS, 128), 0)
        lane = lax.broadcasted_iota(jnp.int32, (CELLS, 128), 1)
        bias_row = jnp.broadcast_to(raw[valid : valid + 1, :], (CELLS, 128))
        bias = jnp.sum(jnp.where(row == lane, bias_row, 0.0), axis=1, keepdims=True) * log2e
        bias = jnp.broadcast_to(bias, (CELLS, 128))
        first = bias.astype(bf16).astype(f32)
        second = (bias - first).astype(bf16).astype(f32)
        third = bias - first - second
        first = jnp.where(row < valid, first, -1e30)
        second = jnp.where(row < valid, second, 0.0)
        third = jnp.where(row < valid, third, 0.0)
        cell = jnp.where(row < valid, raw, 0.0)
        key = jnp.where((lane >= 32) & (lane < 64), cell, 0.0)
        value = jnp.where((lane >= 64) & (lane < 96), cell, 0.0)
        keys = pltpu.roll(key, 96, 1) + key + pltpu.roll(key, 32, 1)
        keys = jnp.where(lane == 96, first, keys)
        keys = jnp.where(lane == 97, second, keys)
        keys = jnp.where(lane == 98, third, keys)
        values = pltpu.roll(value, 64, 1) + pltpu.roll(value, 96, 1)
        values = jnp.where((lane >= 64) & (lane < 67), 1.0, values)
        start = pl.multiple_of(index * CELLS, 32)
        kaug_ref[pl.ds(start, CELLS), :] = keys.astype(bf16)
        vaug_ref[pl.ds(start, CELLS), :] = values.astype(bf16)
        cell_ref[pl.ds(start, CELLS), :] = cell

    prepare(lon)

    def arrive(k, carry):
        source = partner(k, -1)
        incoming(k, source).wait_recv()
        prepare(source)
        return carry

    lax.fori_loop(0, sources - 1, arrive, 0)

    def turn(index, carry):
        start = pl.multiple_of(index * block, block)
        xt_ref[:, pl.ds(start, block)] = cell_ref[pl.ds(start, block), :].T.astype(bf16)
        acc_ref[:, pl.ds(start, block)] = jnp.zeros((64, block), f32)
        return carry

    lax.fori_loop(0, total // block, turn, 0)

    def packed(cells):
        return (cells[:48] + pltpu.roll(cells[48:], 64, 1)).astype(bf16)

    def nearby(source, slot):
        return pltpu.make_async_remote_copy(
            src_ref=near_send.at[source],
            dst_ref=near_ref.at[slot],
            send_sem=near_send_sem.at[source],
            recv_sem=near_recv_sem.at[slot],
            device_id=(lat, source),
            device_id_type=MESH,
        )

    def one_block(turn_index, carry):
        index = (turn_index + lon // group) % (sources // group)
        start = pl.multiple_of(index * block, block)
        xt = xt_ref[:, pl.ds(start, block)].astype(f32)
        query = xt[0:32] * to_log2
        first = query.astype(bf16).astype(f32)
        second = (query - first).astype(bf16).astype(f32)
        third = query - first - second
        qaug = jnp.concatenate(
            [first, second, third, jnp.ones((32, block), f32)], axis=0
        ).astype(bf16)
        t = jnp.dot(kaug_ref[...], qaug, preferred_element_type=f32)
        t_ref[...] = t
        highest = jnp.max(jnp.max(t.reshape(total // 8, 8, block), axis=0), axis=0, keepdims=True)
        p = jnp.exp2(t_ref[...] - highest)
        t_ref[...] = p
        low_p = p.astype(bf16)
        pb_ref[...] = low_p
        norm = jnp.sum(p.reshape(total // 8, 8, block), axis=0)
        heads = jnp.dot(xt_ref[64:96, :], low_p, preferred_element_type=f32)
        inverse = 1.0 / jnp.sum(norm, axis=0, keepdims=True)
        heads = heads * inverse
        back = xt[96:128]
        centred = jnp.sum(back * heads, axis=0, keepdims=True) * inverse
        back = back * inverse
        back_first = back.astype(bf16).astype(f32)
        back_second = back - back_first
        cen_first = centred.astype(bf16).astype(f32)
        cen_second = (centred - cen_first).astype(bf16).astype(f32)
        cen_third = centred - cen_first - cen_second
        sub = lax.broadcasted_iota(jnp.int32, (64, block), 0)
        cen = jnp.where(
            sub == 0,
            cen_first,
            jnp.where(sub == 1, cen_second, jnp.where(sub == 2, cen_third, 0.0)),
        )
        baug = jnp.concatenate([back_first, back_second, -cen], axis=0).astype(bf16)
        nt = (((1,), (1,)), ((), ()))
        dp = jnp.dot(vaug_ref[...], baug, preferred_element_type=f32)
        ds = (t_ref[...] * dp).astype(bf16)
        acc_ref[32:64, :] += lax.dot_general(
            back_first.astype(bf16), pb_ref[...], nt, preferred_element_type=f32
        )
        acc_ref[0:32, :] += lax.dot_general(
            xt_ref[0:32, pl.ds(start, block)], ds, nt, preferred_element_type=f32
        )
        back_queries = jnp.dot(xt_ref[32:64, :], ds, preferred_element_type=f32)
        zeros = jnp.zeros((64, block), f32)
        done = jnp.concatenate([back_queries * scale, heads, zeros], axis=0).T
        for part in range(group):
            source = index * group + part
            near_send[source] = packed(done[part * CELLS : part * CELLS + CELLS])

            @pl.when(source != lon)
            def _():
                nearby(source, lon).start()

        return carry

    lax.fori_loop(0, total // block, one_block, 0)
    near_ref[lon] = near_send[lon]

    def finish(index, carry):
        start = pl.multiple_of(index * block, block)
        both = acc_ref[:, pl.ds(start, block)]
        zeros = jnp.zeros((64, block), f32)
        both = jnp.concatenate([both[0:32] * scale, both[32:64], zeros], axis=0)
        cell_ref[pl.ds(start, block), :] = both.T
        return carry

    lax.fori_loop(0, total // block, finish, 0)

    def final(k, to, slot):
        return pltpu.make_async_remote_copy(
            src_ref=last_send.at[to],
            dst_ref=last_ref.at[slot],
            send_sem=last_send_sem.at[k],
            recv_sem=last_recv_sem.at[k],
            device_id=(lat, to),
            device_id_type=MESH,
        )

    def pack_last(source):
        start = pl.multiple_of(source * CELLS, 32)
        last_send[source] = packed(cell_ref[pl.ds(start, CELLS), :])

    def leave(k, carry):
        to = partner(k, 1)
        pack_last(to)
        final(k, to, lon).start()
        return carry

    lax.fori_loop(0, sources - 1, leave, 0)
    pack_last(lon)
    last_ref[lon] = last_send[lon]

    def settle(k, carry):
        to, source = partner(k, 1), partner(k, -1)
        incoming(k, lon).wait_send()
        nearby(to, lon).wait_send()
        nearby(source, source).wait_recv()
        made = final(k, to, source)
        made.wait_send()
        made.wait_recv()
        return carry

    lax.fori_loop(0, sources - 1, settle, 0)
    halo_arrive(halo)
    halo_leave(halo)


def attend_items(items, slope, slope_edges, valid, scale):
    sources = items.shape[0]
    total = sources * CELLS
    block = 768
    f32, bf16 = jnp.float32, jnp.bfloat16
    vmem = pl.BlockSpec(memory_space=pltpu.VMEM)
    answer = jax.ShapeDtypeStruct((sources, 48, 128), bf16)
    return pl.pallas_call(
        functools.partial(attend_kernel, valid, scale),
        out_shape=(
            answer,
            answer,
            jax.ShapeDtypeStruct(slope.shape, bf16),
            jax.ShapeDtypeStruct((2, 3, 8, slope.shape[2]), f32),
        ),
        in_specs=[vmem] * 3,
        out_specs=(vmem,) * 4,
        scratch_shapes=[
            pltpu.VMEM((sources, CELLS, 128), bf16),
            pltpu.VMEM((sources, 48, 128), bf16),
            pltpu.VMEM((sources, 48, 128), bf16),
            pltpu.VMEM((128, total), bf16),
            pltpu.VMEM((total, 128), bf16),
            pltpu.VMEM((total, 128), bf16),
            pltpu.VMEM((total, block), f32),
            pltpu.VMEM((total, block), bf16),
            pltpu.VMEM((64, total), f32),
            pltpu.VMEM((total, 128), f32),
        ]
        + [pltpu.SemaphoreType.DMA((sources,))] * 6
        + [pltpu.SemaphoreType.DMA((8,))] * 2,
        compiler_params=pltpu.CompilerParams(
            vmem_limit_bytes=48 * 1024 * 1024, collective_id=2, has_side_effects=True
        ),
        name="attend",
    )(items, slope, slope_edges)


def backward_kernel(
    factor,
    near_ref,
    last_ref,
    cot_ref,
    state_ref,
    first_gain,
    expand_ref,
    depth_ref,
    shrink_ref,
    second_gain,
    in_ref,
    weight_out_ref,
    act_ref,
    slope_ref,
    slope_expanded_ref,
    mixed_ref,
    normed_ref,
    inner_ref,
    second_ref,
    slope_rows,
    slope_sides,
    field_ref,
    grad_ref,
    block_ref,
    sums_ref,
    ga,
    gb,
    ra0,
    rb0,
    ra1,
    rb1,
    a1,
    b1,
    ra2,
    rb2,
    ab2,
    rz,
    small,
    s0,
    small0,
    smallz,
    smally,
    smallx,
    cot_pad,
    heads_ref,
    project_ref,
    rows,
    edges,
    row_slots,
    edge_slots,
    wide_back,
    back_normed,
    halo_sends,
    halo_recvs,
    core_sends,
    core_recvs,
    send_sems,
    recv_sems,
):
    f32, bf16 = jnp.float32, jnp.bfloat16
    valid = state_ref.shape[1]
    lat, lon = lax.axis_index("lat"), lax.axis_index("lon")
    x_hi, y = lat // 4, lat % 4
    z, x_lo, core = lon // 4, (lon // 2) % 2, lon % 2
    x = x_hi * 2 + x_lo

    def place(px, py, pz, pc):
        return ((px // 2) * 4 + py, pz * 4 + (px % 2) * 2 + pc)

    other = 1 - core
    sibling = place(x, y, z, other)
    x_peers = [place((x + d) % 4, y, z, core) for d in range(1, 4)]
    y_peers = [place(x, (y + d) % 4, z, core) for d in range(1, 4)]
    z_peers = [place(x, y, (z + d) % 8, core) for d in range(1, 8)]
    barrier = pltpu.get_barrier_semaphore()
    greetings = halo_greet(barrier)
    peers = [sibling] + x_peers + y_peers + z_peers
    for peer in peers:
        pl.semaphore_signal(barrier, inc=1, device_id=peer, device_id_type=MESH)

    cot_pad[...] = jnp.zeros(cot_pad.shape, bf16)
    small[...] = jnp.zeros(small.shape, f32)
    for i in range(2):
        cot_pad[i * CELLS : i * CELLS + valid, :] = cot_ref[i]

    half_lane = lax.broadcasted_iota(jnp.int32, (48, 128), 1)

    def gather(parts, first, second, i, tile):
        cells = slice(tile * 128, tile * 128 + 128)
        for target, column, source in ((first[0], first[1], 0), (second[0], second[1], 32)):
            for half in range(2):
                value = None
                for u in range(4):
                    shift = (u * 32 - source - half * 64) % 128
                    moved = pltpu.roll(parts[u], shift, 1) if shift else parts[u]
                    value = moved if value is None else jnp.where(half_lane < u * 32, value, moved)
                start = i * CELLS + half * 48
                target[start : start + 48, column + cells.start : column + cells.stop] = value.astype(bf16)

    for i in range(2):
        for tile in range(4):
            items = [i * 16 + tile * 4 + u for u in range(4)]
            gather(
                [near_ref[item].astype(f32) for item in items],
                (project_ref, 0),
                (heads_ref, 0),
                i,
                tile,
            )
            gather(
                [last_ref[item].astype(f32) for item in items],
                (project_ref, 512),
                (project_ref, 1024),
                i,
                tile,
            )

    back_second = nt_dot(project_ref[...], in_ref[...])
    field = jnp.dot(heads_ref[...], weight_out_ref[...], preferred_element_type=f32)
    gain_two = jnp.zeros((1, field.shape[1]), f32)
    for i in range(2):
        part = slice(i * CELLS, i * CELLS + CELLS)
        inner = inner_ref[part, :].astype(f32)
        field_ref[i] = (inner + field[part]).astype(bf16)[0:valid]
        inverse = inverse_rms(inner)
        gain_two = gain_two + jnp.sum(back_second[part] * inner * inverse, axis=0, keepdims=True)
        scaled = back_second[part] * second_gain[...]
        back = (
            cot_pad[part, :].astype(f32)
            + inverse * scaled
            - inverse * inverse * inverse * inner * jnp.mean(scaled * inner, axis=-1, keepdims=True)
        )
        rows[i] = back.astype(bf16)
    west, east = edge_pair(rows[0].astype(f32), rows[1].astype(f32), valid - 1)
    edges[0] = west
    edges[1] = east
    pl.semaphore_wait(barrier, greetings + len(peers))
    halo = halo_copies(rows, edges, row_slots, edge_slots, halo_sends, halo_recvs)
    halo_start(halo)

    def half_lanes(top, bottom):
        lane = lax.broadcasted_iota(jnp.int32, top.shape, 1)
        even = jnp.where(lane < 64, top, pltpu.roll(bottom, 64, 1))
        odd = jnp.where(lane < 64, pltpu.roll(top, 64, 1), bottom)
        return even, odd

    def cross(left, right):
        return (
            lax.dot_general(left, right, (((0,), (0,)), ((), ())), preferred_element_type=f32)
            * factor
        )

    def core_copy(source, target, index):
        return pltpu.make_async_remote_copy(
            src_ref=source,
            dst_ref=target,
            send_sem=core_sends.at[index],
            recv_sem=core_recvs.at[index],
            device_id=sibling,
            device_id_type=MESH,
        )

    def core_a(pz):
        return core_copy(ga.at[other, pz], ra0.at[pz], pz)

    def core_b(zz):
        return core_copy(gb.at[other, pl.ds(zz * 2, 2)], rb0.at[pl.ds(zz * 2, 2)], 8 + zz)

    def other_part(zz, carry):
        columns = pl.ds(pl.multiple_of(zz * 128, 128), 128)
        own = jnp.concatenate([rows[0, :, columns], rows[1, :, columns]], axis=0)
        shrink = cross(own, mixed_ref[...])
        grad_in = cross(
            project_ref[:, pl.ds(pl.multiple_of(zz * 384, 128), 384)], second_ref[...]
        )
        grad_out = cross(cot_pad[:, columns], heads_ref[...])
        for sub in range(8):
            pz, plo, pc = zz * 2 + sub // 4, (sub // 2) % 2, sub % 2
            for plat in range(8):
                px, py = (plat // 4) * 2 + plo, plat % 4
                part = slice(sub * 16, sub * 16 + 16)
                ga[pc, pz, px, py, 32:48, :] = shrink[
                    part, plat * 256 : plat * 256 + 128
                ].astype(bf16)
                gb[pc, pz, py, px, 0:16, :] = shrink[
                    part, plat * 256 + 128 : plat * 256 + 256
                ].astype(bf16)
            for pair in range(4):
                tile = slice(pair * 128, pair * 128 + 128)
                top = jnp.concatenate(
                    [grad_in[sub * 48 : sub * 48 + 24, tile], grad_out[sub * 16 : sub * 16 + 8, tile]],
                    axis=0,
                )
                bottom = jnp.concatenate(
                    [
                        grad_in[sub * 48 + 24 : sub * 48 + 48, tile],
                        grad_out[sub * 16 + 8 : sub * 16 + 16, tile],
                    ],
                    axis=0,
                )
                parts = half_lanes(top, bottom)
                for odd in range(2):
                    plat = pair * 2 + odd
                    px, py = (plat // 4) * 2 + plo, plat % 4
                    gb[pc, pz, py, px, 16:48, :] = parts[odd].astype(bf16)
        core_b(zz).start()
        return carry

    lax.fori_loop(0, 4, other_part, 0)
    halo_arrive(halo)
    for r in range(4):
        base = rows[r - 1] if r in (1, 2) else row_slots[r // 3]
        value = halo_row(r, base.astype(f32), edge_slots, valid)
        wide_back[r * CELLS : r * CELLS + CELLS, :] = value.astype(bf16)
    back_normed[...] = jnp.zeros(back_normed.shape, f32)

    def chunk(pz, carry):
        start = pl.multiple_of(pz * CHUNK, CHUNK)
        lanes = pl.ds(start, CHUNK)
        product = nt_dot(wide_back[...], shrink_ref[lanes, :])
        planes = []
        for r in range(4):
            base = slope_ref[r - 1, :, lanes] if r in (1, 2) else slope_rows[r // 3, :, lanes]
            slope = halo_row(r, base.astype(f32), slope_sides, valid, lanes)
            plane = product[r * CELLS : r * CELLS + CELLS] * slope
            planes.append(plane.astype(bf16).astype(f32))
        grads = []
        for b in range(3):
            turned = []
            for i in range(2):
                centre = planes[i + 1]
                centre = jnp.where(inside(centre.shape, valid), centre, 0.0)
                turned.append(pltpu.roll(centre, (CELLS + b - 1) % CELLS, 0) if b != 1 else centre)
            for a in range(3):
                value = act_ref[a, :, lanes].astype(f32) * turned[0]
                value = value + act_ref[a + 1, :, lanes].astype(f32) * turned[1]
                small[a * 3 + b : a * 3 + b + 1, lanes] = (
                    jnp.sum(value, axis=0, keepdims=True) * factor
                )
        outs = []
        for i in range(2):
            sums = []
            for b in range(3):
                part = depth_ref[b : b + 1, lanes] * planes[i + 2]
                for a in (1, 2):
                    part = part + depth_ref[a * 3 + b : a * 3 + b + 1, lanes] * planes[i + 2 - a]
                sums.append(part)
            total = pltpu.roll(sums[0], CELLS - 1, 0) + sums[1] + pltpu.roll(sums[2], 1, 0)
            total = total * slope_expanded_ref[i * CELLS : i * CELLS + CELLS, lanes].astype(f32)
            outs.append(jnp.where(inside(total.shape, valid), total, 0.0).astype(bf16))
        back = jnp.concatenate(outs, axis=0)
        back_normed[...] += nt_dot(back, expand_ref[:, lanes])
        grad = cross(back, normed_ref[...])
        for sub in range(4):
            plo, pc = sub // 2, sub % 2
            for pair in range(4):
                tile = slice(pair * 128, pair * 128 + 128)
                parts = half_lanes(
                    grad[sub * 64 : sub * 64 + 32, tile], grad[sub * 64 + 32 : sub * 64 + 64, tile]
                )
                for odd in range(2):
                    plat = pair * 2 + odd
                    px, py = (plat // 4) * 2 + plo, plat % 4
                    ga[pc, pz, px, py, 0:32, :] = parts[odd].astype(bf16)
        core_a(pz).start()
        return carry

    count = [0]

    def copy(source, target, peer):
        index = count[0]
        count[0] += 1
        made = pltpu.make_async_remote_copy(
            src_ref=source,
            dst_ref=target,
            send_sem=send_sems.at[index],
            recv_sem=recv_sems.at[index],
            device_id=peer,
            device_id_type=MESH,
        )
        made.start()
        return made

    def add_pair(mine, theirs, pz):
        for q in range(4):
            mine[core, pz, q] = (mine[core, pz, q].astype(f32) + theirs[pz, q].astype(f32)).astype(bf16)

    def arrive_b(zz, carry):
        core_b(zz).wait_recv()
        add_pair(gb, rb0, zz * 2)
        add_pair(gb, rb0, zz * 2 + 1)
        return carry

    def arrive_a(pz, carry):
        core_a(pz).wait_recv()
        add_pair(ga, ra0, pz)
        return carry

    lax.fori_loop(0, 4, chunk, 0)
    lax.fori_loop(0, 4, arrive_b, 0)
    next_b = [
        copy(gb.at[core, :, (y + d) % 4], rb1.at[d - 1], y_peers[d - 1]) for d in (1, 2, 3)
    ]
    lax.fori_loop(4, 8, chunk, 0)
    lax.fori_loop(0, 8, arrive_a, 0)
    next_a = [
        copy(ga.at[core, :, (x + d) % 4], ra1.at[d - 1], x_peers[d - 1]) for d in (1, 2, 3)
    ]

    gain_one = jnp.zeros((1, back_normed.shape[1]), f32)
    for i in range(2):
        part = slice(i * CELLS, i * CELLS + valid)
        state = state_ref[i].astype(f32)
        inverse = inverse_rms(state)
        back = back_normed[part, :]
        gain_one = gain_one + jnp.sum(back * state * inverse, axis=0, keepdims=True)
        scaled = back * first_gain[...]
        grad_ref[i] = (
            rows[i, 0:valid, :].astype(f32)
            + inverse * scaled
            - inverse * inverse * inverse * state * jnp.mean(scaled * state, axis=-1, keepdims=True)
        ).astype(bf16)
    width = small.shape[1]
    small[9:10, :] = jnp.concatenate(
        [gain_one * factor, gain_two * factor, jnp.zeros((1, width - 1024), f32)], axis=1
    )
    half = width // 2
    small_lanes = pl.ds(pl.multiple_of(other * half, half), half)
    s0[...] = small[0:16, small_lanes]
    small_core = copy(s0, small0, sibling)
    small_core.wait_recv()
    total = small[0:16, pl.ds(pl.multiple_of(core * half, half), half)] + small0[...]
    smallz[z] = total
    small_z = [copy(smallz.at[z], smallz.at[z], peer) for peer in z_peers]

    def add_four(mine, theirs, total):
        def body(pz, carry):
            value = mine(pz).astype(f32)
            for d in range(3):
                value = value + theirs[d, pz].astype(f32)
            total[pz] = value.astype(bf16)
            return carry

        lax.fori_loop(0, 8, body, 0)

    for made in next_b:
        made.wait_recv()
    add_four(lambda pz: gb[core, pz, y], rb1, b1)
    last_b = [copy(b1.at[:, (x + d) % 4], rb2.at[d - 1], x_peers[d - 1]) for d in (1, 2, 3)]
    for made in next_a:
        made.wait_recv()
    add_four(lambda pz: ga[core, pz, x], ra1, a1)
    last_a = [copy(a1.at[:, (y + d) % 4], ra2.at[d - 1], y_peers[d - 1]) for d in (1, 2, 3)]

    for made in small_z:
        made.wait_recv()
    total = smallz[0]
    for index in range(1, 8):
        total = total + smallz[index]
    smally[y] = total
    small_y = [copy(smally.at[y], smally.at[y], peer) for peer in y_peers]

    def finish_pair(mine, theirs, first_row):
        def body(pz, carry):
            value = mine(pz).astype(f32)
            for d in range(3):
                value = value + theirs[d, pz].astype(f32)
            ab2[pz, first_row : first_row + 48, :] = value.astype(bf16)
            return carry

        lax.fori_loop(0, 8, body, 0)

    for made in last_b:
        made.wait_recv()
    finish_pair(lambda pz: b1[pz, x], rb2, 48)
    for made in last_a:
        made.wait_recv()
    finish_pair(lambda pz: a1[pz, y], ra2, 0)
    last = [copy(ab2.at[(z + d) % 8], rz.at[d - 1], z_peers[d - 1]) for d in range(1, 8)]

    for made in small_y:
        made.wait_recv()
    total = (smally[0] + smally[1]) + (smally[2] + smally[3])
    smallx[x] = total
    small_x = [copy(smallx.at[x], smallx.at[x], peer) for peer in x_peers]

    for made in last:
        made.wait_recv()
    value = ab2[z].astype(f32)
    for d in range(7):
        value = value + rz[d].astype(f32)
    block_ref[...] = value

    for made in small_x:
        made.wait_recv()
    sums_ref[core] = (smallx[0] + smallx[1]) + (smallx[2] + smallx[3])
    final = copy(sums_ref.at[core], sums_ref.at[core], sibling)
    final.wait_recv()
    for made in [small_core, final] + next_a + next_b + last_a + last_b + last + small_z + small_y + small_x:
        made.wait_send()
    halo_leave(halo)

    def leave_a(pz, carry):
        core_a(pz).wait_send()
        return carry

    def leave_b(zz, carry):
        core_b(zz).wait_send()
        return carry

    lax.fori_loop(0, 8, leave_a, 0)
    lax.fori_loop(0, 4, leave_b, 0)


def backward_pass(factor, *operands):
    f32, bf16 = jnp.float32, jnp.bfloat16
    vmem = pl.BlockSpec(memory_space=pltpu.VMEM)
    state = operands[3]
    channels, wide = operands[5].shape
    cells = 2 * CELLS
    half = wide // 2
    copies = 1 + 1 + 12 + 7 + 7 + 3 + 3
    shaped = jax.ShapeDtypeStruct
    return pl.pallas_call(
        functools.partial(backward_kernel, factor),
        out_shape=(
            shaped(state.shape, bf16),
            shaped(state.shape, bf16),
            shaped((96, 128), f32),
            shaped((2, 16, half), f32),
        ),
        in_specs=[vmem] * len(operands),
        out_specs=(vmem,) * 4,
        scratch_shapes=[
            pltpu.VMEM((2, 8, 4, 4, 48, 128), bf16),
            pltpu.VMEM((2, 8, 4, 4, 48, 128), bf16),
            pltpu.VMEM((8, 4, 4, 48, 128), bf16),
            pltpu.VMEM((8, 4, 4, 48, 128), bf16),
            pltpu.VMEM((3, 8, 4, 48, 128), bf16),
            pltpu.VMEM((3, 8, 4, 48, 128), bf16),
            pltpu.VMEM((8, 4, 48, 128), bf16),
            pltpu.VMEM((8, 4, 48, 128), bf16),
            pltpu.VMEM((3, 8, 48, 128), bf16),
            pltpu.VMEM((3, 8, 48, 128), bf16),
            pltpu.VMEM((8, 96, 128), bf16),
            pltpu.VMEM((7, 96, 128), bf16),
            pltpu.VMEM((16, wide), f32),
            pltpu.VMEM((16, half), f32),
            pltpu.VMEM((16, half), f32),
            pltpu.VMEM((8, 16, half), f32),
            pltpu.VMEM((4, 16, half), f32),
            pltpu.VMEM((4, 16, half), f32),
            pltpu.VMEM((cells, channels), bf16),
            pltpu.VMEM((cells, channels), bf16),
            pltpu.VMEM((cells, 3 * channels), bf16),
            pltpu.VMEM((2, CELLS, channels), bf16),
            pltpu.VMEM((2, 8, channels), f32),
            pltpu.VMEM((2, CELLS, channels), bf16),
            pltpu.VMEM((2, 3, 8, channels), f32),
            pltpu.VMEM((4 * CELLS, channels), bf16),
            pltpu.VMEM((cells, channels), f32),
            pltpu.SemaphoreType.DMA((8,)),
            pltpu.SemaphoreType.DMA((8,)),
            pltpu.SemaphoreType.DMA((12,)),
            pltpu.SemaphoreType.DMA((12,)),
            pltpu.SemaphoreType.DMA((copies,)),
            pltpu.SemaphoreType.DMA((copies,)),
        ],
        compiler_params=pltpu.CompilerParams(
            vmem_limit_bytes=52 * 1024 * 1024, collective_id=4, has_side_effects=True
        ),
        name="backward",
    )(*operands)


def owner_blocks(block):
    def unfold(part):
        return jnp.concatenate([part[:, :64], part[:, 64:]], axis=0).T

    expand = unfold(block[0:32])
    shrink = jnp.concatenate([block[32:48], block[48:64]], axis=1).T
    grad_in = unfold(block[64:88])
    grad_out = unfold(block[88:96])
    return expand, shrink, grad_in, grad_out


def per_device(
    state_field,
    cotangent,
    key_bias,
    input_gain,
    expand_weight,
    depth_weight,
    shrink_weight,
    attention_gain,
    attention_in,
    attention_out,
):
    row_count, lon_count, channels = state_field.shape
    head_count = key_bias.shape[2]
    wide_count = expand_weight.shape[1]
    norm_factor = 1.0 / math.sqrt(
        row_count * lon_count * lax.axis_size("lat") * lax.axis_size("lon")
    )
    score_scale = 1.0 / math.sqrt(channels // head_count)
    bias = key_bias.astype(jnp.float32).transpose(0, 2, 1)
    bias = bias.reshape(row_count * head_count, lon_count)
    bias = jnp.pad(bias, ((0, 0), (0, 128 - lon_count)))
    depth = depth_weight.astype(jnp.float32).reshape(9, wide_count)
    first_gain = input_gain.reshape(1, channels)
    second_gain = attention_gain.reshape(1, channels)
    items, act, slope, slope_expanded, mixed, normed, inner, second, slope_edges = forward_pass(
        state_field,
        cotangent,
        bias,
        first_gain,
        expand_weight,
        depth,
        shrink_weight,
        second_gain,
        attention_in,
        attention_out,
    )
    near, last, slope_rows, slope_sides = attend_items(
        items, slope, slope_edges, lon_count, score_scale
    )
    output_field, input_grad, block, sums = backward_pass(
        norm_factor,
        near,
        last,
        cotangent,
        state_field,
        first_gain,
        expand_weight,
        depth,
        shrink_weight,
        second_gain,
        attention_in,
        attention_out,
        act,
        slope,
        slope_expanded,
        mixed,
        normed,
        inner,
        second,
        slope_rows,
        slope_sides,
    )
    depth_grad = jnp.concatenate([sums[0, :9], sums[1, :9]], axis=1).reshape(3, 3, wide_count)
    gains = sums[0, 9]
    return (
        output_field,
        input_grad,
        *owner_blocks(block),
        depth_grad,
        gains[:channels],
        gains[channels : 2 * channels],
    )


def solution(mesh):
    placed = (
        P("lat", "lon", None),
        P("lat", "lon", None),
        P("lat", "lon", None),
        P(),
        P(),
        P(),
        P(),
        P(),
        P(),
        P(),
    )
    return jax.shard_map(
        per_device,
        mesh=mesh,
        in_specs=placed,
        out_specs=(
            P("lat", "lon", None),
            P("lat", "lon", None),
            P("lat", "lon"),
            P("lat", "lon"),
            P("lat", "lon"),
            P("lat", "lon"),
            P(),
            P(),
            P(),
        ),
        check_vma=False,
    )
```

```python
import functools
import math

import jax
import jax.numpy as jnp
from jax import lax
from jax.experimental import pallas as pl
from jax.experimental.pallas import tpu as pltpu
from jax.sharding import PartitionSpec as P

EPSILON = 1e-06
CELLS = 96
MESH = pl.DeviceIdType.MESH
VMEM_MIB = 60


CHUNK = 256


def silu_parts(values):
    sigmoid = 1.0 / (1.0 + jnp.exp(-values))
    return values * sigmoid, sigmoid * (1.0 + values * (1.0 - sigmoid))


def halo_copies(rows, edges, row_slots, edge_slots, sends, recvs):
    lat, lon = lax.axis_index("lat"), lax.axis_index("lon")
    bands, sectors = lax.axis_size("lat"), lax.axis_size("lon")
    west, east = (lon + sectors - 1) % sectors, (lon + 1) % sectors

    def made(source, target, index, peer):
        return pltpu.make_async_remote_copy(
            src_ref=source,
            dst_ref=target,
            send_sem=sends.at[index],
            recv_sem=recvs.at[index],
            device_id=peer,
            device_id_type=MESH,
        )

    north, south = lat > 0, lat < bands - 1
    copies = [
        (north, south, made(rows.at[0], row_slots.at[1], 0, (lat - 1, lon))),
        (south, north, made(rows.at[1], row_slots.at[0], 1, (lat + 1, lon))),
    ]
    for side, column in ((0, west), (1, east)):
        for slot in range(3):
            step = 1 - slot
            sends_it = (None, south, north)[step]
            gets_it = (None, north, south)[step]
            copies.append(
                (
                    sends_it,
                    gets_it,
                    made(
                        edges.at[side],
                        edge_slots.at[side, slot],
                        2 + side * 3 + slot,
                        (lat + step, column),
                    ),
                )
            )
    return copies


def guarded(condition, action):
    if condition is None:
        action()
    else:
        pl.when(condition)(action)


def halo_start(copies):
    for sends_it, _, made in copies:
        guarded(sends_it, made.start)


def halo_arrive(copies):
    for _, gets_it, made in copies:
        guarded(gets_it, made.wait_recv)


def halo_leave(copies):
    for sends_it, _, made in copies:
        guarded(sends_it, made.wait_send)


def halo_greet(barrier):
    lat, lon = lax.axis_index("lat"), lax.axis_index("lon")
    bands, sectors = lax.axis_size("lat"), lax.axis_size("lon")
    west, east = (lon + sectors - 1) % sectors, (lon + 1) % sectors

    def signal(row, column):
        pl.semaphore_signal(barrier, inc=1, device_id=(row, column), device_id_type=MESH)

    signal(lat, west)
    signal(lat, east)

    @pl.when(lat > 0)
    def _():
        for column in (west, lon, east):
            signal(lat - 1, column)

    @pl.when(lat < bands - 1)
    def _():
        for column in (west, lon, east):
            signal(lat + 1, column)

    north, south = (lat + bands - 1) // bands, (2 * bands - 2 - lat) // bands
    return 2 + 3 * north + 3 * south


def edge_pair(top, bottom, last):
    sub = lax.broadcasted_iota(jnp.int32, (8, top.shape[1]), 0)
    west = jnp.where(sub == 0, top[0:1], bottom[0:1])
    east = jnp.where(sub == 0, top[last : last + 1], bottom[last : last + 1])
    return west, east


def halo_row(index, base, edge_slots, valid, lanes=slice(None)):
    slot, row = ((0, 1), (1, 0), (1, 1), (2, 0))[index]
    place = lax.broadcasted_iota(jnp.int32, base.shape, 0)
    east = edge_slots[0, slot, row : row + 1, lanes]
    west = edge_slots[1, slot, row : row + 1, lanes]
    value = jnp.where(place == valid, east, jnp.where(place == CELLS - 1, west, base))
    lat, bands = lax.axis_index("lat"), lax.axis_size("lat")
    if index == 0:
        value = jnp.where(lat > 0, value, 0.0)
    if index == 3:
        value = jnp.where(lat < bands - 1, value, 0.0)
    return value


def inside(shape, valid):
    return lax.broadcasted_iota(jnp.int32, shape, 0) < valid


def inverse_rms(values):
    return lax.rsqrt(jnp.mean(values * values, axis=-1, keepdims=True) + EPSILON)


def nt_dot(left, right):
    return lax.dot_general(
        left, right, (((1,), (1,)), ((), ())), preferred_element_type=jnp.float32
    )


class Refs:
    def __init__(self, names, refs):
        for name, ref in zip(names, refs, strict=True):
            setattr(self, name, ref)


def exchange(source, target, sends, recvs, index, peer, landing=None):
    return pltpu.make_async_remote_copy(
        src_ref=source,
        dst_ref=target,
        send_sem=sends.at[index],
        recv_sem=recvs.at[index if landing is None else landing],
        device_id=peer,
        device_id_type=MESH,
    )


def partner(k, sign):
    lon = lax.axis_index("lon")
    z, low = lon // 4, lon % 4
    ring, side = k // 4, 3 - k % 4
    half = (ring + 1) // 2
    shift = 4 + (1 - 2 * (ring % 2)) * half
    x_lo, core = low // 2, low % 2
    x_lo = x_lo + (side // 2) * (1 - 2 * x_lo)
    core = core + (side % 2) * (1 - 2 * core)
    return ((z + sign * shift + 8) % 8) * 4 + x_lo * 2 + core


def packed(cells):
    return (cells[:48] + pltpu.roll(cells[48:], 64, 1)).astype(jnp.bfloat16)


def unpacked(pair):
    lane = lax.broadcasted_iota(jnp.int32, (48, 128), 1)
    pair = pair.astype(jnp.float32)
    top = jnp.where(lane < 64, pair, 0.0)
    bottom = jnp.where(lane < 64, pltpu.roll(pair, 64, 1), 0.0)
    return jnp.concatenate([top, bottom], axis=0)


def forward_phase(r, load, valid, greetings):
    f32, bf16 = jnp.float32, jnp.bfloat16
    r.rows[...] = jnp.zeros(r.rows.shape, bf16)
    r.cot_pad[...] = jnp.zeros(r.cot_pad.shape, bf16)
    load["state"].wait()
    for i in range(2):
        r.rows[i, 0:valid, :] = r.state[i]
    west, east = edge_pair(r.rows[0].astype(f32), r.rows[1].astype(f32), valid - 1)
    r.edges[0] = west
    r.edges[1] = east
    pl.semaphore_wait(pltpu.get_barrier_semaphore(), greetings)
    copies = halo_copies(r.rows, r.edges, r.row_slots, r.edge_slots, r.state_sends, r.state_recvs)
    halo_start(copies)
    load["cot"].wait()
    load["out"].wait()
    for i in range(2):
        r.cot_pad[i * CELLS : i * CELLS + valid, :] = r.cot[i]
    r.projected[:, 1536:2048] = nt_dot(r.cot_pad[...], r.weight_out[...]).astype(bf16)
    r.total[...] = jnp.zeros(r.total.shape, f32)
    load["expand"].wait()
    load["shrink"].wait()
    halo_arrive(copies)
    for row in range(4):
        base = r.rows[row - 1] if row in (1, 2) else r.row_slots[row // 3]
        value = halo_row(row, base.astype(f32), r.edge_slots, valid)
        value = (value * inverse_rms(value) * r.first_gain[...]).astype(bf16)
        r.wide_normed[row * CELLS : row * CELLS + CELLS, :] = value
        if row in (1, 2):
            own = jnp.where(inside(value.shape, valid), value.astype(f32), 0.0).astype(bf16)
            r.normed[(row - 1) * CELLS : row * CELLS, :] = own

    def chunk(index, carry):
        start = pl.multiple_of(index * CHUNK, CHUNK)
        lanes = pl.ds(start, CHUNK)
        expanded = jnp.dot(r.wide_normed[...], r.expand[:, lanes], preferred_element_type=f32)
        activated, slope = silu_parts(expanded)
        activated = activated.astype(bf16)
        r.slope_expanded[:, lanes] = slope[CELLS : 3 * CELLS].astype(bf16)
        planes = []
        for row in range(4):
            plane = activated[row * CELLS : row * CELLS + CELLS]
            r.act[row, :, lanes] = plane
            planes.append(plane.astype(f32))
        mixes, slopes = [], []
        for i in range(2):
            sums = []
            for b in range(3):
                part = r.depth[b : b + 1, lanes] * planes[i]
                for a in (1, 2):
                    part = part + r.depth[a * 3 + b : a * 3 + b + 1, lanes] * planes[i + a]
                sums.append(part)
            convolved = pltpu.roll(sums[0], 1, 0) + sums[1] + pltpu.roll(sums[2], CELLS - 1, 0)
            mixed, slope = silu_parts(convolved)
            keep = inside(mixed.shape, valid)
            mixes.append(jnp.where(keep, mixed, 0.0).astype(bf16))
            slope = jnp.where(keep, slope, 0.0)
            r.slope[i, :, lanes] = slope.astype(bf16)
            slopes.append(slope)
        west, east = edge_pair(slopes[0], slopes[1], valid - 1)
        r.slope_edges[0, :, lanes] = west
        r.slope_edges[1, :, lanes] = east
        mixed = jnp.concatenate(mixes, axis=0)
        r.mixed[:, lanes] = mixed
        r.total[...] += jnp.dot(
            mixed, r.shrink[pl.ds(start, CHUNK), :], preferred_element_type=f32
        )
        return carry

    lax.fori_loop(0, r.expand.shape[1] // CHUNK, chunk, 0)
    for i in range(2):
        part = slice(i * CELLS, i * CELLS + CELLS)
        inner = (r.rows[i].astype(f32) + r.total[part, :]).astype(bf16)
        r.inner[part, :] = inner
        inner = inner.astype(f32)
        r.second[part, :] = (inner * inverse_rms(inner) * r.second_gain[...]).astype(bf16)
    load["in"].wait()
    return copies


def project_and_pack(r, valid, first, last, target, with_bias):
    f32, bf16 = jnp.float32, jnp.bfloat16
    lane = lax.broadcasted_iota(jnp.int32, (CELLS, 128), 1)
    row = lax.broadcasted_iota(jnp.int32, (CELLS, 128), 0)
    for i in range(2):
        cells = slice(i * CELLS, i * CELLS + CELLS)
        for tile in range(4):
            parts = [
                r.projected[cells, base + tile * 128 : base + tile * 128 + 128].astype(f32)
                for base in (first, last)
            ]
            for u in range(4):
                item = i * 16 + tile * 4 + u
                moved = [
                    value if side == u else pltpu.roll(value, ((side - u) * 32) % 128, 1)
                    for side, value in enumerate(parts)
                ]
                value = jnp.where(lane < 32, moved[0], jnp.where(lane < 64, moved[1], 0.0))
                if with_bias:
                    value = jnp.where(row == valid, r.bias[2 * item : 2 * item + 1, :], value)
                    value = jnp.where(row == valid + 1, r.bias[2 * item + 1 : 2 * item + 2, :], value)
                target[item] = packed(value)


def attention_phase(r, valid, scale):
    sources = r.kv_in.shape[0]
    total = sources * CELLS
    block = r.scores.shape[1]
    group = block // CELLS
    log2e = 1.4426950408889634
    to_log2 = scale * log2e
    f32, bf16 = jnp.float32, jnp.bfloat16
    lat, lon = lax.axis_index("lat"), lax.axis_index("lon")
    groups = sources // group

    def key_copy(k, to, slot):
        return exchange(
            r.kv_out.at[to], r.kv_in.at[slot], r.kv_sends, r.kv_recvs, k, (lat, to)
        )

    def query_copy(to, slot):
        return exchange(
            r.qd_out.at[to], r.qd_in.at[slot], r.qd_sends, r.qd_recvs, to, (lat, to), slot
        )

    def near_copy(to, slot):
        return exchange(
            r.near_out.at[to], r.near_in.at[slot], r.near_sends, r.near_recvs, to, (lat, to), slot
        )

    def last_copy(k, to, slot):
        return exchange(
            r.last_out.at[to], r.last_in.at[slot], r.last_sends, r.last_recvs, k, (lat, to)
        )

    r.projected[:, 512:1536] = jnp.dot(
        r.second[...], r.weight_in[:, 512:1536], preferred_element_type=f32
    ).astype(bf16)
    project_and_pack(r, valid, 512, 1024, r.kv_out, True)

    def push_keys(k, carry):
        key_copy(k, partner(k, 1), lon).start()
        return carry

    lax.fori_loop(0, sources - 1, push_keys, 0)
    r.projected[:, 0:512] = jnp.dot(
        r.second[...], r.weight_in[:, 0:512], preferred_element_type=f32
    ).astype(bf16)
    project_and_pack(r, valid, 0, 1536, r.qd_out, False)

    def push_queries(step, carry):
        to = ((lon // group + groups - step // group) % groups) * group + step % group

        @pl.when(to != lon)
        def _():
            query_copy(to, lon).start()

        return carry

    lax.fori_loop(0, sources, push_queries, 0)
    halo = halo_copies(
        r.slope, r.slope_edges, r.slope_rows, r.slope_sides, r.slope_sends, r.slope_recvs
    )
    halo_start(halo)
    r.kv_in[lon] = r.kv_out[lon]
    r.qd_in[lon] = r.qd_out[lon]

    def prepare(index):
        raw = unpacked(r.kv_in[index])
        row = lax.broadcasted_iota(jnp.int32, (CELLS, 128), 0)
        lane = lax.broadcasted_iota(jnp.int32, (CELLS, 128), 1)
        bias_row = jnp.where(row < 48, raw[valid : valid + 1, :], raw[valid + 1 : valid + 2, :])
        wanted = jnp.where(row < 48, row, row - 48)
        bias = jnp.sum(jnp.where(wanted == lane, bias_row, 0.0), axis=1, keepdims=True) * log2e
        bias = jnp.broadcast_to(bias, (CELLS, 128))
        first = bias.astype(bf16).astype(f32)
        second = (bias - first).astype(bf16).astype(f32)
        third = bias - first - second
        first = jnp.where(row < valid, first, -1e30)
        second = jnp.where(row < valid, second, 0.0)
        third = jnp.where(row < valid, third, 0.0)
        cell = jnp.where(row < valid, raw, 0.0)
        key = jnp.where(lane < 32, cell, 0.0)
        value = jnp.where(lane >= 32, cell, 0.0)
        keys = key + pltpu.roll(key, 32, 1) + pltpu.roll(key, 64, 1)
        keys = jnp.where(lane == 96, first, keys)
        keys = jnp.where(lane == 97, second, keys)
        keys = jnp.where(lane == 98, third, keys)
        values = value + pltpu.roll(value, 96, 1)
        values = jnp.where((lane >= 64) & (lane < 67), 1.0, values)
        start = pl.multiple_of(index * CELLS, 32)
        r.kaug[pl.ds(start, CELLS), :] = keys.astype(bf16)
        r.vaug[pl.ds(start, CELLS), :] = values.astype(bf16)
        r.cell[pl.ds(start, CELLS), :] = cell

    prepare(lon)

    def arrive(k, carry):
        source = partner(k, -1)
        key_copy(k, source, source).wait_recv()
        prepare(source)
        return carry

    lax.fori_loop(0, sources - 1, arrive, 0)

    def turn(index, carry):
        start = pl.multiple_of(index * block, block)
        r.xt[:, pl.ds(start, block)] = r.cell[pl.ds(start, block), :].T[0:64].astype(bf16)
        r.acc[:, pl.ds(start, block)] = jnp.zeros((64, block), f32)
        return carry

    lax.fori_loop(0, total // block, turn, 0)

    def one_block(turn_index, carry):
        index = (turn_index + lon // group) % groups
        for part in range(group):
            source = index * group + part

            @pl.when(source != lon)
            def _():
                query_copy(source, source).wait_recv()

            r.qd_cell[part * CELLS : part * CELLS + CELLS, :] = unpacked(r.qd_in[source])
        xt = r.qd_cell[...].T
        query = xt[0:32] * to_log2
        first = query.astype(bf16).astype(f32)
        second = (query - first).astype(bf16).astype(f32)
        third = query - first - second
        qaug = jnp.concatenate(
            [first, second, third, jnp.ones((32, block), f32)], axis=0
        ).astype(bf16)
        t = jnp.dot(r.kaug[...], qaug, preferred_element_type=f32)
        r.scores[...] = t
        highest = jnp.max(jnp.max(t.reshape(total // 8, 8, block), axis=0), axis=0, keepdims=True)
        p = jnp.exp2(r.scores[...] - highest)
        r.scores[...] = p
        low_p = p.astype(bf16)
        r.low[...] = low_p
        norm = jnp.sum(p.reshape(total // 8, 8, block), axis=0)
        heads = jnp.dot(r.xt[32:64, :], low_p, preferred_element_type=f32)
        inverse = 1.0 / jnp.sum(norm, axis=0, keepdims=True)
        heads = heads * inverse
        back = xt[32:64]
        centred = jnp.sum(back * heads, axis=0, keepdims=True) * inverse
        back = back * inverse
        back_first = back.astype(bf16).astype(f32)
        back_second = back - back_first
        cen_first = centred.astype(bf16).astype(f32)
        cen_second = (centred - cen_first).astype(bf16).astype(f32)
        cen_third = centred - cen_first - cen_second
        sub = lax.broadcasted_iota(jnp.int32, (64, block), 0)
        cen = jnp.where(
            sub == 0,
            cen_first,
            jnp.where(sub == 1, cen_second, jnp.where(sub == 2, cen_third, 0.0)),
        )
        baug = jnp.concatenate([back_first, back_second, -cen], axis=0).astype(bf16)
        dp = jnp.dot(r.vaug[...], baug, preferred_element_type=f32)
        ds = (r.scores[...] * dp).astype(bf16)
        r.acc[32:64, :] += nt_dot(back_first.astype(bf16), r.low[...])
        r.acc[0:32, :] += nt_dot(xt[0:32].astype(bf16), ds)
        back_queries = jnp.dot(r.xt[0:32, :], ds, preferred_element_type=f32)
        zeros = jnp.zeros((64, block), f32)
        done = jnp.concatenate([back_queries * scale, heads, zeros], axis=0).T
        for part in range(group):
            source = index * group + part
            r.near_out[source] = packed(done[part * CELLS : part * CELLS + CELLS])

            @pl.when(source != lon)
            def _():
                near_copy(source, lon).start()

        return carry

    lax.fori_loop(0, groups, one_block, 0)
    r.near_in[lon] = r.near_out[lon]

    def finish(index, carry):
        start = pl.multiple_of(index * block, block)
        both = r.acc[:, pl.ds(start, block)]
        zeros = jnp.zeros((64, block), f32)
        both = jnp.concatenate([both[0:32] * scale, both[32:64], zeros], axis=0)
        r.cell[pl.ds(start, block), :] = both.T
        return carry

    lax.fori_loop(0, total // block, finish, 0)

    def pack_last(source):
        start = pl.multiple_of(source * CELLS, 32)
        r.last_out[source] = packed(r.cell[pl.ds(start, CELLS), :])

    def leave(k, carry):
        to = partner(k, 1)
        pack_last(to)
        last_copy(k, to, lon).start()
        return carry

    lax.fori_loop(0, sources - 1, leave, 0)
    pack_last(lon)
    r.last_in[lon] = r.last_out[lon]

    def near_arrive(k, carry):
        source = partner(k, -1)
        near_copy(source, source).wait_recv()
        return carry

    def last_arrive(k, carry):
        source = partner(k, -1)
        last_copy(k, source, source).wait_recv()
        return carry

    def settle(k, carry):
        to = partner(k, 1)
        key_copy(k, to, lon).wait_send()
        query_copy(to, lon).wait_send()
        near_copy(to, lon).wait_send()
        last_copy(k, to, lon).wait_send()
        return carry

    return (
        halo,
        lambda: lax.fori_loop(0, sources - 1, near_arrive, 0),
        lambda: lax.fori_loop(0, sources - 1, last_arrive, 0),
        lambda: lax.fori_loop(0, sources - 1, settle, 0),
    )


def gather_heads(source, first, second, i, tile):
    half_lane = lax.broadcasted_iota(jnp.int32, (48, 128), 1)
    parts = [source[i * 16 + tile * 4 + u].astype(jnp.float32) for u in range(4)]
    for (target, column), lane in ((first, 0), (second, 32)):
        for half in range(2):
            value = None
            for u in range(4):
                shift = (u * 32 - lane - half * 64) % 128
                moved = pltpu.roll(parts[u], shift, 1) if shift else parts[u]
                value = moved if value is None else jnp.where(half_lane < u * 32, value, moved)
            start, column_start = i * CELLS + half * 48, column + tile * 128
            target[start : start + 48, column_start : column_start + 128] = value.astype(
                jnp.bfloat16
            )


def backward_phase(r, valid, factor, slope_halo, near_arrive, last_arrive, peers):
    f32, bf16 = jnp.float32, jnp.bfloat16
    sibling, x_peers, y_peers, z_peers = peers
    lat, lon = lax.axis_index("lat"), lax.axis_index("lon")
    y = lat % 4
    z, x_lo, core = lon // 4, (lon // 2) % 2, lon % 2
    x = (lat // 4) * 2 + x_lo
    other = 1 - core
    r.small[...] = jnp.zeros(r.small.shape, f32)
    near_arrive()
    for i in range(2):
        for tile in range(4):
            gather_heads(r.near_in, (r.back_project, 0), (r.heads, 0), i, tile)
    field = jnp.dot(r.heads[...], r.weight_out[...], preferred_element_type=f32)
    for i in range(2):
        part = slice(i * CELLS, i * CELLS + CELLS)
        r.field[i] = (r.inner[part, :].astype(f32) + field[part]).astype(bf16)[0:valid]
    back_second = nt_dot(r.back_project[:, 0:512], r.weight_in[:, 0:512])
    last_arrive()
    for i in range(2):
        for tile in range(4):
            gather_heads(r.last_in, (r.back_project, 512), (r.back_project, 1024), i, tile)
    back_second = back_second + nt_dot(r.back_project[:, 512:1536], r.weight_in[:, 512:1536])
    gain_two = jnp.zeros((1, field.shape[1]), f32)
    for i in range(2):
        part = slice(i * CELLS, i * CELLS + CELLS)
        inner = r.inner[part, :].astype(f32)
        inverse = inverse_rms(inner)
        gain_two = gain_two + jnp.sum(back_second[part] * inner * inverse, axis=0, keepdims=True)
        scaled = back_second[part] * r.second_gain[...]
        back = (
            r.cot_pad[part, :].astype(f32)
            + inverse * scaled
            - inverse * inverse * inverse * inner * jnp.mean(scaled * inner, axis=-1, keepdims=True)
        )
        r.back_rows[i] = back.astype(bf16)
    west, east = edge_pair(r.back_rows[0].astype(f32), r.back_rows[1].astype(f32), valid - 1)
    r.back_edges[0] = west
    r.back_edges[1] = east
    halo = halo_copies(
        r.back_rows, r.back_edges, r.back_slots, r.back_sides, r.back_sends, r.back_recvs
    )
    halo_start(halo)

    def half_lanes(top, bottom):
        lane = lax.broadcasted_iota(jnp.int32, top.shape, 1)
        even = jnp.where(lane < 64, top, pltpu.roll(bottom, 64, 1))
        odd = jnp.where(lane < 64, pltpu.roll(top, 64, 1), bottom)
        return even, odd

    def cross(left, right):
        return (
            lax.dot_general(left, right, (((0,), (0,)), ((), ())), preferred_element_type=f32)
            * factor
        )

    def core_copy(mine, theirs, first, width, index):
        rows = pl.ds(first, width)
        return exchange(
            mine.at[other, rows], theirs.at[rows], r.core_sends, r.core_recvs, index, sibling
        )

    def early_x(zz):
        return core_copy(r.ex, r.ex0, zz * 2, 2, zz)

    def early_y(zz):
        return core_copy(r.ey, r.ey0, zz * 2, 2, 4 + zz)

    def late_x(pz):
        return core_copy(r.lx, r.lx0, pz, 1, 8 + pz)

    def late_y(pz):
        return core_copy(r.ly, r.ly0, pz, 1, 16 + pz)

    def early_part(zz, carry):
        columns = pl.ds(pl.multiple_of(zz * 128, 128), 128)
        own = jnp.concatenate([r.back_rows[0, :, columns], r.back_rows[1, :, columns]], axis=0)
        shrink = cross(own, r.mixed[...])
        grad_in = cross(
            r.back_project[:, pl.ds(pl.multiple_of(zz * 384, 128), 384)], r.second[...]
        )
        grad_out = cross(r.cot_pad[:, columns], r.heads[...])
        for sub in range(8):
            pz, plo, pc = zz * 2 + sub // 4, (sub // 2) % 2, sub % 2
            for plat in range(8):
                px, py = (plat // 4) * 2 + plo, plat % 4
                part = slice(sub * 16, sub * 16 + 16)
                for side in range(2):
                    column = plat * 256 + side * 128
                    r.ex[pc, pz, px, py, side * 16 : side * 16 + 16, :] = shrink[
                        part, column : column + 128
                    ].astype(bf16)
            for pair in range(4):
                tile = slice(pair * 128, pair * 128 + 128)
                top = jnp.concatenate(
                    [grad_in[sub * 48 : sub * 48 + 24, tile], grad_out[sub * 16 : sub * 16 + 8, tile]],
                    axis=0,
                )
                bottom = jnp.concatenate(
                    [
                        grad_in[sub * 48 + 24 : sub * 48 + 48, tile],
                        grad_out[sub * 16 + 8 : sub * 16 + 16, tile],
                    ],
                    axis=0,
                )
                parts = half_lanes(top, bottom)
                for odd in range(2):
                    plat = pair * 2 + odd
                    px, py = (plat // 4) * 2 + plo, plat % 4
                    r.ey[pc, pz, py, px] = parts[odd].astype(bf16)
        early_x(zz).start()
        early_y(zz).start()
        return carry

    lax.fori_loop(0, 4, early_part, 0)

    def add_pair(mine, theirs, pz):
        for q in range(4):
            mine[core, pz, q] = (mine[core, pz, q].astype(f32) + theirs[pz, q].astype(f32)).astype(bf16)

    def early_arrive(zz, carry):
        early_x(zz).wait_recv()
        early_y(zz).wait_recv()
        for step in range(2):
            add_pair(r.ex, r.ex0, zz * 2 + step)
            add_pair(r.ey, r.ey0, zz * 2 + step)
        return carry

    lax.fori_loop(0, 4, early_arrive, 0)
    count = [0]

    def copy(source, target, peer):
        index = count[0]
        count[0] += 1
        made = exchange(source, target, r.sends, r.recvs, index, peer)
        made.start()
        return made

    def stage_one(mine, slots, targets, here):
        return [
            copy(mine.at[core, :, (here + d) % 4], slots.at[d - 1], targets[d - 1])
            for d in (1, 2, 3)
        ]

    early_one_x = stage_one(r.ex, r.ex1, x_peers, x)
    early_one_y = stage_one(r.ey, r.ey1, y_peers, y)
    halo_arrive(slope_halo)
    halo_arrive(halo)
    for row in range(4):
        base = r.back_rows[row - 1] if row in (1, 2) else r.back_slots[row // 3]
        value = halo_row(row, base.astype(f32), r.back_sides, valid)
        r.wide_back[row * CELLS : row * CELLS + CELLS, :] = value.astype(bf16)
    r.back_normed[...] = jnp.zeros(r.back_normed.shape, f32)

    def chunk(pz, carry):
        start = pl.multiple_of(pz * CHUNK, CHUNK)
        lanes = pl.ds(start, CHUNK)
        product = nt_dot(r.wide_back[...], r.shrink[lanes, :])
        planes = []
        for row in range(4):
            base = r.slope[row - 1, :, lanes] if row in (1, 2) else r.slope_rows[row // 3, :, lanes]
            slope = halo_row(row, base.astype(f32), r.slope_sides, valid, lanes)
            plane = product[row * CELLS : row * CELLS + CELLS] * slope
            planes.append(plane.astype(bf16).astype(f32))
        for b in range(3):
            turned = []
            for i in range(2):
                centre = planes[i + 1]
                centre = jnp.where(inside(centre.shape, valid), centre, 0.0)
                turned.append(pltpu.roll(centre, (CELLS + b - 1) % CELLS, 0) if b != 1 else centre)
            for a in range(3):
                value = r.act[a, :, lanes].astype(f32) * turned[0]
                value = value + r.act[a + 1, :, lanes].astype(f32) * turned[1]
                r.small[a * 3 + b : a * 3 + b + 1, lanes] = (
                    jnp.sum(value, axis=0, keepdims=True) * factor
                )
        outs = []
        for i in range(2):
            sums = []
            for b in range(3):
                part = r.depth[b : b + 1, lanes] * planes[i + 2]
                for a in (1, 2):
                    part = part + r.depth[a * 3 + b : a * 3 + b + 1, lanes] * planes[i + 2 - a]
                sums.append(part)
            total = pltpu.roll(sums[0], CELLS - 1, 0) + sums[1] + pltpu.roll(sums[2], 1, 0)
            total = total * r.slope_expanded[i * CELLS : i * CELLS + CELLS, lanes].astype(f32)
            outs.append(jnp.where(inside(total.shape, valid), total, 0.0).astype(bf16))
        back = jnp.concatenate(outs, axis=0)
        r.back_normed[...] += nt_dot(back, r.expand[:, lanes])
        grad = cross(back, r.normed[...])
        for sub in range(4):
            plo, pc = sub // 2, sub % 2
            for pair in range(4):
                tile = slice(pair * 128, pair * 128 + 128)
                parts = half_lanes(
                    grad[sub * 64 : sub * 64 + 32, tile], grad[sub * 64 + 32 : sub * 64 + 64, tile]
                )
                for odd in range(2):
                    plat = pair * 2 + odd
                    px, py = (plat // 4) * 2 + plo, plat % 4
                    r.lx[pc, pz, px, py] = parts[odd][0:16].astype(bf16)
                    r.ly[pc, pz, py, px] = parts[odd][16:32].astype(bf16)
        late_x(pz).start()
        late_y(pz).start()
        return carry

    lax.fori_loop(0, 8, chunk, 0)

    def late_arrive(pz, carry):
        late_x(pz).wait_recv()
        late_y(pz).wait_recv()
        add_pair(r.lx, r.lx0, pz)
        add_pair(r.ly, r.ly0, pz)
        return carry

    lax.fori_loop(0, 8, late_arrive, 0)
    late_one_x = stage_one(r.lx, r.lx1, x_peers, x)
    late_one_y = stage_one(r.ly, r.ly1, y_peers, y)

    def add_four(mine, theirs, here, total):
        def body(pz, carry):
            value = mine[core, pz, here].astype(f32)
            for d in range(3):
                value = value + theirs[d, pz].astype(f32)
            total[pz] = value.astype(bf16)
            return carry

        lax.fori_loop(0, 8, body, 0)

    def stage_two(arrivals, mine, slots, here, total, next_slots, targets, there):
        for made in arrivals:
            made.wait_recv()
        add_four(mine, slots, here, total)
        return [
            copy(total.at[:, (there + d) % 4], next_slots.at[d - 1], targets[d - 1])
            for d in (1, 2, 3)
        ]

    early_two_x = stage_two(early_one_x, r.ex, r.ex1, x, r.ext, r.ex2, y_peers, y)
    early_two_y = stage_two(early_one_y, r.ey, r.ey1, y, r.eyt, r.ey2, x_peers, x)

    gain_one = jnp.zeros((1, r.back_normed.shape[1]), f32)
    for i in range(2):
        part = slice(i * CELLS, i * CELLS + valid)
        state = r.state[i].astype(f32)
        inverse = inverse_rms(state)
        back = r.back_normed[part, :]
        gain_one = gain_one + jnp.sum(back * state * inverse, axis=0, keepdims=True)
        scaled = back * r.first_gain[...]
        r.grad[i] = (
            r.back_rows[i, 0:valid, :].astype(f32)
            + inverse * scaled
            - inverse * inverse * inverse * state * jnp.mean(scaled * state, axis=-1, keepdims=True)
        ).astype(bf16)
    width = r.small.shape[1]
    r.small[9:10, :] = jnp.concatenate(
        [gain_one * factor, gain_two * factor, jnp.zeros((1, width - 1024), f32)], axis=1
    )
    half = width // 2
    r.small_half[...] = r.small[:, pl.ds(pl.multiple_of(other * half, half), half)]
    small_core = copy(r.small_half, r.small_other, sibling)
    small_core.wait_recv()
    total = r.small[:, pl.ds(pl.multiple_of(core * half, half), half)] + r.small_other[...]
    for index in range(8):
        r.small_split[index] = total[:, index * 128 : index * 128 + 128]
    small_z = [
        copy(r.small_split.at[(z + d) % 8], r.small_z.at[z], z_peers[d - 1]) for d in range(1, 8)
    ]
    r.small_z[z] = r.small_split[z]

    def stage_three(arrivals, total, slots, here, first, count_rows):
        for made in arrivals:
            made.wait_recv()

        def body(pz, carry):
            value = total[pz, here].astype(f32)
            for d in range(3):
                value = value + slots[d, pz].astype(f32)
            r.final[pz, first : first + count_rows, :] = value.astype(bf16)
            return carry

        lax.fori_loop(0, 8, body, 0)

    def send_final(first, count_rows):
        rows = pl.ds(first, count_rows)
        return [
            copy(r.final.at[(z + d) % 8, rows], r.final_in.at[d - 1, rows], z_peers[d - 1])
            for d in range(1, 8)
        ]

    stage_three(early_two_x, r.ext, r.ex2, y, 0, 32)
    stage_three(early_two_y, r.eyt, r.ey2, x, 32, 32)
    final_early = send_final(0, 64)
    late_two_x = stage_two(late_one_x, r.lx, r.lx1, x, r.lxt, r.lx2, y_peers, y)
    late_two_y = stage_two(late_one_y, r.ly, r.ly1, y, r.lyt, r.ly2, x_peers, x)

    for made in small_z:
        made.wait_recv()
    total = r.small_z[0]
    for index in range(1, 8):
        total = total + r.small_z[index]
    r.small_y[y] = total
    small_y = [copy(r.small_y.at[y], r.small_y.at[y], peer) for peer in y_peers]

    stage_three(late_two_x, r.lxt, r.lx2, y, 64, 16)
    stage_three(late_two_y, r.lyt, r.ly2, x, 80, 16)
    final_late = send_final(64, 32)

    for made in small_y:
        made.wait_recv()
    r.small_x[x] = (r.small_y[0] + r.small_y[1]) + (r.small_y[2] + r.small_y[3])
    small_x = [copy(r.small_x.at[x], r.small_x.at[x], peer) for peer in x_peers]
    for made in small_x:
        made.wait_recv()
    r.sums[core, z] = (r.small_x[0] + r.small_x[1]) + (r.small_x[2] + r.small_x[3])
    small_all = [copy(r.sums.at[core, z], r.sums.at[core, z], peer) for peer in z_peers]

    for made in final_early + final_late:
        made.wait_recv()
    value = r.final[z].astype(f32)
    for d in range(7):
        value = value + r.final_in[d].astype(f32)
    r.block[...] = value
    for made in small_all:
        made.wait_recv()
    small_last = copy(r.sums.at[core], r.sums.at[core], sibling)
    small_last.wait_recv()
    for made in (
        early_one_x
        + early_one_y
        + late_one_x
        + late_one_y
        + early_two_x
        + early_two_y
        + late_two_x
        + late_two_y
        + final_early
        + final_late
        + small_z
        + small_y
        + small_x
        + small_all
        + [small_core, small_last]
    ):
        made.wait_send()

    def settle(pz, carry):
        late_x(pz).wait_send()
        late_y(pz).wait_send()
        return carry

    def settle_early(zz, carry):
        early_x(zz).wait_send()
        early_y(zz).wait_send()
        return carry

    lax.fori_loop(0, 8, settle, 0)
    lax.fori_loop(0, 4, settle_early, 0)
    halo_leave(halo)


def step_kernel(names, valid, scale, factor, *refs):
    r = Refs(names, refs)
    lat, lon = lax.axis_index("lat"), lax.axis_index("lon")
    sectors = lax.axis_size("lon")
    y, z, x_lo, core = lat % 4, lon // 4, (lon // 2) % 2, lon % 2
    x = (lat // 4) * 2 + x_lo

    def place(px, py, pz, pc):
        return ((px // 2) * 4 + py, pz * 4 + (px % 2) * 2 + pc)

    barrier = pltpu.get_barrier_semaphore()
    peers = (
        place(x, y, z, 1 - core),
        [place((x + d) % 4, y, z, core) for d in range(1, 4)],
        [place(x, (y + d) % 4, z, core) for d in range(1, 4)],
        [place(x, y, (z + d) % 8, core) for d in range(1, 8)],
    )
    greetings = halo_greet(barrier)
    for peer in peers[1] + peers[2]:
        pl.semaphore_signal(barrier, inc=1, device_id=peer, device_id_type=MESH)

    def greet(k, carry):
        pl.semaphore_signal(barrier, inc=1, device_id=(lat, partner(k, 1)), device_id_type=MESH)
        return carry

    lax.fori_loop(0, sectors - 1, greet, 0)
    greetings = greetings + len(peers[1]) + len(peers[2]) + sectors - 1
    load = {}
    for index, (name, source, target) in enumerate(
        (
            ("state", r.state_hbm, r.state),
            ("cot", r.cot_hbm, r.cot),
            ("out", r.out_hbm, r.weight_out),
            ("expand", r.expand_hbm, r.expand),
            ("shrink", r.shrink_hbm, r.shrink),
            ("in", r.in_hbm, r.weight_in),
        )
    ):
        load[name] = pltpu.make_async_copy(source, target, r.loads.at[index])
        load[name].start()
    state_halo = forward_phase(r, load, valid, greetings)
    slope_halo, near_arrive, last_arrive, settle = attention_phase(r, valid, scale)
    backward_phase(r, valid, factor, slope_halo, near_arrive, last_arrive, peers)
    settle()
    halo_leave(state_halo)
    halo_leave(slope_halo)


def whole_step(factor, scale, operands, bias, depth, first_gain, second_gain):
    f32, bf16 = jnp.float32, jnp.bfloat16
    state, cot, expand, shrink, weight_in, weight_out = operands
    valid = state.shape[1]
    channels, wide = expand.shape
    cells, half = 2 * CELLS, wide // 2
    sources = lax.axis_size("lon")
    total, block = sources * CELLS, 768
    vmem, dma = pltpu.VMEM, pltpu.SemaphoreType.DMA
    message = vmem((sources, 48, 128), bf16)

    def tree(name, rows):
        return {
            name: vmem((2, 8, 4, 4, rows, 128), bf16),
            name + "0": vmem((8, 4, 4, rows, 128), bf16),
            name + "1": vmem((3, 8, 4, rows, 128), bf16),
            name + "t": vmem((8, 4, rows, 128), bf16),
            name + "2": vmem((3, 8, rows, 128), bf16),
        }

    def halo_set(prefix, width):
        return {prefix + "sends": dma((8,)), prefix + "recvs": dma((8,))}

    scratch = {
        "state": vmem(state.shape, bf16),
        "cot": vmem(cot.shape, bf16),
        "expand": vmem(expand.shape, bf16),
        "shrink": vmem(shrink.shape, bf16),
        "weight_in": vmem(weight_in.shape, bf16),
        "weight_out": vmem(weight_out.shape, bf16),
        "rows": vmem((2, CELLS, channels), bf16),
        "edges": vmem((2, 8, channels), f32),
        "row_slots": vmem((2, CELLS, channels), bf16),
        "edge_slots": vmem((2, 3, 8, channels), f32),
        "back_rows": vmem((2, CELLS, channels), bf16),
        "back_edges": vmem((2, 8, channels), f32),
        "back_slots": vmem((2, CELLS, channels), bf16),
        "back_sides": vmem((2, 3, 8, channels), f32),
        "slope": vmem((2, CELLS, wide), bf16),
        "slope_edges": vmem((2, 8, wide), f32),
        "slope_rows": vmem((2, CELLS, wide), bf16),
        "slope_sides": vmem((2, 3, 8, wide), f32),
        "wide_normed": vmem((4 * CELLS, channels), bf16),
        "wide_back": vmem((4 * CELLS, channels), bf16),
        "total": vmem((cells, channels), f32),
        "back_normed": vmem((cells, channels), f32),
        "projected": vmem((cells, 4 * channels), bf16),
        "back_project": vmem((cells, 3 * channels), bf16),
        "heads": vmem((cells, channels), bf16),
        "cot_pad": vmem((cells, channels), bf16),
        "act": vmem((4, CELLS, wide), bf16),
        "slope_expanded": vmem((cells, wide), bf16),
        "mixed": vmem((cells, wide), bf16),
        "normed": vmem((cells, channels), bf16),
        "inner": vmem((cells, channels), bf16),
        "second": vmem((cells, channels), bf16),
        "kv_out": message,
        "kv_in": message,
        "qd_out": message,
        "qd_in": message,
        "near_out": message,
        "near_in": message,
        "last_out": message,
        "last_in": message,
        "xt": vmem((64, total), bf16),
        "kaug": vmem((total, 128), bf16),
        "vaug": vmem((total, 128), bf16),
        "scores": vmem((total, block), f32),
        "low": vmem((total, block), bf16),
        "acc": vmem((64, total), f32),
        "cell": vmem((total, 128), f32),
        "qd_cell": vmem((block, 128), f32),
        **tree("ex", 32),
        **tree("ey", 32),
        **tree("lx", 16),
        **tree("ly", 16),
        "final": vmem((8, 96, 128), bf16),
        "final_in": vmem((7, 96, 128), bf16),
        "small": vmem((16, wide), f32),
        "small_half": vmem((16, half), f32),
        "small_other": vmem((16, half), f32),
        "small_split": vmem((8, 16, 128), f32),
        "small_z": vmem((8, 16, 128), f32),
        "small_y": vmem((4, 16, 128), f32),
        "small_x": vmem((4, 16, 128), f32),
        "loads": dma((6,)),
        "core_sends": dma((24,)),
        "core_recvs": dma((24,)),
        "sends": dma((66,)),
        "recvs": dma((66,)),
    }
    for prefix in ("state_", "slope_", "back_"):
        scratch[prefix + "sends"] = dma((8,))
        scratch[prefix + "recvs"] = dma((8,))
    for prefix in ("kv_", "qd_", "near_", "last_"):
        scratch[prefix + "sends"] = dma((sources,))
        scratch[prefix + "recvs"] = dma((sources,))
    inputs = [name + "_hbm" for name in ("state", "cot", "expand", "shrink", "in", "out")]
    inputs += ["bias", "depth", "first_gain", "second_gain"]
    outputs = {
        "field": (state.shape, bf16),
        "grad": (state.shape, bf16),
        "block": ((96, 128), f32),
        "sums": ((2, 8, 16, 128), f32),
    }
    names = inputs + list(outputs) + list(scratch)
    whole, anywhere = pl.BlockSpec(memory_space=vmem), pl.BlockSpec(memory_space=pl.ANY)
    return pl.pallas_call(
        functools.partial(step_kernel, names, valid, scale, factor),
        out_shape=tuple(jax.ShapeDtypeStruct(*kind) for kind in outputs.values()),
        in_specs=[anywhere] * 6 + [whole] * 4,
        out_specs=(whole,) * 4,
        scratch_shapes=list(scratch.values()),
        compiler_params=pltpu.CompilerParams(
            vmem_limit_bytes=VMEM_MIB * 1024 * 1024, collective_id=1, has_side_effects=True
        ),
        name="step",
    )(*operands, bias, depth, first_gain, second_gain)


def owner_blocks(block):
    def unfold(part):
        return jnp.concatenate([part[:, :64], part[:, 64:]], axis=0).T

    expand = unfold(block[64:96])
    shrink = jnp.concatenate([block[0:16], block[16:32]], axis=1).T
    grad_in = unfold(block[32:56])
    grad_out = unfold(block[56:64])
    return expand, shrink, grad_in, grad_out


def per_device(
    state_field,
    cotangent,
    key_bias,
    input_gain,
    expand_weight,
    depth_weight,
    shrink_weight,
    attention_gain,
    attention_in,
    attention_out,
):
    row_count, lon_count, channels = state_field.shape
    head_count = key_bias.shape[2]
    wide_count = expand_weight.shape[1]
    norm_factor = 1.0 / math.sqrt(
        row_count * lon_count * lax.axis_size("lat") * lax.axis_size("lon")
    )
    score_scale = 1.0 / math.sqrt(channels // head_count)
    bias = key_bias.astype(jnp.float32).transpose(0, 2, 1)
    bias = bias.reshape(row_count * head_count, lon_count)
    bias = jnp.pad(bias, ((0, 0), (0, CELLS - lon_count))).reshape(-1, CELLS // 2)
    bias = jnp.pad(bias, ((0, 0), (0, 128 - CELLS // 2)))
    output_field, input_grad, block, sums = whole_step(
        norm_factor,
        score_scale,
        (state_field, cotangent, expand_weight, shrink_weight, attention_in, attention_out),
        bias,
        depth_weight.astype(jnp.float32).reshape(9, wide_count),
        input_gain.reshape(1, channels),
        attention_gain.reshape(1, channels),
    )
    sums = sums.transpose(2, 0, 1, 3).reshape(16, wide_count)
    return (
        output_field,
        input_grad,
        *owner_blocks(block),
        sums[:9].reshape(3, 3, wide_count),
        sums[9, :channels],
        sums[9, channels : 2 * channels],
    )


def solution(mesh):
    placed = (
        P("lat", "lon", None),
        P("lat", "lon", None),
        P("lat", "lon", None),
        P(),
        P(),
        P(),
        P(),
        P(),
        P(),
        P(),
    )
    return jax.shard_map(
        per_device,
        mesh=mesh,
        in_specs=placed,
        out_specs=(
            P("lat", "lon", None),
            P("lat", "lon", None),
            P("lat", "lon"),
            P("lat", "lon"),
            P("lat", "lon"),
            P("lat", "lon"),
            P(),
            P(),
            P(),
        ),
        check_vma=False,
    )
```

```python
import functools
import math

import jax
import jax.numpy as jnp
from jax import lax
from jax.experimental import pallas as pl
from jax.experimental.pallas import tpu as pltpu
from jax.sharding import PartitionSpec as P

EPSILON = 1e-06
CELLS = 96
MESH = pl.DeviceIdType.MESH
VMEM_MIB = 54


CHUNK = 256


def silu_parts(values):
    sigmoid = 1.0 / (1.0 + jnp.exp(-values))
    return values * sigmoid, sigmoid * (1.0 + values * (1.0 - sigmoid))


def halo_copies(rows, edges, row_slots, edge_slots, sends, recvs):
    lat, lon = lax.axis_index("lat"), lax.axis_index("lon")
    bands, sectors = lax.axis_size("lat"), lax.axis_size("lon")
    west, east = (lon + sectors - 1) % sectors, (lon + 1) % sectors

    def made(source, target, index, peer):
        return pltpu.make_async_remote_copy(
            src_ref=source,
            dst_ref=target,
            send_sem=sends.at[index],
            recv_sem=recvs.at[index],
            device_id=peer,
            device_id_type=MESH,
        )

    north, south = lat > 0, lat < bands - 1
    copies = [
        (north, south, made(rows.at[0], row_slots.at[1], 0, (lat - 1, lon))),
        (south, north, made(rows.at[1], row_slots.at[0], 1, (lat + 1, lon))),
    ]
    for side, column in ((0, west), (1, east)):
        for slot in range(3):
            step = 1 - slot
            sends_it = (None, south, north)[step]
            gets_it = (None, north, south)[step]
            copies.append(
                (
                    sends_it,
                    gets_it,
                    made(
                        edges.at[side],
                        edge_slots.at[side, slot],
                        2 + side * 3 + slot,
                        (lat + step, column),
                    ),
                )
            )
    return copies


def guarded(condition, action):
    if condition is None:
        action()
    else:
        pl.when(condition)(action)


def halo_start(copies):
    for sends_it, _, made in copies:
        guarded(sends_it, made.start)


def halo_arrive(copies):
    for _, gets_it, made in copies:
        guarded(gets_it, made.wait_recv)


def halo_leave(copies):
    for sends_it, _, made in copies:
        guarded(sends_it, made.wait_send)


def halo_greet(barrier):
    lat, lon = lax.axis_index("lat"), lax.axis_index("lon")
    bands, sectors = lax.axis_size("lat"), lax.axis_size("lon")
    west, east = (lon + sectors - 1) % sectors, (lon + 1) % sectors

    def signal(row, column):
        pl.semaphore_signal(barrier, inc=1, device_id=(row, column), device_id_type=MESH)

    signal(lat, west)
    signal(lat, east)

    @pl.when(lat > 0)
    def _():
        for column in (west, lon, east):
            signal(lat - 1, column)

    @pl.when(lat < bands - 1)
    def _():
        for column in (west, lon, east):
            signal(lat + 1, column)

    north, south = (lat + bands - 1) // bands, (2 * bands - 2 - lat) // bands
    return 2 + 3 * north + 3 * south


def edge_pair(top, bottom, last):
    sub = lax.broadcasted_iota(jnp.int32, (8, top.shape[1]), 0)
    west = jnp.where(sub == 0, top[0:1], bottom[0:1])
    east = jnp.where(sub == 0, top[last : last + 1], bottom[last : last + 1])
    return west, east


def halo_row(index, base, edge_slots, valid, lanes=slice(None)):
    slot, row = ((0, 1), (1, 0), (1, 1), (2, 0))[index]
    place = lax.broadcasted_iota(jnp.int32, base.shape, 0)
    east = edge_slots[0, slot, row : row + 1, lanes]
    west = edge_slots[1, slot, row : row + 1, lanes]
    value = jnp.where(place == valid, east, jnp.where(place == CELLS - 1, west, base))
    lat, bands = lax.axis_index("lat"), lax.axis_size("lat")
    if index == 0:
        value = jnp.where(lat > 0, value, 0.0)
    if index == 3:
        value = jnp.where(lat < bands - 1, value, 0.0)
    return value


def inside(shape, valid):
    return lax.broadcasted_iota(jnp.int32, shape, 0) < valid


def inverse_rms(values):
    return lax.rsqrt(jnp.mean(values * values, axis=-1, keepdims=True) + EPSILON)


def nt_dot(left, right):
    return lax.dot_general(
        left, right, (((1,), (1,)), ((), ())), preferred_element_type=jnp.float32
    )


class Refs:
    def __init__(self, names, refs):
        for name, ref in zip(names, refs, strict=True):
            setattr(self, name, ref)


def exchange(source, target, sends, recvs, index, peer, landing=None):
    return pltpu.make_async_remote_copy(
        src_ref=source,
        dst_ref=target,
        send_sem=sends.at[index],
        recv_sem=recvs.at[index if landing is None else landing],
        device_id=peer,
        device_id_type=MESH,
    )


class Ring:
    def __init__(self):
        lon = lax.axis_index("lon")
        z, low = lax.div(lon, 4), lax.rem(lon, 4)
        x_lo, core = lax.div(low, 2), lax.rem(low, 2)
        self.column, self.x_lo, self.core = lon, x_lo, core
        self.starts = [lax.rem(z + d, 8) * 4 for d in range(8)]
        self.sides = [self.side(low_x, low_c) for low_x in range(2) for low_c in range(2)]

    def side(self, flip_x, flip_core):
        x_lo = self.x_lo + flip_x * (1 - 2 * self.x_lo)
        core = self.core + flip_core * (1 - 2 * self.core)
        return x_lo * 2 + core

    def start(self, ring, sign):
        half = (ring + 1) // 2
        return self.starts[(sign * (4 + (half if ring % 2 == 0 else -half))) % 8]

    def partner(self, k, sign):
        return self.start(k // 4, sign) + self.sides[3 - k % 4]


def packed(cells):
    return (cells[:48] + pltpu.roll(cells[48:], 64, 1)).astype(jnp.bfloat16)


def unpacked(pair):
    lane = lax.broadcasted_iota(jnp.int32, (48, 128), 1)
    pair = pair.astype(jnp.float32)
    top = jnp.where(lane < 64, pair, 0.0)
    bottom = jnp.where(lane < 64, pltpu.roll(pair, 64, 1), 0.0)
    return jnp.concatenate([top, bottom], axis=0)


def forward_phase(r, load, valid, greetings):
    f32, bf16 = jnp.float32, jnp.bfloat16
    r.rows[...] = jnp.zeros(r.rows.shape, bf16)
    r.cot_pad[...] = jnp.zeros(r.cot_pad.shape, bf16)
    load["state"].wait()
    for i in range(2):
        r.rows[i, 0:valid, :] = r.state[:, i, :]
    west, east = edge_pair(r.rows[0].astype(f32), r.rows[1].astype(f32), valid - 1)
    r.edges[0] = west
    r.edges[1] = east
    load["cot"].wait()
    load["out"].wait()
    for i in range(2):
        r.cot_pad[i * CELLS : i * CELLS + valid, :] = r.cot[:, i, :]
    r.projected[:, 1536:2048] = nt_dot(r.cot_pad[...], r.weight_out[...]).astype(bf16)
    pl.semaphore_wait(pltpu.get_barrier_semaphore(), greetings)
    copies = halo_copies(r.rows, r.edges, r.row_slots, r.edge_slots, r.state_sends, r.state_recvs)
    halo_start(copies)
    r.total[...] = jnp.zeros(r.total.shape, f32)
    r.bias_cells[...] = jnp.zeros(r.bias_cells.shape, f32)
    bias_lane = lax.broadcasted_iota(jnp.int32, (16, 128), 1)
    for i in range(2):
        r.bias_cells[i, :, 0:valid] = r.bias[i].astype(f32)
        heads = r.bias_cells[i]
        r.bias_low[i * 16 : i * 16 + 16, :] = jnp.where(bias_lane < 48, heads, 0.0)
        r.bias_high[i * 16 : i * 16 + 16, :] = jnp.where(bias_lane < 48, pltpu.roll(heads, 80, 1), 0.0)
    for a in range(3):
        r.depth[a * 3 : a * 3 + 3, :] = r.depth_low[a].astype(f32)
    load["expand"].wait()
    load["shrink"].wait()
    halo_arrive(copies)
    for row in range(4):
        base = r.rows[row - 1] if row in (1, 2) else r.row_slots[row // 3]
        value = halo_row(row, base.astype(f32), r.edge_slots, valid)
        value = (value * inverse_rms(value) * r.first_gain[...]).astype(bf16)
        r.wide_normed[row * CELLS : row * CELLS + CELLS, :] = value
        if row in (1, 2):
            own = jnp.where(inside(value.shape, valid), value.astype(f32), 0.0).astype(bf16)
            r.normed[(row - 1) * CELLS : row * CELLS, :] = own

    def chunk(index, carry):
        start = pl.multiple_of(index * CHUNK, CHUNK)
        lanes = pl.ds(start, CHUNK)
        expanded = jnp.dot(r.wide_normed[...], r.expand[:, lanes], preferred_element_type=f32)
        activated, slope = silu_parts(expanded)
        activated = activated.astype(bf16)
        r.slope_expanded[:, lanes] = slope[CELLS : 3 * CELLS].astype(bf16)
        planes = []
        for row in range(4):
            plane = activated[row * CELLS : row * CELLS + CELLS]
            r.act[row, :, lanes] = plane
            planes.append(plane.astype(f32))
        mixes, slopes = [], []
        for i in range(2):
            sums = []
            for b in range(3):
                part = r.depth[b : b + 1, lanes] * planes[i]
                for a in (1, 2):
                    part = part + r.depth[a * 3 + b : a * 3 + b + 1, lanes] * planes[i + a]
                sums.append(part)
            convolved = pltpu.roll(sums[0], 1, 0) + sums[1] + pltpu.roll(sums[2], CELLS - 1, 0)
            mixed, slope = silu_parts(convolved)
            keep = inside(mixed.shape, valid)
            mixes.append(jnp.where(keep, mixed, 0.0).astype(bf16))
            slope = jnp.where(keep, slope, 0.0)
            r.slope[i, :, lanes] = slope.astype(bf16)
            slopes.append(slope)
        west, east = edge_pair(slopes[0], slopes[1], valid - 1)
        r.slope_edges[0, :, lanes] = west
        r.slope_edges[1, :, lanes] = east
        mixed = jnp.concatenate(mixes, axis=0)
        r.mixed[:, lanes] = mixed
        r.total[...] += jnp.dot(
            mixed, r.shrink[pl.ds(start, CHUNK), :], preferred_element_type=f32
        )
        return carry

    lax.fori_loop(0, r.expand.shape[1] // CHUNK, chunk, 0)
    for i in range(2):
        part = slice(i * CELLS, i * CELLS + CELLS)
        inner = (r.rows[i].astype(f32) + r.total[part, :]).astype(bf16)
        r.inner[part, :] = inner
        inner = inner.astype(f32)
        r.second[part, :] = (inner * inverse_rms(inner) * r.second_gain[...]).astype(bf16)
    load["in"].wait()
    return copies


def project_and_pack(r, valid, first, last, target, with_bias):
    f32, bf16 = jnp.float32, jnp.bfloat16
    lane = lax.broadcasted_iota(jnp.int32, (CELLS, 128), 1)
    row = lax.broadcasted_iota(jnp.int32, (CELLS, 128), 0)
    for i in range(2):
        cells = slice(i * CELLS, i * CELLS + CELLS)
        for tile in range(4):
            parts = [
                r.projected[cells, base + tile * 128 : base + tile * 128 + 128].astype(f32)
                for base in (first, last)
            ]
            for u in range(4):
                item = i * 16 + tile * 4 + u
                moved = [
                    value if side == u else pltpu.roll(value, ((side - u) * 32) % 128, 1)
                    for side, value in enumerate(parts)
                ]
                value = jnp.where(lane < 32, moved[0], jnp.where(lane < 64, moved[1], 0.0))
                if with_bias:
                    value = jnp.where(row == valid, r.bias_low[item : item + 1, :], value)
                    value = jnp.where(row == valid + 1, r.bias_high[item : item + 1, :], value)
                target[item] = packed(value)


def attention_phase(r, valid, scale):
    sources = r.kv_in.shape[0]
    total = sources * CELLS
    block = r.scores.shape[1]
    group = block // CELLS
    log2e = 1.4426950408889634
    to_log2 = scale * log2e
    f32, bf16 = jnp.float32, jnp.bfloat16
    lat, lon = lax.axis_index("lat"), lax.axis_index("lon")
    groups = sources // group
    ring, own_group = r.ring, lax.div(lon, group)

    def key_copy(k, to, slot):
        return exchange(
            r.kv_out.at[to], r.kv_in.at[slot], r.kv_sends, r.kv_recvs, k, (lat, to)
        )

    def query_copy(to, slot):
        return exchange(
            r.qd_out.at[to], r.qd_in.at[slot], r.qd_sends, r.qd_recvs, to, (lat, to), slot
        )

    def near_copy(to, slot):
        return exchange(
            r.near_out.at[to], r.near_in.at[slot], r.near_sends, r.near_recvs, to, (lat, to), slot
        )

    def last_copy(k, to, slot):
        return exchange(
            r.last_out.at[to], r.last_in.at[slot], r.last_sends, r.last_recvs, k, (lat, to)
        )

    r.projected[:, 512:1536] = jnp.dot(
        r.second[...], r.weight_in[:, 512:1536], preferred_element_type=f32
    ).astype(bf16)
    project_and_pack(r, valid, 512, 1024, r.kv_out, True)

    for k in range(sources - 1):
        key_copy(k, ring.partner(k, 1), lon).start()
    r.projected[:, 0:512] = jnp.dot(
        r.second[...], r.weight_in[:, 0:512], preferred_element_type=f32
    ).astype(bf16)
    project_and_pack(r, valid, 0, 1536, r.qd_out, False)

    for step in range(groups):
        target = lax.rem(own_group + groups - step, groups) * group
        for part in range(group):
            to = target + part
            if step:
                query_copy(to, lon).start()
            else:

                @pl.when(to != lon)
                def _():
                    query_copy(to, lon).start()

    halo = halo_copies(
        r.slope, r.slope_edges, r.slope_rows, r.slope_sides, r.slope_sends, r.slope_recvs
    )
    halo_start(halo)
    r.kv_in[lon] = r.kv_out[lon]
    r.qd_in[lon] = r.qd_out[lon]

    def prepare(index):
        raw = unpacked(r.kv_in[index])
        row = lax.broadcasted_iota(jnp.int32, (CELLS, 128), 0)
        lane = lax.broadcasted_iota(jnp.int32, (CELLS, 128), 1)
        bias_row = jnp.where(row < 48, raw[valid : valid + 1, :], raw[valid + 1 : valid + 2, :])
        wanted = jnp.where(row < 48, row, row - 48)
        bias = jnp.sum(jnp.where(wanted == lane, bias_row, 0.0), axis=1, keepdims=True) * log2e
        bias = jnp.broadcast_to(bias, (CELLS, 128))
        first = bias.astype(bf16).astype(f32)
        second = (bias - first).astype(bf16).astype(f32)
        third = bias - first - second
        first = jnp.where(row < valid, first, -1e30)
        second = jnp.where(row < valid, second, 0.0)
        third = jnp.where(row < valid, third, 0.0)
        cell = jnp.where(row < valid, raw, 0.0)
        key = jnp.where(lane < 32, cell, 0.0)
        value = jnp.where(lane >= 32, cell, 0.0)
        keys = key + pltpu.roll(key, 32, 1) + pltpu.roll(key, 64, 1)
        keys = jnp.where(lane == 96, first, keys)
        keys = jnp.where(lane == 97, second, keys)
        keys = jnp.where(lane == 98, third, keys)
        values = value + pltpu.roll(value, 96, 1)
        values = jnp.where((lane >= 64) & (lane < 67), 1.0, values)
        start = pl.multiple_of(index * CELLS, 32)
        r.kaug[pl.ds(start, CELLS), :] = keys.astype(bf16)
        r.vaug[pl.ds(start, CELLS), :] = values.astype(bf16)
        r.cell[pl.ds(start, CELLS), :] = cell

    prepare(lon)

    for part in range(8):
        first = ring.start(part, -1)

        def arrive(step, carry):
            flip_x = (step < 2).astype(jnp.int32)
            flip_core = 3 - step - 2 * flip_x
            source = first + ring.side(flip_x, flip_core)
            key_copy(part * 4 + step, source, source).wait_recv()
            prepare(source)
            return carry

        lax.fori_loop(0, 4 if part < 7 else 3, arrive, 0)

    def turn(index, carry):
        start = pl.multiple_of(index * block, block)
        r.xt[:, pl.ds(start, block)] = r.cell[pl.ds(start, block), :].T[0:64].astype(bf16)
        r.acc[:, pl.ds(start, block)] = jnp.zeros((64, block), f32)
        return carry

    lax.fori_loop(0, total // block, turn, 0)

    def one_block(turn_index, carry):
        index = lax.rem(turn_index + own_group, groups)
        for part in range(group):
            source = index * group + part

            @pl.when(source != lon)
            def _():
                query_copy(source, source).wait_recv()

            r.qd_cell[part * CELLS : part * CELLS + CELLS, :] = unpacked(r.qd_in[source])
        xt = r.qd_cell[...].T
        query = xt[0:32] * to_log2
        first = query.astype(bf16).astype(f32)
        second = (query - first).astype(bf16).astype(f32)
        third = query - first - second
        qaug = jnp.concatenate(
            [first, second, third, jnp.ones((32, block), f32)], axis=0
        ).astype(bf16)
        t = jnp.dot(r.kaug[...], qaug, preferred_element_type=f32)
        r.scores[...] = t
        highest = jnp.max(jnp.max(t.reshape(total // 8, 8, block), axis=0), axis=0, keepdims=True)
        p = jnp.exp2(r.scores[...] - highest)
        r.scores[...] = p
        low_p = p.astype(bf16)
        r.low[...] = low_p
        norm = jnp.sum(p.reshape(total // 8, 8, block), axis=0)
        heads = jnp.dot(r.xt[32:64, :], low_p, preferred_element_type=f32)
        inverse = 1.0 / jnp.sum(norm, axis=0, keepdims=True)
        heads = heads * inverse
        back = xt[32:64]
        centred = jnp.sum(back * heads, axis=0, keepdims=True) * inverse
        back = back * inverse
        back_first = back.astype(bf16).astype(f32)
        back_second = back - back_first
        cen_first = centred.astype(bf16).astype(f32)
        cen_second = (centred - cen_first).astype(bf16).astype(f32)
        cen_third = centred - cen_first - cen_second
        sub = lax.broadcasted_iota(jnp.int32, (64, block), 0)
        cen = jnp.where(
            sub == 0,
            cen_first,
            jnp.where(sub == 1, cen_second, jnp.where(sub == 2, cen_third, 0.0)),
        )
        baug = jnp.concatenate([back_first, back_second, -cen], axis=0).astype(bf16)
        dp = jnp.dot(r.vaug[...], baug, preferred_element_type=f32)
        ds = (r.scores[...] * dp).astype(bf16)
        r.acc[32:64, :] += nt_dot(back_first.astype(bf16), r.low[...])
        r.acc[0:32, :] += nt_dot(xt[0:32].astype(bf16), ds)
        back_queries = jnp.dot(r.xt[0:32, :], ds, preferred_element_type=f32)
        zeros = jnp.zeros((64, block), f32)
        done = jnp.concatenate([back_queries * scale, heads, zeros], axis=0).T
        for part in range(group):
            source = index * group + part
            r.near_out[source] = packed(done[part * CELLS : part * CELLS + CELLS])

            @pl.when(source != lon)
            def _():
                near_copy(source, lon).start()

        return carry

    lax.fori_loop(0, groups, one_block, 0)
    r.near_in[lon] = r.near_out[lon]

    def finish(index, carry):
        start = pl.multiple_of(index * block, block)
        both = r.acc[:, pl.ds(start, block)]
        zeros = jnp.zeros((64, block), f32)
        both = jnp.concatenate([both[0:32] * scale, both[32:64], zeros], axis=0)
        r.cell[pl.ds(start, block), :] = both.T
        return carry

    lax.fori_loop(0, total // block, finish, 0)

    def pack_last(source):
        start = pl.multiple_of(source * CELLS, 32)
        r.last_out[source] = packed(r.cell[pl.ds(start, CELLS), :])

    for k in range(sources - 1):
        to = ring.partner(k, 1)
        pack_last(to)
        last_copy(k, to, lon).start()
    pack_last(lon)
    r.last_in[lon] = r.last_out[lon]

    def near_arrive():
        for k in range(sources - 1):
            source = ring.partner(k, -1)
            near_copy(source, source).wait_recv()

    def last_arrive():
        for k in range(sources - 1):
            source = ring.partner(k, -1)
            last_copy(k, source, source).wait_recv()

    def settle():
        for k in range(sources - 1):
            to = ring.partner(k, 1)
            key_copy(k, to, lon).wait_send()
            query_copy(to, lon).wait_send()
            near_copy(to, lon).wait_send()
            last_copy(k, to, lon).wait_send()

    return halo, near_arrive, last_arrive, settle


def gather_heads(source, first, second, i, tile):
    half_lane = lax.broadcasted_iota(jnp.int32, (48, 128), 1)
    parts = [source[i * 16 + tile * 4 + u].astype(jnp.float32) for u in range(4)]
    for (target, column), lane in ((first, 0), (second, 32)):
        for half in range(2):
            value = None
            for u in range(4):
                shift = (u * 32 - lane - half * 64) % 128
                moved = pltpu.roll(parts[u], shift, 1) if shift else parts[u]
                value = moved if value is None else jnp.where(half_lane < u * 32, value, moved)
            start, column_start = i * CELLS + half * 48, column + tile * 128
            target[start : start + 48, column_start : column_start + 128] = value.astype(
                jnp.bfloat16
            )


def backward_phase(r, valid, factor, slope_halo, near_arrive, last_arrive, peers):
    f32, bf16 = jnp.float32, jnp.bfloat16
    sibling, x_peers, y_peers, z_peers = peers
    lat, lon = lax.axis_index("lat"), lax.axis_index("lon")
    y = lax.rem(lat, 4)
    z, x_lo, core = lax.div(lon, 4), r.ring.x_lo, r.ring.core
    x = lax.div(lat, 4) * 2 + x_lo
    other = 1 - core
    xs, ys = [lax.rem(x + d, 4) for d in range(4)], [lax.rem(y + d, 4) for d in range(4)]
    zs = [lax.rem(z + d, 8) for d in range(8)]
    r.small[...] = jnp.zeros(r.small.shape, f32)
    near_arrive()
    for i in range(2):
        for tile in range(4):
            gather_heads(r.near_in, (r.back_project, 0), (r.heads, 0), i, tile)
    field = jnp.dot(r.heads[...], r.weight_out[...], preferred_element_type=f32)
    for i in range(2):
        part = slice(i * CELLS, i * CELLS + CELLS)
        r.field[i] = (r.inner[part, :].astype(f32) + field[part]).astype(bf16)[0:valid]
    back_second = nt_dot(r.back_project[:, 0:512], r.weight_in[:, 0:512])
    last_arrive()
    for i in range(2):
        for tile in range(4):
            gather_heads(r.last_in, (r.back_project, 512), (r.back_project, 1024), i, tile)
    back_second = back_second + nt_dot(r.back_project[:, 512:1536], r.weight_in[:, 512:1536])
    gain_two = jnp.zeros((1, field.shape[1]), f32)
    for i in range(2):
        part = slice(i * CELLS, i * CELLS + CELLS)
        inner = r.inner[part, :].astype(f32)
        inverse = inverse_rms(inner)
        gain_two = gain_two + jnp.sum(back_second[part] * inner * inverse, axis=0, keepdims=True)
        scaled = back_second[part] * r.second_gain[...]
        back = (
            r.cot_pad[part, :].astype(f32)
            + inverse * scaled
            - inverse * inverse * inverse * inner * jnp.mean(scaled * inner, axis=-1, keepdims=True)
        )
        r.back_rows[i] = back.astype(bf16)
    west, east = edge_pair(r.back_rows[0].astype(f32), r.back_rows[1].astype(f32), valid - 1)
    r.back_edges[0] = west
    r.back_edges[1] = east
    halo = halo_copies(
        r.back_rows, r.back_edges, r.back_slots, r.back_sides, r.back_sends, r.back_recvs
    )
    halo_start(halo)

    def half_lanes(top, bottom):
        lane = lax.broadcasted_iota(jnp.int32, top.shape, 1)
        even = jnp.where(lane < 64, top, pltpu.roll(bottom, 64, 1))
        odd = jnp.where(lane < 64, pltpu.roll(top, 64, 1), bottom)
        return even, odd

    def cross(left, right):
        return (
            lax.dot_general(left, right, (((0,), (0,)), ((), ())), preferred_element_type=f32)
            * factor
        )

    def core_copy(mine, theirs, first, width, index):
        rows = pl.ds(first, width)
        return exchange(
            mine.at[other, rows], theirs.at[rows], r.core_sends, r.core_recvs, index, sibling
        )

    def early_x(zz):
        return core_copy(r.ex, r.ex0, zz * 2, 2, zz)

    def early_y(zz):
        return core_copy(r.ey, r.ey0, zz * 2, 2, 4 + zz)

    def late_x(pz):
        return core_copy(r.lx, r.lx0, pz, 1, 8 + pz)

    def late_y(pz):
        return core_copy(r.ly, r.ly0, pz, 1, 16 + pz)

    def early_part(zz, carry):
        columns = pl.ds(pl.multiple_of(zz * 128, 128), 128)
        own = jnp.concatenate([r.back_rows[0, :, columns], r.back_rows[1, :, columns]], axis=0)
        shrink = cross(own, r.mixed[...])
        grad_in = cross(
            r.back_project[:, pl.ds(pl.multiple_of(zz * 384, 128), 384)], r.second[...]
        )
        grad_out = cross(r.cot_pad[:, columns], r.heads[...])
        for sub in range(8):
            pz, plo, pc = zz * 2 + sub // 4, (sub // 2) % 2, sub % 2
            for plat in range(8):
                px, py = (plat // 4) * 2 + plo, plat % 4
                part = slice(sub * 16, sub * 16 + 16)
                for side in range(2):
                    column = plat * 256 + side * 128
                    r.ex[pc, pz, px, py, side * 16 : side * 16 + 16, :] = shrink[
                        part, column : column + 128
                    ].astype(bf16)
            for pair in range(4):
                tile = slice(pair * 128, pair * 128 + 128)
                top = jnp.concatenate(
                    [grad_in[sub * 48 : sub * 48 + 24, tile], grad_out[sub * 16 : sub * 16 + 8, tile]],
                    axis=0,
                )
                bottom = jnp.concatenate(
                    [
                        grad_in[sub * 48 + 24 : sub * 48 + 48, tile],
                        grad_out[sub * 16 + 8 : sub * 16 + 16, tile],
                    ],
                    axis=0,
                )
                parts = half_lanes(top, bottom)
                for odd in range(2):
                    plat = pair * 2 + odd
                    px, py = (plat // 4) * 2 + plo, plat % 4
                    r.ey[pc, pz, py, px] = parts[odd].astype(bf16)
        early_x(zz).start()
        early_y(zz).start()
        return carry

    lax.fori_loop(0, 4, early_part, 0)

    def add_pair(mine, theirs, pz):
        for q in range(4):
            mine[core, pz, q] = (mine[core, pz, q].astype(f32) + theirs[pz, q].astype(f32)).astype(bf16)

    def early_arrive(zz, carry):
        early_x(zz).wait_recv()
        early_y(zz).wait_recv()
        for step in range(2):
            add_pair(r.ex, r.ex0, zz * 2 + step)
            add_pair(r.ey, r.ey0, zz * 2 + step)
        return carry

    lax.fori_loop(0, 4, early_arrive, 0)
    count = [0]

    def copy(source, target, peer):
        index = count[0]
        count[0] += 1
        made = exchange(source, target, r.sends, r.recvs, index, peer)
        made.start()
        return made

    def stage_one(mine, slots, targets, turns):
        return [
            copy(mine.at[core, :, turns[d]], slots.at[d - 1], targets[d - 1])
            for d in (1, 2, 3)
        ]

    early_one_x = stage_one(r.ex, r.ex1, x_peers, xs)
    early_one_y = stage_one(r.ey, r.ey1, y_peers, ys)
    halo_arrive(slope_halo)
    halo_arrive(halo)
    for row in range(4):
        base = r.back_rows[row - 1] if row in (1, 2) else r.back_slots[row // 3]
        value = halo_row(row, base.astype(f32), r.back_sides, valid)
        r.wide_back[row * CELLS : row * CELLS + CELLS, :] = value.astype(bf16)
    r.back_normed[...] = jnp.zeros(r.back_normed.shape, f32)

    def chunk(pz, carry):
        start = pl.multiple_of(pz * CHUNK, CHUNK)
        lanes = pl.ds(start, CHUNK)
        product = nt_dot(r.wide_back[...], r.shrink[lanes, :])
        planes = []
        for row in range(4):
            base = r.slope[row - 1, :, lanes] if row in (1, 2) else r.slope_rows[row // 3, :, lanes]
            slope = halo_row(row, base.astype(f32), r.slope_sides, valid, lanes)
            plane = product[row * CELLS : row * CELLS + CELLS] * slope
            planes.append(plane.astype(bf16).astype(f32))
        for b in range(3):
            turned = []
            for i in range(2):
                centre = planes[i + 1]
                centre = jnp.where(inside(centre.shape, valid), centre, 0.0)
                turned.append(pltpu.roll(centre, (CELLS + b - 1) % CELLS, 0) if b != 1 else centre)
            for a in range(3):
                value = r.act[a, :, lanes].astype(f32) * turned[0]
                value = value + r.act[a + 1, :, lanes].astype(f32) * turned[1]
                r.small[a * 3 + b : a * 3 + b + 1, lanes] = (
                    jnp.sum(value, axis=0, keepdims=True) * factor
                )
        outs = []
        for i in range(2):
            sums = []
            for b in range(3):
                part = r.depth[b : b + 1, lanes] * planes[i + 2]
                for a in (1, 2):
                    part = part + r.depth[a * 3 + b : a * 3 + b + 1, lanes] * planes[i + 2 - a]
                sums.append(part)
            total = pltpu.roll(sums[0], CELLS - 1, 0) + sums[1] + pltpu.roll(sums[2], 1, 0)
            total = total * r.slope_expanded[i * CELLS : i * CELLS + CELLS, lanes].astype(f32)
            outs.append(jnp.where(inside(total.shape, valid), total, 0.0).astype(bf16))
        back = jnp.concatenate(outs, axis=0)
        r.back_normed[...] += nt_dot(back, r.expand[:, lanes])
        grad = cross(back, r.normed[...])
        for sub in range(4):
            plo, pc = sub // 2, sub % 2
            for pair in range(4):
                tile = slice(pair * 128, pair * 128 + 128)
                parts = half_lanes(
                    grad[sub * 64 : sub * 64 + 32, tile], grad[sub * 64 + 32 : sub * 64 + 64, tile]
                )
                for odd in range(2):
                    plat = pair * 2 + odd
                    px, py = (plat // 4) * 2 + plo, plat % 4
                    r.lx[pc, pz, px, py] = parts[odd][0:16].astype(bf16)
                    r.ly[pc, pz, py, px] = parts[odd][16:32].astype(bf16)
        late_x(pz).start()
        late_y(pz).start()
        return carry

    lax.fori_loop(0, 8, chunk, 0)
    gain_one = jnp.zeros((1, r.back_normed.shape[1]), f32)
    for i in range(2):
        part = slice(i * CELLS, i * CELLS + valid)
        state = r.rows[i, 0:valid, :].astype(f32)
        inverse = inverse_rms(state)
        back = r.back_normed[part, :]
        gain_one = gain_one + jnp.sum(back * state * inverse, axis=0, keepdims=True)
        scaled = back * r.first_gain[...]
        r.grad[i] = (
            r.back_rows[i, 0:valid, :].astype(f32)
            + inverse * scaled
            - inverse * inverse * inverse * state * jnp.mean(scaled * state, axis=-1, keepdims=True)
        ).astype(bf16)
    width = r.small.shape[1]
    r.small[9:10, :] = jnp.concatenate(
        [gain_one * factor, gain_two * factor, jnp.zeros((1, width - 1024), f32)], axis=1
    )
    for tile in range(16):
        for part in range(2):
            r.small_split[tile * 2 + part] = r.small[
                part * 8 : part * 8 + 8, tile * 128 : tile * 128 + 128
            ]
    sectors, bands = r.small_lon.shape[0], r.small_lat.shape[0]
    columns = [(r.ring.partner(k, 1), r.ring.partner(k, -1)) for k in range(sectors - 1)]

    def scatter(k, to, slot):
        return exchange(
            r.small_split.at[to], r.small_lon.at[slot], r.small_sends, r.small_recvs, k, (lat, to)
        )

    def spread(k, to, slot):
        return exchange(
            r.sums.at[lon], r.sums.at[slot], r.spread_sends, r.spread_recvs, k, (lat, to)
        )

    for k, (to, _) in enumerate(columns):
        scatter(k, to, lon).start()
    r.small_lon[lon] = r.small_split[lon]

    def late_arrive(pz, carry):
        late_x(pz).wait_recv()
        late_y(pz).wait_recv()
        add_pair(r.lx, r.lx0, pz)
        add_pair(r.ly, r.ly0, pz)
        return carry

    lax.fori_loop(0, 8, late_arrive, 0)
    late_one_x = stage_one(r.lx, r.lx1, x_peers, xs)
    late_one_y = stage_one(r.ly, r.ly1, y_peers, ys)

    def add_four(mine, theirs, here, total):
        def body(pz, carry):
            value = mine[core, pz, here].astype(f32)
            for d in range(3):
                value = value + theirs[d, pz].astype(f32)
            total[pz] = value.astype(bf16)
            return carry

        lax.fori_loop(0, 8, body, 0)

    def stage_two(arrivals, mine, slots, here, total, next_slots, targets, turns):
        for made in arrivals:
            made.wait_recv()
        add_four(mine, slots, here, total)
        return [
            copy(total.at[:, turns[d]], next_slots.at[d - 1], targets[d - 1])
            for d in (1, 2, 3)
        ]

    early_two_x = stage_two(early_one_x, r.ex, r.ex1, x, r.ext, r.ex2, y_peers, ys)
    early_two_y = stage_two(early_one_y, r.ey, r.ey1, y, r.eyt, r.ey2, x_peers, xs)

    def stage_three(arrivals, total, slots, here, first, count_rows):
        for made in arrivals:
            made.wait_recv()

        def body(pz, carry):
            value = total[pz, here].astype(f32)
            for d in range(3):
                value = value + slots[d, pz].astype(f32)
            r.final[pz, first : first + count_rows, :] = value.astype(bf16)
            return carry

        lax.fori_loop(0, 8, body, 0)

    def send_final(first, count_rows):
        rows = pl.ds(first, count_rows)
        return [
            copy(r.final.at[zs[d], rows], r.final_in.at[d - 1, rows], z_peers[d - 1])
            for d in range(1, 8)
        ]

    stage_three(early_two_x, r.ext, r.ex2, y, 0, 32)
    stage_three(early_two_y, r.eyt, r.ey2, x, 32, 32)
    final_early = send_final(0, 64)
    late_two_x = stage_two(late_one_x, r.lx, r.lx1, x, r.lxt, r.lx2, y_peers, ys)
    late_two_y = stage_two(late_one_y, r.ly, r.ly1, y, r.lyt, r.ly2, x_peers, xs)

    for k, (_, source) in enumerate(columns):
        scatter(k, source, source).wait_recv()
    total = r.small_lon[0]
    for index in range(1, sectors):
        total = total + r.small_lon[index]
    r.small_lat[lat] = total
    small_lat = [
        copy(r.small_lat.at[lat], r.small_lat.at[lat], (lax.rem(lat + d, bands), lon))
        for d in range(1, bands)
    ]

    stage_three(late_two_x, r.lxt, r.lx2, y, 64, 16)
    stage_three(late_two_y, r.lyt, r.ly2, x, 80, 16)
    final_late = send_final(64, 32)

    for made in small_lat:
        made.wait_recv()
    total = r.small_lat[0]
    for index in range(1, bands):
        total = total + r.small_lat[index]
    r.sums[lon] = total
    for k, (to, _) in enumerate(columns):
        spread(k, to, lon).start()

    for made in final_early + final_late:
        made.wait_recv()
    value = r.final[z].astype(f32)
    for d in range(7):
        value = value + r.final_in[d].astype(f32)
    r.block[...] = value
    for k, (to, source) in enumerate(columns):
        spread(k, source, source).wait_recv()
        spread(k, to, lon).wait_send()
        scatter(k, to, lon).wait_send()
    for made in (
        early_one_x
        + early_one_y
        + late_one_x
        + late_one_y
        + early_two_x
        + early_two_y
        + late_two_x
        + late_two_y
        + final_early
        + final_late
        + small_lat
    ):
        made.wait_send()

    def settle(pz, carry):
        late_x(pz).wait_send()
        late_y(pz).wait_send()
        return carry

    def settle_early(zz, carry):
        early_x(zz).wait_send()
        early_y(zz).wait_send()
        return carry

    lax.fori_loop(0, 8, settle, 0)
    lax.fori_loop(0, 4, settle_early, 0)
    halo_leave(halo)


def step_kernel(names, valid, scale, factor, *refs):
    r = Refs(names, refs)
    lat, lon = lax.axis_index("lat"), lax.axis_index("lon")
    sectors = lax.axis_size("lon")
    y, z, core = lax.rem(lat, 4), lax.div(lon, 4), lax.rem(lon, 2)
    x = lax.div(lat, 4) * 2 + lax.rem(lax.div(lon, 2), 2)

    def place(px, py, pz, pc):
        return (lax.div(px, 2) * 4 + py, pz * 4 + lax.rem(px, 2) * 2 + pc)

    barrier = pltpu.get_barrier_semaphore()
    peers = (
        place(x, y, z, 1 - core),
        [place(lax.rem(x + d, 4), y, z, core) for d in range(1, 4)],
        [place(x, lax.rem(y + d, 4), z, core) for d in range(1, 4)],
        [place(x, y, lax.rem(z + d, 8), core) for d in range(1, 8)],
    )
    greetings = halo_greet(barrier)
    bands = lax.axis_size("lat")
    band_peers = [(lax.rem(lat + d, bands), lon) for d in range(1, bands)]
    for peer in peers[1] + peers[2] + band_peers:
        pl.semaphore_signal(barrier, inc=1, device_id=peer, device_id_type=MESH)

    r.ring = Ring()
    for k in range(sectors - 1):
        pl.semaphore_signal(
            barrier, inc=1, device_id=(lat, r.ring.partner(k, 1)), device_id_type=MESH
        )
    greetings = greetings + len(peers[1]) + len(peers[2]) + bands - 1 + sectors - 1
    load = {}
    for index, (name, source, target) in enumerate(
        (
            ("state", r.state_hbm, r.state),
            ("cot", r.cot_hbm, r.cot),
            ("out", r.out_hbm, r.weight_out),
            ("expand", r.expand_hbm, r.expand),
            ("shrink", r.shrink_hbm, r.shrink),
            ("in", r.in_hbm, r.weight_in),
        )
    ):
        load[name] = pltpu.make_async_copy(source, target, r.loads.at[index])
        load[name].start()
    state_halo = forward_phase(r, load, valid, greetings)
    slope_halo, near_arrive, last_arrive, settle = attention_phase(r, valid, scale)
    backward_phase(r, valid, factor, slope_halo, near_arrive, last_arrive, peers)
    settle()
    halo_leave(state_halo)
    halo_leave(slope_halo)


def whole_step(factor, scale, operands, bias, depth, first_gain, second_gain):
    f32, bf16 = jnp.float32, jnp.bfloat16
    state, cot, expand, shrink, weight_in, weight_out = operands
    valid = state.shape[0]
    channels, wide = expand.shape
    cells = 2 * CELLS
    sources = lax.axis_size("lon")
    total, block = sources * CELLS, 768
    vmem, dma = pltpu.VMEM, pltpu.SemaphoreType.DMA
    message = vmem((sources, 48, 128), bf16)

    def tree(name, rows):
        return {
            name: vmem((2, 8, 4, 4, rows, 128), bf16),
            name + "0": vmem((8, 4, 4, rows, 128), bf16),
            name + "1": vmem((3, 8, 4, rows, 128), bf16),
            name + "t": vmem((8, 4, rows, 128), bf16),
            name + "2": vmem((3, 8, rows, 128), bf16),
        }

    def halo_set(prefix, width):
        return {prefix + "sends": dma((8,)), prefix + "recvs": dma((8,))}

    scratch = {
        "state": vmem(state.shape, bf16),
        "cot": vmem(cot.shape, bf16),
        "expand": vmem(expand.shape, bf16),
        "shrink": vmem(shrink.shape, bf16),
        "weight_in": vmem(weight_in.shape, bf16),
        "weight_out": vmem(weight_out.shape, bf16),
        "bias_cells": vmem((2, 16, 128), f32),
        "bias_low": vmem((32, 128), f32),
        "bias_high": vmem((32, 128), f32),
        "depth": vmem((16, wide), f32),
        "rows": vmem((2, CELLS, channels), bf16),
        "edges": vmem((2, 8, channels), f32),
        "row_slots": vmem((2, CELLS, channels), bf16),
        "edge_slots": vmem((2, 3, 8, channels), f32),
        "back_rows": vmem((2, CELLS, channels), bf16),
        "back_edges": vmem((2, 8, channels), f32),
        "back_slots": vmem((2, CELLS, channels), bf16),
        "back_sides": vmem((2, 3, 8, channels), f32),
        "slope": vmem((2, CELLS, wide), bf16),
        "slope_edges": vmem((2, 8, wide), f32),
        "slope_rows": vmem((2, CELLS, wide), bf16),
        "slope_sides": vmem((2, 3, 8, wide), f32),
        "wide_normed": vmem((4 * CELLS, channels), bf16),
        "wide_back": vmem((4 * CELLS, channels), bf16),
        "total": vmem((cells, channels), f32),
        "back_normed": vmem((cells, channels), f32),
        "projected": vmem((cells, 4 * channels), bf16),
        "back_project": vmem((cells, 3 * channels), bf16),
        "heads": vmem((cells, channels), bf16),
        "cot_pad": vmem((cells, channels), bf16),
        "act": vmem((4, CELLS, wide), bf16),
        "slope_expanded": vmem((cells, wide), bf16),
        "mixed": vmem((cells, wide), bf16),
        "normed": vmem((cells, channels), bf16),
        "inner": vmem((cells, channels), bf16),
        "second": vmem((cells, channels), bf16),
        "kv_out": message,
        "kv_in": message,
        "qd_out": message,
        "qd_in": message,
        "near_out": message,
        "near_in": message,
        "last_out": message,
        "last_in": message,
        "xt": vmem((64, total), bf16),
        "kaug": vmem((total, 128), bf16),
        "vaug": vmem((total, 128), bf16),
        "scores": vmem((total, block), f32),
        "low": vmem((total, block), bf16),
        "acc": vmem((64, total), f32),
        "cell": vmem((total, 128), f32),
        "qd_cell": vmem((block, 128), f32),
        **tree("ex", 32),
        **tree("ey", 32),
        **tree("lx", 16),
        **tree("ly", 16),
        "final": vmem((8, 96, 128), bf16),
        "final_in": vmem((7, 96, 128), bf16),
        "small": vmem((16, wide), f32),
        "small_split": vmem((sources, 8, 128), f32),
        "small_lon": vmem((sources, 8, 128), f32),
        "small_lat": vmem((lax.axis_size("lat"), 8, 128), f32),
        "loads": dma((6,)),
        "core_sends": dma((24,)),
        "core_recvs": dma((24,)),
        "sends": dma((66,)),
        "recvs": dma((66,)),
    }
    for prefix in ("state_", "slope_", "back_"):
        scratch[prefix + "sends"] = dma((8,))
        scratch[prefix + "recvs"] = dma((8,))
    for prefix in ("kv_", "qd_", "near_", "last_", "small_", "spread_"):
        scratch[prefix + "sends"] = dma((sources,))
        scratch[prefix + "recvs"] = dma((sources,))
    inputs = [name + "_hbm" for name in ("state", "cot", "expand", "shrink", "in", "out")]
    inputs += ["bias", "depth_low", "first_gain", "second_gain"]
    outputs = {
        "field": ((2, valid, channels), bf16),
        "grad": ((2, valid, channels), bf16),
        "block": ((96, 128), f32),
        "sums": ((sources, 8, 128), f32),
    }
    names = inputs + list(outputs) + list(scratch)
    whole, anywhere = pl.BlockSpec(memory_space=vmem), pl.BlockSpec(memory_space=pl.ANY)
    return pl.pallas_call(
        functools.partial(step_kernel, names, valid, scale, factor),
        out_shape=tuple(jax.ShapeDtypeStruct(*kind) for kind in outputs.values()),
        in_specs=[anywhere] * 6 + [whole] * 4,
        out_specs=(whole,) * 4,
        scratch_shapes=list(scratch.values()),
        compiler_params=pltpu.CompilerParams(
            vmem_limit_bytes=VMEM_MIB * 1024 * 1024, collective_id=1, has_side_effects=True
        ),
        name="step",
    )(*operands, bias, depth, first_gain, second_gain)


def deliver_kernel(block_ref, sums_ref, expand_ref, shrink_ref, in_ref, out_ref, depth_ref, one_ref, two_ref):
    def unfold(part):
        return jnp.concatenate([part, pltpu.roll(part, 64, 1)], axis=0)

    block = block_ref[...]
    expand = unfold(block[64:96])
    expand = jnp.concatenate([expand, jnp.zeros_like(expand)], axis=0).T
    expand_ref[...] = expand[0:64, 0:64]
    shrink_ref[:, 0:128] = block[0:16]
    shrink_ref[:, 128:256] = block[16:32]
    in_ref[...] = unfold(block[32:56])[:, 0:64]
    out_ref[...] = unfold(block[56:64])[:, 0:64]
    for tile in range(16):
        lanes = slice(tile * 128, tile * 128 + 128)
        low, high = sums_ref[tile * 2], sums_ref[tile * 2 + 1]
        depth_ref[0, :, lanes] = low[0:3]
        depth_ref[1, :, lanes] = low[3:6]
        depth_ref[2, 0:2, lanes] = low[6:8]
        depth_ref[2, 2:3, lanes] = high[0:1]
        if tile < 4:
            one_ref[:, lanes] = high[1:2]
        elif tile < 8:
            two_ref[:, tile * 128 - 512 : tile * 128 - 384] = high[1:2]


def deliver(block, sums, channels, wide):
    vmem = pl.BlockSpec(memory_space=pltpu.VMEM)
    shapes = [(64, 64), (16, 256), (48, 64), (16, 64), (3, 3, wide), (1, channels), (1, channels)]
    expand, shrink, grad_in, grad_out, depth, one, two = pl.pallas_call(
        deliver_kernel,
        out_shape=tuple(jax.ShapeDtypeStruct(shape, jnp.float32) for shape in shapes),
        in_specs=[vmem] * 2,
        out_specs=(vmem,) * 7,
        name="deliver",
    )(block, sums)
    one, two = one.reshape(channels), two.reshape(channels)
    return expand, shrink.T, grad_in.T, grad_out.T, depth, one, two


def per_device(
    state_field,
    cotangent,
    key_bias,
    input_gain,
    expand_weight,
    depth_weight,
    shrink_weight,
    attention_gain,
    attention_in,
    attention_out,
):
    row_count, lon_count, channels = state_field.shape
    head_count = key_bias.shape[2]
    wide_count = expand_weight.shape[1]
    norm_factor = 1.0 / math.sqrt(
        row_count * lon_count * lax.axis_size("lat") * lax.axis_size("lon")
    )
    score_scale = 1.0 / math.sqrt(channels // head_count)
    output_field, input_grad, block, sums = whole_step(
        norm_factor,
        score_scale,
        (state_field.transpose(1, 0, 2), cotangent.transpose(1, 0, 2), expand_weight, shrink_weight, attention_in, attention_out),
        key_bias.transpose(0, 2, 1),
        depth_weight,
        input_gain.reshape(1, channels),
        attention_gain.reshape(1, channels),
    )
    return (output_field, input_grad, *deliver(block, sums, channels, wide_count))


def solution(mesh):
    placed = (
        P("lat", "lon", None),
        P("lat", "lon", None),
        P("lat", "lon", None),
        P(),
        P(),
        P(),
        P(),
        P(),
        P(),
        P(),
    )
    return jax.shard_map(
        per_device,
        mesh=mesh,
        in_specs=placed,
        out_specs=(
            P("lat", "lon", None),
            P("lat", "lon", None),
            P("lat", "lon"),
            P("lat", "lon"),
            P("lat", "lon"),
            P("lat", "lon"),
            P(),
            P(),
            P(),
        ),
        check_vma=False,
    )
```

```python
import functools
import math

import jax
import jax.numpy as jnp
from jax import lax
from jax.experimental import pallas as pl
from jax.experimental.pallas import tpu as pltpu
from jax.sharding import PartitionSpec as P

EPSILON = 1e-06
CELLS = 96
MESH = pl.DeviceIdType.MESH
VMEM_MIB = 54


CHUNK = 256


def silu_parts(values):
    sigmoid = 1.0 / (1.0 + jnp.exp(-values))
    return values * sigmoid, sigmoid * (1.0 + values * (1.0 - sigmoid))


def halo_copies(rows, edges, row_slots, edge_slots, sends, recvs):
    lat, lon = lax.axis_index("lat"), lax.axis_index("lon")
    bands, sectors = lax.axis_size("lat"), lax.axis_size("lon")
    west, east = (lon + sectors - 1) % sectors, (lon + 1) % sectors

    def made(source, target, index, peer):
        return pltpu.make_async_remote_copy(
            src_ref=source,
            dst_ref=target,
            send_sem=sends.at[index],
            recv_sem=recvs.at[index],
            device_id=peer,
            device_id_type=MESH,
        )

    north, south = lat > 0, lat < bands - 1
    copies = [
        (north, south, made(rows.at[0], row_slots.at[1], 0, (lat - 1, lon))),
        (south, north, made(rows.at[1], row_slots.at[0], 1, (lat + 1, lon))),
    ]
    for side, column in ((0, west), (1, east)):
        for slot in range(3):
            step = 1 - slot
            sends_it = (None, south, north)[step]
            gets_it = (None, north, south)[step]
            copies.append(
                (
                    sends_it,
                    gets_it,
                    made(
                        edges.at[side],
                        edge_slots.at[side, slot],
                        2 + side * 3 + slot,
                        (lat + step, column),
                    ),
                )
            )
    return copies


def guarded(condition, action):
    if condition is None:
        action()
    else:
        pl.when(condition)(action)


def halo_start(copies):
    for sends_it, _, made in copies:
        guarded(sends_it, made.start)


def halo_arrive(copies):
    for _, gets_it, made in copies:
        guarded(gets_it, made.wait_recv)


def halo_leave(copies):
    for sends_it, _, made in copies:
        guarded(sends_it, made.wait_send)


def halo_greet(barrier):
    lat, lon = lax.axis_index("lat"), lax.axis_index("lon")
    bands, sectors = lax.axis_size("lat"), lax.axis_size("lon")
    west, east = (lon + sectors - 1) % sectors, (lon + 1) % sectors

    def signal(row, column):
        pl.semaphore_signal(barrier, inc=1, device_id=(row, column), device_id_type=MESH)

    signal(lat, west)
    signal(lat, east)

    @pl.when(lat > 0)
    def _():
        for column in (west, lon, east):
            signal(lat - 1, column)

    @pl.when(lat < bands - 1)
    def _():
        for column in (west, lon, east):
            signal(lat + 1, column)

    north, south = (lat + bands - 1) // bands, (2 * bands - 2 - lat) // bands
    return 2 + 3 * north + 3 * south


def edge_pair(top, bottom, last):
    sub = lax.broadcasted_iota(jnp.int32, (8, top.shape[1]), 0)
    west = jnp.where(sub == 0, top[0:1], bottom[0:1])
    east = jnp.where(sub == 0, top[last : last + 1], bottom[last : last + 1])
    return west, east


def halo_row(index, base, edge_slots, valid, lanes=slice(None)):
    slot, row = ((0, 1), (1, 0), (1, 1), (2, 0))[index]
    place = lax.broadcasted_iota(jnp.int32, base.shape, 0)
    east = edge_slots[0, slot, row : row + 1, lanes]
    west = edge_slots[1, slot, row : row + 1, lanes]
    value = jnp.where(place == valid, east, jnp.where(place == CELLS - 1, west, base))
    lat, bands = lax.axis_index("lat"), lax.axis_size("lat")
    if index == 0:
        value = jnp.where(lat > 0, value, 0.0)
    if index == 3:
        value = jnp.where(lat < bands - 1, value, 0.0)
    return value


def inside(shape, valid):
    return lax.broadcasted_iota(jnp.int32, shape, 0) < valid


def inverse_rms(values):
    return lax.rsqrt(jnp.mean(values * values, axis=-1, keepdims=True) + EPSILON)


def nt_dot(left, right):
    return lax.dot_general(
        left, right, (((1,), (1,)), ((), ())), preferred_element_type=jnp.float32
    )


class Refs:
    def __init__(self, names, refs):
        for name, ref in zip(names, refs, strict=True):
            setattr(self, name, ref)


def exchange(source, target, sends, recvs, index, peer, landing=None):
    return pltpu.make_async_remote_copy(
        src_ref=source,
        dst_ref=target,
        send_sem=sends.at[index],
        recv_sem=recvs.at[index if landing is None else landing],
        device_id=peer,
        device_id_type=MESH,
    )


class Ring:
    def __init__(self):
        lon = lax.axis_index("lon")
        z, low = lax.div(lon, 4), lax.rem(lon, 4)
        x_lo, core = lax.div(low, 2), lax.rem(low, 2)
        self.column, self.x_lo, self.core = lon, x_lo, core
        self.starts = [lax.rem(z + d, 8) * 4 for d in range(8)]
        self.sides = [self.side(low_x, low_c) for low_x in range(2) for low_c in range(2)]

    def side(self, flip_x, flip_core):
        x_lo = self.x_lo + flip_x * (1 - 2 * self.x_lo)
        core = self.core + flip_core * (1 - 2 * self.core)
        return x_lo * 2 + core

    def start(self, ring, sign):
        half = (ring + 1) // 2
        return self.starts[(sign * (4 + (half if ring % 2 == 0 else -half))) % 8]

    def partner(self, k, sign):
        return self.start(k // 4, sign) + self.sides[3 - k % 4]


def packed(cells):
    return (cells[:48] + pltpu.roll(cells[48:], 64, 1)).astype(jnp.bfloat16)


def unpacked(pair):
    lane = lax.broadcasted_iota(jnp.int32, (48, 128), 1)
    pair = pair.astype(jnp.float32)
    top = jnp.where(lane < 64, pair, 0.0)
    bottom = jnp.where(lane < 64, pltpu.roll(pair, 64, 1), 0.0)
    return jnp.concatenate([top, bottom], axis=0)


def forward_phase(r, load, valid, greetings):
    f32, bf16 = jnp.float32, jnp.bfloat16
    r.rows[...] = jnp.zeros(r.rows.shape, bf16)
    r.cot_pad[...] = jnp.zeros(r.cot_pad.shape, bf16)
    load["state"].wait()
    for i in range(2):
        r.rows[i, 0:valid, :] = r.state[:, i, :]
    west, east = edge_pair(r.rows[0].astype(f32), r.rows[1].astype(f32), valid - 1)
    r.edges[0] = west
    r.edges[1] = east
    load["cot"].wait()
    load["out"].wait()
    for i in range(2):
        r.cot_pad[i * CELLS : i * CELLS + valid, :] = r.cot[:, i, :]
    r.projected[:, 1536:2048] = nt_dot(r.cot_pad[...], r.weight_out[...]).astype(bf16)
    for i in range(2):
        value = r.rows[i].astype(f32)
        value = value * inverse_rms(value) * r.first_gain[...]
        r.normed[i * CELLS : i * CELLS + CELLS, :] = value.astype(bf16)
    load["expand"].wait()

    def own_chunk(index, carry):
        lanes = pl.ds(pl.multiple_of(index * CHUNK, CHUNK), CHUNK)
        expanded = jnp.dot(r.normed[...], r.expand[:, lanes], preferred_element_type=f32)
        activated, slope = silu_parts(expanded)
        r.slope_expanded[:, lanes] = slope.astype(bf16)
        for i in range(2):
            r.act[i + 1, :, lanes] = activated[i * CELLS : i * CELLS + CELLS].astype(bf16)
        return carry

    lax.fori_loop(0, r.expand.shape[1] // CHUNK, own_chunk, 0)
    pl.semaphore_wait(pltpu.get_barrier_semaphore(), greetings)
    copies = halo_copies(r.rows, r.edges, r.row_slots, r.edge_slots, r.state_sends, r.state_recvs)
    halo_start(copies)
    r.total[...] = jnp.zeros(r.total.shape, f32)
    r.bias_cells[...] = jnp.zeros(r.bias_cells.shape, f32)
    bias_lane = lax.broadcasted_iota(jnp.int32, (16, 128), 1)
    for i in range(2):
        r.bias_cells[i, :, 0:valid] = r.bias[i].astype(f32)
        heads = r.bias_cells[i]
        r.bias_low[i * 16 : i * 16 + 16, :] = jnp.where(bias_lane < 48, heads, 0.0)
        r.bias_high[i * 16 : i * 16 + 16, :] = jnp.where(bias_lane < 48, pltpu.roll(heads, 80, 1), 0.0)
    for a in range(3):
        r.depth[a * 3 : a * 3 + 3, :] = r.depth_low[a].astype(f32)
    load["shrink"].wait()
    halo_arrive(copies)
    far = [halo_row(row, r.row_slots[row // 3].astype(f32), r.edge_slots, valid) for row in (0, 3)]
    far = jnp.concatenate(far + [r.edge_slots[0, 1], r.edge_slots[1, 1]], axis=0)
    far = far * inverse_rms(far) * r.first_gain[...]
    r.wide_normed[...] = far.astype(bf16)

    def chunk(index, carry):
        start = pl.multiple_of(index * CHUNK, CHUNK)
        lanes = pl.ds(start, CHUNK)
        expanded = jnp.dot(r.wide_normed[...], r.expand[:, lanes], preferred_element_type=f32)
        activated = silu_parts(expanded)[0].astype(bf16)
        r.act[0, :, lanes] = activated[0:CELLS]
        r.act[3, :, lanes] = activated[CELLS : 2 * CELLS]
        activated = activated.astype(f32)
        planes = [activated[0:CELLS]]
        for i in range(2):
            base = r.act[i + 1, :, lanes].astype(f32)
            spot = lax.broadcasted_iota(jnp.int32, base.shape, 0)
            east, west = 2 * CELLS + i, 2 * CELLS + 8 + i
            plane = jnp.where(
                spot == valid,
                activated[east : east + 1],
                jnp.where(spot == CELLS - 1, activated[west : west + 1], base),
            )
            r.act[i + 1, :, lanes] = plane.astype(bf16)
            planes.append(plane)
        planes.append(activated[CELLS : 2 * CELLS])
        mixes, slopes = [], []
        for i in range(2):
            sums = []
            for b in range(3):
                part = r.depth[b : b + 1, lanes] * planes[i]
                for a in (1, 2):
                    part = part + r.depth[a * 3 + b : a * 3 + b + 1, lanes] * planes[i + a]
                sums.append(part)
            convolved = pltpu.roll(sums[0], 1, 0) + sums[1] + pltpu.roll(sums[2], CELLS - 1, 0)
            mixed, slope = silu_parts(convolved)
            keep = inside(mixed.shape, valid)
            mixes.append(jnp.where(keep, mixed, 0.0).astype(bf16))
            slope = jnp.where(keep, slope, 0.0)
            r.slope[i, :, lanes] = slope.astype(bf16)
            slopes.append(slope)
        west, east = edge_pair(slopes[0], slopes[1], valid - 1)
        r.slope_edges[0, :, lanes] = west
        r.slope_edges[1, :, lanes] = east
        mixed = jnp.concatenate(mixes, axis=0)
        r.mixed[:, lanes] = mixed
        r.total[...] += jnp.dot(
            mixed, r.shrink[pl.ds(start, CHUNK), :], preferred_element_type=f32
        )
        return carry

    lax.fori_loop(0, r.expand.shape[1] // CHUNK, chunk, 0)
    for i in range(2):
        part = slice(i * CELLS, i * CELLS + CELLS)
        inner = (r.rows[i].astype(f32) + r.total[part, :]).astype(bf16)
        r.inner[part, :] = inner
        inner = inner.astype(f32)
        r.second[part, :] = (inner * inverse_rms(inner) * r.second_gain[...]).astype(bf16)
    load["in"].wait()
    return copies


def project_and_pack(r, valid, first, last, target, with_bias):
    f32, bf16 = jnp.float32, jnp.bfloat16
    lane = lax.broadcasted_iota(jnp.int32, (CELLS, 128), 1)
    row = lax.broadcasted_iota(jnp.int32, (CELLS, 128), 0)
    for i in range(2):
        cells = slice(i * CELLS, i * CELLS + CELLS)
        for tile in range(4):
            parts = [
                r.projected[cells, base + tile * 128 : base + tile * 128 + 128].astype(f32)
                for base in (first, last)
            ]
            for u in range(4):
                item = i * 16 + tile * 4 + u
                moved = [
                    value if side == u else pltpu.roll(value, ((side - u) * 32) % 128, 1)
                    for side, value in enumerate(parts)
                ]
                value = jnp.where(lane < 32, moved[0], jnp.where(lane < 64, moved[1], 0.0))
                if with_bias:
                    value = jnp.where(row == valid, r.bias_low[item : item + 1, :], value)
                    value = jnp.where(row == valid + 1, r.bias_high[item : item + 1, :], value)
                target[item] = packed(value)


def attention_phase(r, valid, scale):
    sources = r.kv_in.shape[0]
    total = sources * CELLS
    block = r.scores.shape[1]
    group = block // CELLS
    log2e = 1.4426950408889634
    to_log2 = scale * log2e
    f32, bf16 = jnp.float32, jnp.bfloat16
    lat, lon = lax.axis_index("lat"), lax.axis_index("lon")
    groups = sources // group
    ring, own_group = r.ring, lax.div(lon, group)

    def key_copy(k, to, slot):
        return exchange(
            r.kv_out.at[to], r.kv_in.at[slot], r.kv_sends, r.kv_recvs, k, (lat, to)
        )

    def query_copy(to, slot):
        return exchange(
            r.qd_out.at[to], r.qd_in.at[slot], r.qd_sends, r.qd_recvs, to, (lat, to), slot
        )

    def near_copy(to, slot):
        return exchange(
            r.near_out.at[to], r.near_in.at[slot], r.near_sends, r.near_recvs, to, (lat, to), slot
        )

    def last_copy(k, to, slot):
        return exchange(
            r.last_out.at[to], r.last_in.at[slot], r.last_sends, r.last_recvs, k, (lat, to)
        )

    r.projected[:, 512:1536] = jnp.dot(
        r.second[...], r.weight_in[:, 512:1536], preferred_element_type=f32
    ).astype(bf16)
    project_and_pack(r, valid, 512, 1024, r.kv_out, True)

    for k in range(sources - 1):
        key_copy(k, ring.partner(k, 1), lon).start()
    r.projected[:, 0:512] = jnp.dot(
        r.second[...], r.weight_in[:, 0:512], preferred_element_type=f32
    ).astype(bf16)
    project_and_pack(r, valid, 0, 1536, r.qd_out, False)

    for step in range(groups):
        target = lax.rem(own_group + groups - step, groups) * group
        for part in range(group):
            to = target + part
            if step:
                query_copy(to, lon).start()
            else:

                @pl.when(to != lon)
                def _():
                    query_copy(to, lon).start()

    halo = halo_copies(
        r.slope, r.slope_edges, r.slope_rows, r.slope_sides, r.slope_sends, r.slope_recvs
    )
    halo_start(halo)
    r.kv_in[lon] = r.kv_out[lon]
    r.qd_in[lon] = r.qd_out[lon]

    def prepare(index):
        raw = unpacked(r.kv_in[index])
        row = lax.broadcasted_iota(jnp.int32, (CELLS, 128), 0)
        lane = lax.broadcasted_iota(jnp.int32, (CELLS, 128), 1)
        bias_row = jnp.where(row < 48, raw[valid : valid + 1, :], raw[valid + 1 : valid + 2, :])
        wanted = jnp.where(row < 48, row, row - 48)
        bias = jnp.sum(jnp.where(wanted == lane, bias_row, 0.0), axis=1, keepdims=True) * log2e
        bias = jnp.broadcast_to(bias, (CELLS, 128))
        first = bias.astype(bf16).astype(f32)
        second = (bias - first).astype(bf16).astype(f32)
        third = bias - first - second
        first = jnp.where(row < valid, first, -1e30)
        second = jnp.where(row < valid, second, 0.0)
        third = jnp.where(row < valid, third, 0.0)
        cell = jnp.where(row < valid, raw, 0.0)
        key = jnp.where(lane < 32, cell, 0.0)
        value = jnp.where(lane >= 32, cell, 0.0)
        keys = key + pltpu.roll(key, 32, 1) + pltpu.roll(key, 64, 1)
        keys = jnp.where(lane == 96, first, keys)
        keys = jnp.where(lane == 97, second, keys)
        keys = jnp.where(lane == 98, third, keys)
        values = value + pltpu.roll(value, 96, 1)
        values = jnp.where((lane >= 64) & (lane < 67), 1.0, values)
        start = pl.multiple_of(index * CELLS, 32)
        r.kaug[pl.ds(start, CELLS), :] = keys.astype(bf16)
        r.vaug[pl.ds(start, CELLS), :] = values.astype(bf16)
        r.cell[pl.ds(start, CELLS), :] = cell

    prepare(lon)

    for part in range(8):
        first = ring.start(part, -1)

        def arrive(step, carry):
            flip_x = (step < 2).astype(jnp.int32)
            flip_core = 3 - step - 2 * flip_x
            source = first + ring.side(flip_x, flip_core)
            key_copy(part * 4 + step, source, source).wait_recv()
            prepare(source)
            return carry

        lax.fori_loop(0, 4 if part < 7 else 3, arrive, 0)

    def turn(index, carry):
        start = pl.multiple_of(index * block, block)
        r.xt[:, pl.ds(start, block)] = r.cell[pl.ds(start, block), :].T[0:64].astype(bf16)
        r.acc[:, pl.ds(start, block)] = jnp.zeros((64, block), f32)
        return carry

    lax.fori_loop(0, total // block, turn, 0)

    def one_block(turn_index, carry):
        index = lax.rem(turn_index + own_group, groups)
        for part in range(group):
            source = index * group + part

            @pl.when(source != lon)
            def _():
                query_copy(source, source).wait_recv()

            r.qd_cell[part * CELLS : part * CELLS + CELLS, :] = unpacked(r.qd_in[source])
        xt = r.qd_cell[...].T
        query = xt[0:32] * to_log2
        first = query.astype(bf16).astype(f32)
        second = (query - first).astype(bf16).astype(f32)
        third = query - first - second
        qaug = jnp.concatenate(
            [first, second, third, jnp.ones((32, block), f32)], axis=0
        ).astype(bf16)
        t = jnp.dot(r.kaug[...], qaug, preferred_element_type=f32)
        r.scores[...] = t
        highest = jnp.max(jnp.max(t.reshape(total // 8, 8, block), axis=0), axis=0, keepdims=True)
        p = jnp.exp2(r.scores[...] - highest)
        r.scores[...] = p
        low_p = p.astype(bf16)
        r.low[...] = low_p
        norm = jnp.sum(p.reshape(total // 8, 8, block), axis=0)
        heads = jnp.dot(r.xt[32:64, :], low_p, preferred_element_type=f32)
        inverse = 1.0 / jnp.sum(norm, axis=0, keepdims=True)
        heads = heads * inverse
        back = xt[32:64]
        centred = jnp.sum(back * heads, axis=0, keepdims=True) * inverse
        back = back * inverse
        back_first = back.astype(bf16).astype(f32)
        back_second = back - back_first
        cen_first = centred.astype(bf16).astype(f32)
        cen_second = (centred - cen_first).astype(bf16).astype(f32)
        cen_third = centred - cen_first - cen_second
        sub = lax.broadcasted_iota(jnp.int32, (64, block), 0)
        cen = jnp.where(
            sub == 0,
            cen_first,
            jnp.where(sub == 1, cen_second, jnp.where(sub == 2, cen_third, 0.0)),
        )
        baug = jnp.concatenate([back_first, back_second, -cen], axis=0).astype(bf16)
        dp = jnp.dot(r.vaug[...], baug, preferred_element_type=f32)
        ds = (r.scores[...] * dp).astype(bf16)
        r.acc[32:64, :] += nt_dot(back_first.astype(bf16), r.low[...])
        r.acc[0:32, :] += nt_dot(xt[0:32].astype(bf16), ds)
        back_queries = jnp.dot(r.xt[0:32, :], ds, preferred_element_type=f32)
        zeros = jnp.zeros((64, block), f32)
        done = jnp.concatenate([back_queries * scale, heads, zeros], axis=0).T
        for part in range(group):
            source = index * group + part
            r.near_out[source] = packed(done[part * CELLS : part * CELLS + CELLS])

            @pl.when(source != lon)
            def _():
                near_copy(source, lon).start()

        return carry

    lax.fori_loop(0, groups, one_block, 0)
    r.near_in[lon] = r.near_out[lon]

    def finish(index, carry):
        start = pl.multiple_of(index * block, block)
        both = r.acc[:, pl.ds(start, block)]
        zeros = jnp.zeros((64, block), f32)
        both = jnp.concatenate([both[0:32] * scale, both[32:64], zeros], axis=0)
        r.cell[pl.ds(start, block), :] = both.T
        return carry

    lax.fori_loop(0, total // block, finish, 0)

    def pack_last(source):
        start = pl.multiple_of(source * CELLS, 32)
        r.last_out[source] = packed(r.cell[pl.ds(start, CELLS), :])

    for k in range(sources - 1):
        to = ring.partner(k, 1)
        pack_last(to)
        last_copy(k, to, lon).start()
    pack_last(lon)
    r.last_in[lon] = r.last_out[lon]

    def near_arrive():
        for k in range(sources - 1):
            source = ring.partner(k, -1)
            near_copy(source, source).wait_recv()

    def last_arrive():
        for k in range(sources - 1):
            source = ring.partner(k, -1)
            last_copy(k, source, source).wait_recv()

    def settle():
        for k in range(sources - 1):
            to = ring.partner(k, 1)
            key_copy(k, to, lon).wait_send()
            query_copy(to, lon).wait_send()
            near_copy(to, lon).wait_send()
            last_copy(k, to, lon).wait_send()

    return halo, near_arrive, last_arrive, settle


def gather_heads(source, first, second, i, tile):
    half_lane = lax.broadcasted_iota(jnp.int32, (48, 128), 1)
    parts = [source[i * 16 + tile * 4 + u].astype(jnp.float32) for u in range(4)]
    for (target, column), lane in ((first, 0), (second, 32)):
        for half in range(2):
            value = None
            for u in range(4):
                shift = (u * 32 - lane - half * 64) % 128
                moved = pltpu.roll(parts[u], shift, 1) if shift else parts[u]
                value = moved if value is None else jnp.where(half_lane < u * 32, value, moved)
            start, column_start = i * CELLS + half * 48, column + tile * 128
            target[start : start + 48, column_start : column_start + 128] = value.astype(
                jnp.bfloat16
            )


def backward_phase(r, valid, factor, slope_halo, near_arrive, last_arrive, peers):
    f32, bf16 = jnp.float32, jnp.bfloat16
    sibling, x_peers, y_peers, z_peers = peers
    lat, lon = lax.axis_index("lat"), lax.axis_index("lon")
    y = lax.rem(lat, 4)
    z, x_lo, core = lax.div(lon, 4), r.ring.x_lo, r.ring.core
    x = lax.div(lat, 4) * 2 + x_lo
    other = 1 - core
    xs, ys = [lax.rem(x + d, 4) for d in range(4)], [lax.rem(y + d, 4) for d in range(4)]
    zs = [lax.rem(z + d, 8) for d in range(8)]
    r.small[...] = jnp.zeros(r.small.shape, f32)
    near_arrive()
    for i in range(2):
        for tile in range(4):
            gather_heads(r.near_in, (r.back_project, 0), (r.heads, 0), i, tile)
    field = jnp.dot(r.heads[...], r.weight_out[...], preferred_element_type=f32)
    for i in range(2):
        part = slice(i * CELLS, i * CELLS + CELLS)
        r.field[i] = (r.inner[part, :].astype(f32) + field[part]).astype(bf16)[0:valid]
    back_second = nt_dot(r.back_project[:, 0:512], r.weight_in[:, 0:512])
    last_arrive()
    for i in range(2):
        for tile in range(4):
            gather_heads(r.last_in, (r.back_project, 512), (r.back_project, 1024), i, tile)
    back_second = back_second + nt_dot(r.back_project[:, 512:1536], r.weight_in[:, 512:1536])
    gain_two = jnp.zeros((1, field.shape[1]), f32)
    for i in range(2):
        part = slice(i * CELLS, i * CELLS + CELLS)
        inner = r.inner[part, :].astype(f32)
        inverse = inverse_rms(inner)
        gain_two = gain_two + jnp.sum(back_second[part] * inner * inverse, axis=0, keepdims=True)
        scaled = back_second[part] * r.second_gain[...]
        back = (
            r.cot_pad[part, :].astype(f32)
            + inverse * scaled
            - inverse * inverse * inverse * inner * jnp.mean(scaled * inner, axis=-1, keepdims=True)
        )
        r.back_rows[i] = back.astype(bf16)
    west, east = edge_pair(r.back_rows[0].astype(f32), r.back_rows[1].astype(f32), valid - 1)
    r.back_edges[0] = west
    r.back_edges[1] = east
    halo = halo_copies(
        r.back_rows, r.back_edges, r.back_slots, r.back_sides, r.back_sends, r.back_recvs
    )
    halo_start(halo)

    def half_lanes(top, bottom):
        lane = lax.broadcasted_iota(jnp.int32, top.shape, 1)
        even = jnp.where(lane < 64, top, pltpu.roll(bottom, 64, 1))
        odd = jnp.where(lane < 64, pltpu.roll(top, 64, 1), bottom)
        return even, odd

    def cross(left, right):
        return (
            lax.dot_general(left, right, (((0,), (0,)), ((), ())), preferred_element_type=f32)
            * factor
        )

    def core_copy(mine, theirs, first, width, index):
        rows = pl.ds(first, width)
        return exchange(
            mine.at[other, rows], theirs.at[rows], r.core_sends, r.core_recvs, index, sibling
        )

    def early_x(zz):
        return core_copy(r.ex, r.ex0, zz * 2, 2, zz)

    def early_y(zz):
        return core_copy(r.ey, r.ey0, zz * 2, 2, 4 + zz)

    def late_x(pz):
        return core_copy(r.lx, r.lx0, pz, 1, 8 + pz)

    def late_y(pz):
        return core_copy(r.ly, r.ly0, pz, 1, 16 + pz)

    def early_part(zz, carry):
        columns = pl.ds(pl.multiple_of(zz * 128, 128), 128)
        own = jnp.concatenate([r.back_rows[0, :, columns], r.back_rows[1, :, columns]], axis=0)
        shrink = cross(own, r.mixed[...])
        grad_in = cross(
            r.back_project[:, pl.ds(pl.multiple_of(zz * 384, 128), 384)], r.second[...]
        )
        grad_out = cross(r.cot_pad[:, columns], r.heads[...])
        for sub in range(8):
            pz, plo, pc = zz * 2 + sub // 4, (sub // 2) % 2, sub % 2
            for plat in range(8):
                px, py = (plat // 4) * 2 + plo, plat % 4
                part = slice(sub * 16, sub * 16 + 16)
                for side in range(2):
                    column = plat * 256 + side * 128
                    r.ex[pc, pz, px, py, side * 16 : side * 16 + 16, :] = shrink[
                        part, column : column + 128
                    ].astype(bf16)
            for pair in range(4):
                tile = slice(pair * 128, pair * 128 + 128)
                top = jnp.concatenate(
                    [grad_in[sub * 48 : sub * 48 + 24, tile], grad_out[sub * 16 : sub * 16 + 8, tile]],
                    axis=0,
                )
                bottom = jnp.concatenate(
                    [
                        grad_in[sub * 48 + 24 : sub * 48 + 48, tile],
                        grad_out[sub * 16 + 8 : sub * 16 + 16, tile],
                    ],
                    axis=0,
                )
                parts = half_lanes(top, bottom)
                for odd in range(2):
                    plat = pair * 2 + odd
                    px, py = (plat // 4) * 2 + plo, plat % 4
                    r.ey[pc, pz, py, px] = parts[odd].astype(bf16)
        early_x(zz).start()
        early_y(zz).start()
        return carry

    lax.fori_loop(0, 4, early_part, 0)

    def add_pair(mine, theirs, pz):
        for q in range(4):
            mine[core, pz, q] = (mine[core, pz, q].astype(f32) + theirs[pz, q].astype(f32)).astype(bf16)

    def early_arrive(zz, carry):
        early_x(zz).wait_recv()
        early_y(zz).wait_recv()
        for step in range(2):
            add_pair(r.ex, r.ex0, zz * 2 + step)
            add_pair(r.ey, r.ey0, zz * 2 + step)
        return carry

    lax.fori_loop(0, 4, early_arrive, 0)
    count = [0]

    def copy(source, target, peer):
        index = count[0]
        count[0] += 1
        made = exchange(source, target, r.sends, r.recvs, index, peer)
        made.start()
        return made

    def stage_one(mine, slots, targets, turns):
        return [
            copy(mine.at[core, :, turns[d]], slots.at[d - 1], targets[d - 1])
            for d in (1, 2, 3)
        ]

    early_one_x = stage_one(r.ex, r.ex1, x_peers, xs)
    early_one_y = stage_one(r.ey, r.ey1, y_peers, ys)
    halo_arrive(slope_halo)
    halo_arrive(halo)
    for row in range(4):
        base = r.back_rows[row - 1] if row in (1, 2) else r.back_slots[row // 3]
        value = halo_row(row, base.astype(f32), r.back_sides, valid)
        r.wide_back[row * CELLS : row * CELLS + CELLS, :] = value.astype(bf16)
    r.back_normed[...] = jnp.zeros(r.back_normed.shape, f32)

    def chunk(pz, carry):
        start = pl.multiple_of(pz * CHUNK, CHUNK)
        lanes = pl.ds(start, CHUNK)
        product = nt_dot(r.wide_back[...], r.shrink[lanes, :])
        planes = []
        for row in range(4):
            base = r.slope[row - 1, :, lanes] if row in (1, 2) else r.slope_rows[row // 3, :, lanes]
            slope = halo_row(row, base.astype(f32), r.slope_sides, valid, lanes)
            plane = product[row * CELLS : row * CELLS + CELLS] * slope
            planes.append(plane.astype(bf16).astype(f32))
        for b in range(3):
            turned = []
            for i in range(2):
                centre = planes[i + 1]
                centre = jnp.where(inside(centre.shape, valid), centre, 0.0)
                turned.append(pltpu.roll(centre, (CELLS + b - 1) % CELLS, 0) if b != 1 else centre)
            for a in range(3):
                value = r.act[a, :, lanes].astype(f32) * turned[0]
                value = value + r.act[a + 1, :, lanes].astype(f32) * turned[1]
                r.small[a * 3 + b : a * 3 + b + 1, lanes] = (
                    jnp.sum(value, axis=0, keepdims=True) * factor
                )
        outs = []
        for i in range(2):
            sums = []
            for b in range(3):
                part = r.depth[b : b + 1, lanes] * planes[i + 2]
                for a in (1, 2):
                    part = part + r.depth[a * 3 + b : a * 3 + b + 1, lanes] * planes[i + 2 - a]
                sums.append(part)
            total = pltpu.roll(sums[0], CELLS - 1, 0) + sums[1] + pltpu.roll(sums[2], 1, 0)
            total = total * r.slope_expanded[i * CELLS : i * CELLS + CELLS, lanes].astype(f32)
            outs.append(jnp.where(inside(total.shape, valid), total, 0.0).astype(bf16))
        back = jnp.concatenate(outs, axis=0)
        r.back_normed[...] += nt_dot(back, r.expand[:, lanes])
        grad = cross(back, r.normed[...])
        for sub in range(4):
            plo, pc = sub // 2, sub % 2
            for pair in range(4):
                tile = slice(pair * 128, pair * 128 + 128)
                parts = half_lanes(
                    grad[sub * 64 : sub * 64 + 32, tile], grad[sub * 64 + 32 : sub * 64 + 64, tile]
                )
                for odd in range(2):
                    plat = pair * 2 + odd
                    px, py = (plat // 4) * 2 + plo, plat % 4
                    r.lx[pc, pz, px, py] = parts[odd][0:16].astype(bf16)
                    r.ly[pc, pz, py, px] = parts[odd][16:32].astype(bf16)
        late_x(pz).start()
        late_y(pz).start()
        return carry

    lax.fori_loop(0, 8, chunk, 0)
    gain_one = jnp.zeros((1, r.back_normed.shape[1]), f32)
    for i in range(2):
        part = slice(i * CELLS, i * CELLS + valid)
        state = r.rows[i, 0:valid, :].astype(f32)
        inverse = inverse_rms(state)
        back = r.back_normed[part, :]
        gain_one = gain_one + jnp.sum(back * state * inverse, axis=0, keepdims=True)
        scaled = back * r.first_gain[...]
        r.grad[i] = (
            r.back_rows[i, 0:valid, :].astype(f32)
            + inverse * scaled
            - inverse * inverse * inverse * state * jnp.mean(scaled * state, axis=-1, keepdims=True)
        ).astype(bf16)
    width = r.small.shape[1]
    r.small[9:10, :] = jnp.concatenate(
        [gain_one * factor, gain_two * factor, jnp.zeros((1, width - 1024), f32)], axis=1
    )
    for tile in range(16):
        for part in range(2):
            r.small_split[tile * 2 + part] = r.small[
                part * 8 : part * 8 + 8, tile * 128 : tile * 128 + 128
            ]
    sectors, bands = r.small_lon.shape[0], r.small_lat.shape[0]
    columns = [(r.ring.partner(k, 1), r.ring.partner(k, -1)) for k in range(sectors - 1)]

    def scatter(k, to, slot):
        return exchange(
            r.small_split.at[to], r.small_lon.at[slot], r.small_sends, r.small_recvs, k, (lat, to)
        )

    def spread(k, to, slot):
        return exchange(
            r.sums.at[lon], r.sums.at[slot], r.spread_sends, r.spread_recvs, k, (lat, to)
        )

    for k, (to, _) in enumerate(columns):
        scatter(k, to, lon).start()
    r.small_lon[lon] = r.small_split[lon]

    def late_arrive(pz, carry):
        late_x(pz).wait_recv()
        late_y(pz).wait_recv()
        add_pair(r.lx, r.lx0, pz)
        add_pair(r.ly, r.ly0, pz)
        return carry

    lax.fori_loop(0, 8, late_arrive, 0)
    late_one_x = stage_one(r.lx, r.lx1, x_peers, xs)
    late_one_y = stage_one(r.ly, r.ly1, y_peers, ys)

    def add_four(mine, theirs, here, total):
        def body(pz, carry):
            value = mine[core, pz, here].astype(f32)
            for d in range(3):
                value = value + theirs[d, pz].astype(f32)
            total[pz] = value.astype(bf16)
            return carry

        lax.fori_loop(0, 8, body, 0)

    def stage_two(arrivals, mine, slots, here, total, next_slots, targets, turns):
        for made in arrivals:
            made.wait_recv()
        add_four(mine, slots, here, total)
        return [
            copy(total.at[:, turns[d]], next_slots.at[d - 1], targets[d - 1])
            for d in (1, 2, 3)
        ]

    early_two_x = stage_two(early_one_x, r.ex, r.ex1, x, r.ext, r.ex2, y_peers, ys)
    early_two_y = stage_two(early_one_y, r.ey, r.ey1, y, r.eyt, r.ey2, x_peers, xs)

    def stage_three(arrivals, total, slots, here, first, count_rows):
        for made in arrivals:
            made.wait_recv()

        def body(pz, carry):
            value = total[pz, here].astype(f32)
            for d in range(3):
                value = value + slots[d, pz].astype(f32)
            r.final[pz, first : first + count_rows, :] = value.astype(bf16)
            return carry

        lax.fori_loop(0, 8, body, 0)

    def send_final(first, count_rows):
        rows = pl.ds(first, count_rows)
        return [
            copy(r.final.at[zs[d], rows], r.final_in.at[d - 1, rows], z_peers[d - 1])
            for d in range(1, 8)
        ]

    stage_three(early_two_x, r.ext, r.ex2, y, 0, 32)
    stage_three(early_two_y, r.eyt, r.ey2, x, 32, 32)
    final_early = send_final(0, 64)
    late_two_x = stage_two(late_one_x, r.lx, r.lx1, x, r.lxt, r.lx2, y_peers, ys)
    late_two_y = stage_two(late_one_y, r.ly, r.ly1, y, r.lyt, r.ly2, x_peers, xs)

    for k, (_, source) in enumerate(columns):
        scatter(k, source, source).wait_recv()
    total = r.small_lon[0]
    for index in range(1, sectors):
        total = total + r.small_lon[index]
    r.small_lat[lat] = total
    small_lat = [
        copy(r.small_lat.at[lat], r.small_lat.at[lat], (lax.rem(lat + d, bands), lon))
        for d in range(1, bands)
    ]

    stage_three(late_two_x, r.lxt, r.lx2, y, 64, 16)
    stage_three(late_two_y, r.lyt, r.ly2, x, 80, 16)
    final_late = send_final(64, 32)

    for made in small_lat:
        made.wait_recv()
    total = r.small_lat[0]
    for index in range(1, bands):
        total = total + r.small_lat[index]
    r.sums[lon] = total
    for k, (to, _) in enumerate(columns):
        spread(k, to, lon).start()

    for made in final_early + final_late:
        made.wait_recv()
    value = r.final[z].astype(f32)
    for d in range(7):
        value = value + r.final_in[d].astype(f32)
    r.block[...] = value
    for k, (to, source) in enumerate(columns):
        spread(k, source, source).wait_recv()
        spread(k, to, lon).wait_send()
        scatter(k, to, lon).wait_send()
    for made in (
        early_one_x
        + early_one_y
        + late_one_x
        + late_one_y
        + early_two_x
        + early_two_y
        + late_two_x
        + late_two_y
        + final_early
        + final_late
        + small_lat
    ):
        made.wait_send()

    def settle(pz, carry):
        late_x(pz).wait_send()
        late_y(pz).wait_send()
        return carry

    def settle_early(zz, carry):
        early_x(zz).wait_send()
        early_y(zz).wait_send()
        return carry

    lax.fori_loop(0, 8, settle, 0)
    lax.fori_loop(0, 4, settle_early, 0)
    halo_leave(halo)


def step_kernel(names, valid, scale, factor, *refs):
    r = Refs(names, refs)
    lat, lon = lax.axis_index("lat"), lax.axis_index("lon")
    sectors = lax.axis_size("lon")
    y, z, core = lax.rem(lat, 4), lax.div(lon, 4), lax.rem(lon, 2)
    x = lax.div(lat, 4) * 2 + lax.rem(lax.div(lon, 2), 2)

    def place(px, py, pz, pc):
        return (lax.div(px, 2) * 4 + py, pz * 4 + lax.rem(px, 2) * 2 + pc)

    barrier = pltpu.get_barrier_semaphore()
    peers = (
        place(x, y, z, 1 - core),
        [place(lax.rem(x + d, 4), y, z, core) for d in range(1, 4)],
        [place(x, lax.rem(y + d, 4), z, core) for d in range(1, 4)],
        [place(x, y, lax.rem(z + d, 8), core) for d in range(1, 8)],
    )
    greetings = halo_greet(barrier)
    bands = lax.axis_size("lat")
    band_peers = [(lax.rem(lat + d, bands), lon) for d in range(1, bands)]
    for peer in peers[1] + peers[2] + band_peers:
        pl.semaphore_signal(barrier, inc=1, device_id=peer, device_id_type=MESH)

    r.ring = Ring()
    for k in range(sectors - 1):
        pl.semaphore_signal(
            barrier, inc=1, device_id=(lat, r.ring.partner(k, 1)), device_id_type=MESH
        )
    greetings = greetings + len(peers[1]) + len(peers[2]) + bands - 1 + sectors - 1
    load = {}
    for index, (name, source, target) in enumerate(
        (
            ("state", r.state_hbm, r.state),
            ("cot", r.cot_hbm, r.cot),
            ("out", r.out_hbm, r.weight_out),
            ("expand", r.expand_hbm, r.expand),
            ("shrink", r.shrink_hbm, r.shrink),
            ("in", r.in_hbm, r.weight_in),
        )
    ):
        load[name] = pltpu.make_async_copy(source, target, r.loads.at[index])
        load[name].start()
    state_halo = forward_phase(r, load, valid, greetings)
    slope_halo, near_arrive, last_arrive, settle = attention_phase(r, valid, scale)
    backward_phase(r, valid, factor, slope_halo, near_arrive, last_arrive, peers)
    settle()
    halo_leave(state_halo)
    halo_leave(slope_halo)


def whole_step(factor, scale, operands, bias, depth, first_gain, second_gain):
    f32, bf16 = jnp.float32, jnp.bfloat16
    state, cot, expand, shrink, weight_in, weight_out = operands
    valid = state.shape[0]
    channels, wide = expand.shape
    cells = 2 * CELLS
    sources = lax.axis_size("lon")
    total, block = sources * CELLS, 768
    vmem, dma = pltpu.VMEM, pltpu.SemaphoreType.DMA
    message = vmem((sources, 48, 128), bf16)

    def tree(name, rows):
        return {
            name: vmem((2, 8, 4, 4, rows, 128), bf16),
            name + "0": vmem((8, 4, 4, rows, 128), bf16),
            name + "1": vmem((3, 8, 4, rows, 128), bf16),
            name + "t": vmem((8, 4, rows, 128), bf16),
            name + "2": vmem((3, 8, rows, 128), bf16),
        }

    def halo_set(prefix, width):
        return {prefix + "sends": dma((8,)), prefix + "recvs": dma((8,))}

    scratch = {
        "state": vmem(state.shape, bf16),
        "cot": vmem(cot.shape, bf16),
        "expand": vmem(expand.shape, bf16),
        "shrink": vmem(shrink.shape, bf16),
        "weight_in": vmem(weight_in.shape, bf16),
        "weight_out": vmem(weight_out.shape, bf16),
        "bias_cells": vmem((2, 16, 128), f32),
        "bias_low": vmem((32, 128), f32),
        "bias_high": vmem((32, 128), f32),
        "depth": vmem((16, wide), f32),
        "rows": vmem((2, CELLS, channels), bf16),
        "edges": vmem((2, 8, channels), f32),
        "row_slots": vmem((2, CELLS, channels), bf16),
        "edge_slots": vmem((2, 3, 8, channels), f32),
        "back_rows": vmem((2, CELLS, channels), bf16),
        "back_edges": vmem((2, 8, channels), f32),
        "back_slots": vmem((2, CELLS, channels), bf16),
        "back_sides": vmem((2, 3, 8, channels), f32),
        "slope": vmem((2, CELLS, wide), bf16),
        "slope_edges": vmem((2, 8, wide), f32),
        "slope_rows": vmem((2, CELLS, wide), bf16),
        "slope_sides": vmem((2, 3, 8, wide), f32),
        "wide_normed": vmem((2 * CELLS + 16, channels), bf16),
        "wide_back": vmem((4 * CELLS, channels), bf16),
        "total": vmem((cells, channels), f32),
        "back_normed": vmem((cells, channels), f32),
        "projected": vmem((cells, 4 * channels), bf16),
        "back_project": vmem((cells, 3 * channels), bf16),
        "heads": vmem((cells, channels), bf16),
        "cot_pad": vmem((cells, channels), bf16),
        "act": vmem((4, CELLS, wide), bf16),
        "slope_expanded": vmem((cells, wide), bf16),
        "mixed": vmem((cells, wide), bf16),
        "normed": vmem((cells, channels), bf16),
        "inner": vmem((cells, channels), bf16),
        "second": vmem((cells, channels), bf16),
        "kv_out": message,
        "kv_in": message,
        "qd_out": message,
        "qd_in": message,
        "near_out": message,
        "near_in": message,
        "last_out": message,
        "last_in": message,
        "xt": vmem((64, total), bf16),
        "kaug": vmem((total, 128), bf16),
        "vaug": vmem((total, 128), bf16),
        "scores": vmem((total, block), f32),
        "low": vmem((total, block), bf16),
        "acc": vmem((64, total), f32),
        "cell": vmem((total, 128), f32),
        "qd_cell": vmem((block, 128), f32),
        **tree("ex", 32),
        **tree("ey", 32),
        **tree("lx", 16),
        **tree("ly", 16),
        "final": vmem((8, 96, 128), bf16),
        "final_in": vmem((7, 96, 128), bf16),
        "small": vmem((16, wide), f32),
        "small_split": vmem((sources, 8, 128), f32),
        "small_lon": vmem((sources, 8, 128), f32),
        "small_lat": vmem((lax.axis_size("lat"), 8, 128), f32),
        "loads": dma((6,)),
        "core_sends": dma((24,)),
        "core_recvs": dma((24,)),
        "sends": dma((66,)),
        "recvs": dma((66,)),
    }
    for prefix in ("state_", "slope_", "back_"):
        scratch[prefix + "sends"] = dma((8,))
        scratch[prefix + "recvs"] = dma((8,))
    for prefix in ("kv_", "qd_", "near_", "last_", "small_", "spread_"):
        scratch[prefix + "sends"] = dma((sources,))
        scratch[prefix + "recvs"] = dma((sources,))
    inputs = [name + "_hbm" for name in ("state", "cot", "expand", "shrink", "in", "out")]
    inputs += ["bias", "depth_low", "first_gain", "second_gain"]
    outputs = {
        "field": ((2, valid, channels), bf16),
        "grad": ((2, valid, channels), bf16),
        "block": ((96, 128), f32),
        "sums": ((sources, 8, 128), f32),
    }
    names = inputs + list(outputs) + list(scratch)
    whole, anywhere = pl.BlockSpec(memory_space=vmem), pl.BlockSpec(memory_space=pl.ANY)
    return pl.pallas_call(
        functools.partial(step_kernel, names, valid, scale, factor),
        out_shape=tuple(jax.ShapeDtypeStruct(*kind) for kind in outputs.values()),
        in_specs=[anywhere] * 6 + [whole] * 4,
        out_specs=(whole,) * 4,
        scratch_shapes=list(scratch.values()),
        compiler_params=pltpu.CompilerParams(
            vmem_limit_bytes=VMEM_MIB * 1024 * 1024, collective_id=1, has_side_effects=True
        ),
        name="step",
    )(*operands, bias, depth, first_gain, second_gain)


def deliver_kernel(
    block_ref,
    sums_ref,
    field_ref,
    grad_ref,
    expand_ref,
    shrink_ref,
    in_ref,
    out_ref,
    depth_ref,
    one_ref,
    two_ref,
    field_out,
    grad_out,
):
    for source, target in ((field_ref, field_out), (grad_ref, grad_out)):
        for i in range(2):
            target[:, i, :] = source[i]

    def unfold(part):
        return jnp.concatenate([part, pltpu.roll(part, 64, 1)], axis=0)

    block = block_ref[...]
    expand = unfold(block[64:96])
    expand = jnp.concatenate([expand, jnp.zeros_like(expand)], axis=0).T
    expand_ref[...] = expand[0:64, 0:64]
    shrink_ref[:, 0:128] = block[0:16]
    shrink_ref[:, 128:256] = block[16:32]
    in_ref[...] = unfold(block[32:56])[:, 0:64]
    out_ref[...] = unfold(block[56:64])[:, 0:64]
    for tile in range(16):
        lanes = slice(tile * 128, tile * 128 + 128)
        low, high = sums_ref[tile * 2], sums_ref[tile * 2 + 1]
        depth_ref[0, :, lanes] = low[0:3]
        depth_ref[1, :, lanes] = low[3:6]
        depth_ref[2, 0:2, lanes] = low[6:8]
        depth_ref[2, 2:3, lanes] = high[0:1]
        if tile < 4:
            one_ref[:, lanes] = high[1:2]
        elif tile < 8:
            two_ref[:, tile * 128 - 512 : tile * 128 - 384] = high[1:2]


def deliver(block, sums, field, grad, channels, wide):
    vmem = pl.BlockSpec(memory_space=pltpu.VMEM)
    shapes = [(64, 64), (16, 256), (48, 64), (16, 64), (3, 3, wide), (1, channels), (1, channels)]
    turned = jax.ShapeDtypeStruct((field.shape[1], 2, channels), field.dtype)
    expand, shrink, grad_in, grad_out, depth, one, two, field, grad = pl.pallas_call(
        deliver_kernel,
        out_shape=tuple(jax.ShapeDtypeStruct(shape, jnp.float32) for shape in shapes)
        + (turned, turned),
        in_specs=[vmem] * 4,
        out_specs=(vmem,) * 9,
        compiler_params=pltpu.CompilerParams(vmem_limit_bytes=16 * 1024 * 1024),
        name="deliver",
    )(block, sums, field, grad)
    field, grad = field.transpose(1, 0, 2), grad.transpose(1, 0, 2)
    one, two = one.reshape(channels), two.reshape(channels)
    return field, grad, expand, shrink.T, grad_in.T, grad_out.T, depth, one, two


def per_device(
    state_field,
    cotangent,
    key_bias,
    input_gain,
    expand_weight,
    depth_weight,
    shrink_weight,
    attention_gain,
    attention_in,
    attention_out,
):
    row_count, lon_count, channels = state_field.shape
    head_count = key_bias.shape[2]
    wide_count = expand_weight.shape[1]
    norm_factor = 1.0 / math.sqrt(
        row_count * lon_count * lax.axis_size("lat") * lax.axis_size("lon")
    )
    score_scale = 1.0 / math.sqrt(channels // head_count)
    output_field, input_grad, block, sums = whole_step(
        norm_factor,
        score_scale,
        (state_field.transpose(1, 0, 2), cotangent.transpose(1, 0, 2), expand_weight, shrink_weight, attention_in, attention_out),
        key_bias.transpose(0, 2, 1),
        depth_weight,
        input_gain.reshape(1, channels),
        attention_gain.reshape(1, channels),
    )
    return deliver(block, sums, output_field, input_grad, channels, wide_count)


def solution(mesh):
    placed = (
        P("lat", "lon", None),
        P("lat", "lon", None),
        P("lat", "lon", None),
        P(),
        P(),
        P(),
        P(),
        P(),
        P(),
        P(),
    )
    return jax.shard_map(
        per_device,
        mesh=mesh,
        in_specs=placed,
        out_specs=(
            P("lat", "lon", None),
            P("lat", "lon", None),
            P("lat", "lon"),
            P("lat", "lon"),
            P("lat", "lon"),
            P("lat", "lon"),
            P(),
            P(),
            P(),
        ),
        check_vma=False,
    )
```

```python
import functools
import math

import jax
import jax.numpy as jnp
from jax import lax
from jax.experimental import pallas as pl
from jax.experimental.pallas import tpu as pltpu
from jax.sharding import PartitionSpec as P

EPSILON = 1e-06
CELLS = 96
MESH = pl.DeviceIdType.MESH
VMEM_MIB = 54


CHUNK = 256


def silu_parts(values):
    sigmoid = 1.0 / (1.0 + jnp.exp(-values))
    return values * sigmoid, sigmoid * (1.0 + values * (1.0 - sigmoid))


def halo_copies(rows, edges, row_slots, edge_slots, sends, recvs):
    lat, lon = lax.axis_index("lat"), lax.axis_index("lon")
    bands, sectors = lax.axis_size("lat"), lax.axis_size("lon")
    west, east = (lon + sectors - 1) % sectors, (lon + 1) % sectors

    def made(source, target, index, peer):
        return pltpu.make_async_remote_copy(
            src_ref=source,
            dst_ref=target,
            send_sem=sends.at[index],
            recv_sem=recvs.at[index],
            device_id=peer,
            device_id_type=MESH,
        )

    north, south = lat > 0, lat < bands - 1
    copies = [
        (north, south, made(rows.at[0], row_slots.at[1], 0, (lat - 1, lon))),
        (south, north, made(rows.at[1], row_slots.at[0], 1, (lat + 1, lon))),
    ]
    for side, column in ((0, west), (1, east)):
        for slot in range(3):
            step = 1 - slot
            sends_it = (None, south, north)[step]
            gets_it = (None, north, south)[step]
            copies.append(
                (
                    sends_it,
                    gets_it,
                    made(
                        edges.at[side],
                        edge_slots.at[side, slot],
                        2 + side * 3 + slot,
                        (lat + step, column),
                    ),
                )
            )
    return copies


def guarded(condition, action):
    if condition is None:
        action()
    else:
        pl.when(condition)(action)


def halo_start(copies):
    for sends_it, _, made in copies:
        guarded(sends_it, made.start)


def halo_arrive(copies):
    for _, gets_it, made in copies:
        guarded(gets_it, made.wait_recv)


def halo_leave(copies):
    for sends_it, _, made in copies:
        guarded(sends_it, made.wait_send)


def halo_greet(barrier):
    lat, lon = lax.axis_index("lat"), lax.axis_index("lon")
    bands, sectors = lax.axis_size("lat"), lax.axis_size("lon")
    west, east = (lon + sectors - 1) % sectors, (lon + 1) % sectors

    def signal(row, column):
        pl.semaphore_signal(barrier, inc=1, device_id=(row, column), device_id_type=MESH)

    signal(lat, west)
    signal(lat, east)

    @pl.when(lat > 0)
    def _():
        for column in (west, lon, east):
            signal(lat - 1, column)

    @pl.when(lat < bands - 1)
    def _():
        for column in (west, lon, east):
            signal(lat + 1, column)

    north, south = (lat + bands - 1) // bands, (2 * bands - 2 - lat) // bands
    return 2 + 3 * north + 3 * south


def edge_pair(top, bottom, last):
    sub = lax.broadcasted_iota(jnp.int32, (8, top.shape[1]), 0)
    west = jnp.where(sub == 0, top[0:1], bottom[0:1])
    east = jnp.where(sub == 0, top[last : last + 1], bottom[last : last + 1])
    return west, east


def halo_row(index, base, edge_slots, valid, lanes=slice(None)):
    slot, row = ((0, 1), (1, 0), (1, 1), (2, 0))[index]
    place = lax.broadcasted_iota(jnp.int32, base.shape, 0)
    east = edge_slots[0, slot, row : row + 1, lanes]
    west = edge_slots[1, slot, row : row + 1, lanes]
    value = jnp.where(place == valid, east, jnp.where(place == CELLS - 1, west, base))
    lat, bands = lax.axis_index("lat"), lax.axis_size("lat")
    if index == 0:
        value = jnp.where(lat > 0, value, 0.0)
    if index == 3:
        value = jnp.where(lat < bands - 1, value, 0.0)
    return value


def inside(shape, valid):
    return lax.broadcasted_iota(jnp.int32, shape, 0) < valid


def inverse_rms(values):
    return lax.rsqrt(jnp.mean(values * values, axis=-1, keepdims=True) + EPSILON)


def nt_dot(left, right):
    return lax.dot_general(
        left, right, (((1,), (1,)), ((), ())), preferred_element_type=jnp.float32
    )


class Refs:
    def __init__(self, names, refs):
        for name, ref in zip(names, refs, strict=True):
            setattr(self, name, ref)


def exchange(source, target, sends, recvs, index, peer, landing=None):
    return pltpu.make_async_remote_copy(
        src_ref=source,
        dst_ref=target,
        send_sem=sends.at[index],
        recv_sem=recvs.at[index if landing is None else landing],
        device_id=peer,
        device_id_type=MESH,
    )


class Ring:
    def __init__(self):
        lon = lax.axis_index("lon")
        z, low = lax.div(lon, 4), lax.rem(lon, 4)
        x_lo, core = lax.div(low, 2), lax.rem(low, 2)
        self.column, self.x_lo, self.core = lon, x_lo, core
        self.starts = [lax.rem(z + d, 8) * 4 for d in range(8)]
        self.sides = [self.side(low_x, low_c) for low_x in range(2) for low_c in range(2)]

    def side(self, flip_x, flip_core):
        x_lo = self.x_lo + flip_x * (1 - 2 * self.x_lo)
        core = self.core + flip_core * (1 - 2 * self.core)
        return x_lo * 2 + core

    def start(self, ring, sign):
        half = (ring + 1) // 2
        return self.starts[(sign * (4 + (half if ring % 2 == 0 else -half))) % 8]

    def partner(self, k, sign):
        return self.start(k // 4, sign) + self.sides[3 - k % 4]


def packed(cells):
    return (cells[:48] + pltpu.roll(cells[48:], 64, 1)).astype(jnp.bfloat16)


def unpacked(pair):
    lane = lax.broadcasted_iota(jnp.int32, (48, 128), 1)
    pair = pair.astype(jnp.float32)
    top = jnp.where(lane < 64, pair, 0.0)
    bottom = jnp.where(lane < 64, pltpu.roll(pair, 64, 1), 0.0)
    return jnp.concatenate([top, bottom], axis=0)


def forward_phase(r, load, valid, greetings):
    f32, bf16 = jnp.float32, jnp.bfloat16
    r.rows[...] = jnp.zeros(r.rows.shape, bf16)
    r.cot_pad[...] = jnp.zeros(r.cot_pad.shape, bf16)
    load["state"].wait()
    for i in range(2):
        r.rows[i, 0:valid, :] = r.state[:, i, :]
    west, east = edge_pair(r.rows[0].astype(f32), r.rows[1].astype(f32), valid - 1)
    r.edges[0] = west
    r.edges[1] = east
    load["cot"].wait()
    load["out"].wait()
    for i in range(2):
        r.cot_pad[i * CELLS : i * CELLS + valid, :] = r.cot[:, i, :]
    r.projected[:, 1536:2048] = nt_dot(r.cot_pad[...], r.weight_out[...]).astype(bf16)
    for i in range(2):
        value = r.rows[i].astype(f32)
        value = value * inverse_rms(value) * r.first_gain[...]
        r.normed[i * CELLS : i * CELLS + CELLS, :] = value.astype(bf16)
    load["expand"].wait()

    def own_chunk(index, carry):
        lanes = pl.ds(pl.multiple_of(index * CHUNK, CHUNK), CHUNK)
        expanded = jnp.dot(r.normed[...], r.expand[:, lanes], preferred_element_type=f32)
        activated, slope = silu_parts(expanded)
        r.slope_expanded[:, lanes] = slope.astype(bf16)
        for i in range(2):
            r.act[i + 1, :, lanes] = activated[i * CELLS : i * CELLS + CELLS].astype(bf16)
        return carry

    lax.fori_loop(0, r.expand.shape[1] // CHUNK, own_chunk, 0)
    pl.semaphore_wait(pltpu.get_barrier_semaphore(), greetings)
    copies = halo_copies(r.rows, r.edges, r.row_slots, r.edge_slots, r.state_sends, r.state_recvs)
    halo_start(copies)
    r.total[...] = jnp.zeros(r.total.shape, f32)
    r.bias_cells[...] = jnp.zeros(r.bias_cells.shape, f32)
    bias_lane = lax.broadcasted_iota(jnp.int32, (16, 128), 1)
    for i in range(2):
        r.bias_cells[i, :, 0:valid] = r.bias[i].astype(f32)
        heads = r.bias_cells[i]
        r.bias_low[i * 16 : i * 16 + 16, :] = jnp.where(bias_lane < 48, heads, 0.0)
        r.bias_high[i * 16 : i * 16 + 16, :] = jnp.where(bias_lane < 48, pltpu.roll(heads, 80, 1), 0.0)
    for a in range(3):
        r.depth[a * 3 : a * 3 + 3, :] = r.depth_low[a].astype(f32)
    load["shrink"].wait()
    halo_arrive(copies)
    far = [halo_row(row, r.row_slots[row // 3].astype(f32), r.edge_slots, valid) for row in (0, 3)]
    far = jnp.concatenate(far + [r.edge_slots[0, 1], r.edge_slots[1, 1]], axis=0)
    far = far * inverse_rms(far) * r.first_gain[...]
    r.wide_normed[...] = far.astype(bf16)

    def chunk(index, carry):
        start = pl.multiple_of(index * CHUNK, CHUNK)
        lanes = pl.ds(start, CHUNK)
        expanded = jnp.dot(r.wide_normed[...], r.expand[:, lanes], preferred_element_type=f32)
        activated = silu_parts(expanded)[0].astype(bf16)
        r.act[0, :, lanes] = activated[0:CELLS]
        r.act[3, :, lanes] = activated[CELLS : 2 * CELLS]
        activated = activated.astype(f32)
        planes = [activated[0:CELLS]]
        for i in range(2):
            base = r.act[i + 1, :, lanes].astype(f32)
            spot = lax.broadcasted_iota(jnp.int32, base.shape, 0)
            east, west = 2 * CELLS + i, 2 * CELLS + 8 + i
            plane = jnp.where(
                spot == valid,
                activated[east : east + 1],
                jnp.where(spot == CELLS - 1, activated[west : west + 1], base),
            )
            r.act[i + 1, :, lanes] = plane.astype(bf16)
            planes.append(plane)
        planes.append(activated[CELLS : 2 * CELLS])
        mixes, slopes = [], []
        for i in range(2):
            sums = []
            for b in range(3):
                part = r.depth[b : b + 1, lanes] * planes[i]
                for a in (1, 2):
                    part = part + r.depth[a * 3 + b : a * 3 + b + 1, lanes] * planes[i + a]
                sums.append(part)
            convolved = pltpu.roll(sums[0], 1, 0) + sums[1] + pltpu.roll(sums[2], CELLS - 1, 0)
            mixed, slope = silu_parts(convolved)
            keep = inside(mixed.shape, valid)
            mixes.append(jnp.where(keep, mixed, 0.0).astype(bf16))
            slope = jnp.where(keep, slope, 0.0)
            r.slope[i, :, lanes] = slope.astype(bf16)
            slopes.append(slope)
        west, east = edge_pair(slopes[0], slopes[1], valid - 1)
        r.slope_edges[0, :, lanes] = west
        r.slope_edges[1, :, lanes] = east
        mixed = jnp.concatenate(mixes, axis=0)
        r.mixed[:, lanes] = mixed
        r.total[...] += jnp.dot(
            mixed, r.shrink[pl.ds(start, CHUNK), :], preferred_element_type=f32
        )
        return carry

    lax.fori_loop(0, r.expand.shape[1] // CHUNK, chunk, 0)
    for i in range(2):
        part = slice(i * CELLS, i * CELLS + CELLS)
        inner = (r.rows[i].astype(f32) + r.total[part, :]).astype(bf16)
        r.inner[part, :] = inner
        inner = inner.astype(f32)
        r.second[part, :] = (inner * inverse_rms(inner) * r.second_gain[...]).astype(bf16)
    load["in"].wait()
    return copies


def project_and_pack(r, valid, first, last, target, with_bias):
    f32, bf16 = jnp.float32, jnp.bfloat16
    lane = lax.broadcasted_iota(jnp.int32, (CELLS, 128), 1)
    row = lax.broadcasted_iota(jnp.int32, (CELLS, 128), 0)
    for i in range(2):
        cells = slice(i * CELLS, i * CELLS + CELLS)
        for tile in range(4):
            parts = [
                r.projected[cells, base + tile * 128 : base + tile * 128 + 128].astype(f32)
                for base in (first, last)
            ]
            for u in range(4):
                item = i * 16 + tile * 4 + u
                moved = [
                    value if side == u else pltpu.roll(value, ((side - u) * 32) % 128, 1)
                    for side, value in enumerate(parts)
                ]
                value = jnp.where(lane < 32, moved[0], jnp.where(lane < 64, moved[1], 0.0))
                if with_bias:
                    value = jnp.where(row == valid, r.bias_low[item : item + 1, :], value)
                    value = jnp.where(row == valid + 1, r.bias_high[item : item + 1, :], value)
                target[item] = packed(value)


def attention_phase(r, valid, scale):
    sources = r.kv_in.shape[0]
    total = sources * CELLS
    block = r.scores.shape[1]
    group = block // CELLS
    log2e = 1.4426950408889634
    to_log2 = scale * log2e
    f32, bf16 = jnp.float32, jnp.bfloat16
    lat, lon = lax.axis_index("lat"), lax.axis_index("lon")
    groups = sources // group
    ring, own_group = r.ring, lax.div(lon, group)

    def key_copy(k, to, slot):
        return exchange(
            r.kv_out.at[to], r.kv_in.at[slot], r.kv_sends, r.kv_recvs, k, (lat, to)
        )

    def query_copy(to, slot):
        return exchange(
            r.qd_out.at[to], r.qd_in.at[slot], r.qd_sends, r.qd_recvs, to, (lat, to), slot
        )

    def near_copy(to, slot):
        return exchange(
            r.near_out.at[to], r.near_in.at[slot], r.near_sends, r.near_recvs, to, (lat, to), slot
        )

    def last_copy(k, to, slot):
        return exchange(
            r.last_out.at[to], r.last_in.at[slot], r.last_sends, r.last_recvs, k, (lat, to)
        )

    r.projected[:, 512:1536] = jnp.dot(
        r.second[...], r.weight_in[:, 512:1536], preferred_element_type=f32
    ).astype(bf16)
    project_and_pack(r, valid, 512, 1024, r.kv_out, True)

    for k in range(sources - 1):
        key_copy(k, ring.partner(k, 1), lon).start()
    r.projected[:, 0:512] = jnp.dot(
        r.second[...], r.weight_in[:, 0:512], preferred_element_type=f32
    ).astype(bf16)
    project_and_pack(r, valid, 0, 1536, r.qd_out, False)

    def push_queries(step):
        target = lax.rem(own_group + groups - step, groups) * group
        for part in range(group):
            to = target + part
            if step:
                query_copy(to, lon).start()
            else:

                @pl.when(to != lon)
                def _():
                    query_copy(to, lon).start()

    push_queries(0)
    halo = halo_copies(
        r.slope, r.slope_edges, r.slope_rows, r.slope_sides, r.slope_sends, r.slope_recvs
    )
    halo_start(halo)
    r.kv_in[lon] = r.kv_out[lon]
    r.qd_in[lon] = r.qd_out[lon]

    def prepare(index):
        raw = unpacked(r.kv_in[index])
        row = lax.broadcasted_iota(jnp.int32, (CELLS, 128), 0)
        lane = lax.broadcasted_iota(jnp.int32, (CELLS, 128), 1)
        bias_row = jnp.where(row < 48, raw[valid : valid + 1, :], raw[valid + 1 : valid + 2, :])
        wanted = jnp.where(row < 48, row, row - 48)
        bias = jnp.sum(jnp.where(wanted == lane, bias_row, 0.0), axis=1, keepdims=True) * log2e
        bias = jnp.broadcast_to(bias, (CELLS, 128))
        first = bias.astype(bf16).astype(f32)
        second = (bias - first).astype(bf16).astype(f32)
        third = bias - first - second
        first = jnp.where(row < valid, first, -1e30)
        second = jnp.where(row < valid, second, 0.0)
        third = jnp.where(row < valid, third, 0.0)
        cell = jnp.where(row < valid, raw, 0.0)
        key = jnp.where(lane < 32, cell, 0.0)
        value = jnp.where(lane >= 32, cell, 0.0)
        keys = key + pltpu.roll(key, 32, 1) + pltpu.roll(key, 64, 1)
        keys = jnp.where(lane == 96, first, keys)
        keys = jnp.where(lane == 97, second, keys)
        keys = jnp.where(lane == 98, third, keys)
        values = value + pltpu.roll(value, 96, 1)
        values = jnp.where((lane >= 64) & (lane < 67), 1.0, values)
        start = pl.multiple_of(index * CELLS, 32)
        r.kaug[pl.ds(start, CELLS), :] = keys.astype(bf16)
        r.vaug[pl.ds(start, CELLS), :] = values.astype(bf16)
        r.cell[pl.ds(start, CELLS), :] = cell

    prepare(lon)

    for part in range(8):
        first = ring.start(part, -1)

        def arrive(step, carry):
            flip_x = (step < 2).astype(jnp.int32)
            flip_core = 3 - step - 2 * flip_x
            source = first + ring.side(flip_x, flip_core)
            key_copy(part * 4 + step, source, source).wait_recv()
            prepare(source)
            return carry

        lax.fori_loop(0, 4 if part < 7 else 3, arrive, 0)

    for step in range(1, groups):
        push_queries(step)

    def turn(index, carry):
        start = pl.multiple_of(index * block, block)
        r.xt[:, pl.ds(start, block)] = r.cell[pl.ds(start, block), :].T[0:64].astype(bf16)
        r.acc[:, pl.ds(start, block)] = jnp.zeros((64, block), f32)
        return carry

    lax.fori_loop(0, total // block, turn, 0)

    def one_block(turn_index, carry):
        index = lax.rem(turn_index + own_group, groups)
        for part in range(group):
            source = index * group + part

            @pl.when(source != lon)
            def _():
                query_copy(source, source).wait_recv()

            r.qd_cell[part * CELLS : part * CELLS + CELLS, :] = unpacked(r.qd_in[source])
        xt = r.qd_cell[...].T
        query = xt[0:32] * to_log2
        first = query.astype(bf16).astype(f32)
        second = (query - first).astype(bf16).astype(f32)
        third = query - first - second
        qaug = jnp.concatenate(
            [first, second, third, jnp.ones((32, block), f32)], axis=0
        ).astype(bf16)
        t = jnp.dot(r.kaug[...], qaug, preferred_element_type=f32)
        r.scores[...] = t
        highest = jnp.max(jnp.max(t.reshape(total // 8, 8, block), axis=0), axis=0, keepdims=True)
        p = jnp.exp2(r.scores[...] - highest)
        r.scores[...] = p
        low_p = p.astype(bf16)
        r.low[...] = low_p
        norm = jnp.sum(p.reshape(total // 8, 8, block), axis=0)
        heads = jnp.dot(r.xt[32:64, :], low_p, preferred_element_type=f32)
        inverse = 1.0 / jnp.sum(norm, axis=0, keepdims=True)
        heads = heads * inverse
        back = xt[32:64]
        centred = jnp.sum(back * heads, axis=0, keepdims=True) * inverse
        back = back * inverse
        back_first = back.astype(bf16).astype(f32)
        back_second = back - back_first
        cen_first = centred.astype(bf16).astype(f32)
        cen_second = (centred - cen_first).astype(bf16).astype(f32)
        cen_third = centred - cen_first - cen_second
        sub = lax.broadcasted_iota(jnp.int32, (64, block), 0)
        cen = jnp.where(
            sub == 0,
            cen_first,
            jnp.where(sub == 1, cen_second, jnp.where(sub == 2, cen_third, 0.0)),
        )
        baug = jnp.concatenate([back_first, back_second, -cen], axis=0).astype(bf16)
        dp = jnp.dot(r.vaug[...], baug, preferred_element_type=f32)
        ds = (r.scores[...] * dp).astype(bf16)
        r.acc[32:64, :] += nt_dot(back_first.astype(bf16), r.low[...])
        r.acc[0:32, :] += nt_dot(xt[0:32].astype(bf16), ds)
        back_queries = jnp.dot(r.xt[0:32, :], ds, preferred_element_type=f32)
        zeros = jnp.zeros((64, block), f32)
        done = jnp.concatenate([back_queries * scale, heads, zeros], axis=0).T
        for part in range(group):
            source = index * group + part
            r.near_out[source] = packed(done[part * CELLS : part * CELLS + CELLS])

            @pl.when(source != lon)
            def _():
                near_copy(source, lon).start()

        return carry

    lax.fori_loop(0, groups, one_block, 0)
    r.near_in[lon] = r.near_out[lon]

    def finish(index, carry):
        start = pl.multiple_of(index * block, block)
        both = r.acc[:, pl.ds(start, block)]
        zeros = jnp.zeros((64, block), f32)
        both = jnp.concatenate([both[0:32] * scale, both[32:64], zeros], axis=0)
        r.cell[pl.ds(start, block), :] = both.T
        return carry

    lax.fori_loop(0, total // block, finish, 0)

    def pack_last(source):
        start = pl.multiple_of(source * CELLS, 32)
        r.last_out[source] = packed(r.cell[pl.ds(start, CELLS), :])

    for k in range(sources - 1):
        to = ring.partner(k, 1)
        pack_last(to)
        last_copy(k, to, lon).start()
    pack_last(lon)
    r.last_in[lon] = r.last_out[lon]

    def near_arrive():
        for k in range(sources - 1):
            source = ring.partner(k, -1)
            near_copy(source, source).wait_recv()

    def last_arrive():
        for k in range(sources - 1):
            source = ring.partner(k, -1)
            last_copy(k, source, source).wait_recv()

    def settle():
        for k in range(sources - 1):
            to = ring.partner(k, 1)
            key_copy(k, to, lon).wait_send()
            query_copy(to, lon).wait_send()
            near_copy(to, lon).wait_send()
            last_copy(k, to, lon).wait_send()

    return halo, near_arrive, last_arrive, settle


def gather_heads(source, first, second, i, tile):
    half_lane = lax.broadcasted_iota(jnp.int32, (48, 128), 1)
    parts = [source[i * 16 + tile * 4 + u].astype(jnp.float32) for u in range(4)]
    for (target, column), lane in ((first, 0), (second, 32)):
        for half in range(2):
            value = None
            for u in range(4):
                shift = (u * 32 - lane - half * 64) % 128
                moved = pltpu.roll(parts[u], shift, 1) if shift else parts[u]
                value = moved if value is None else jnp.where(half_lane < u * 32, value, moved)
            start, column_start = i * CELLS + half * 48, column + tile * 128
            target[start : start + 48, column_start : column_start + 128] = value.astype(
                jnp.bfloat16
            )


def backward_phase(r, valid, factor, slope_halo, near_arrive, last_arrive, peers):
    f32, bf16 = jnp.float32, jnp.bfloat16
    sibling, x_peers, y_peers, z_peers = peers
    lat, lon = lax.axis_index("lat"), lax.axis_index("lon")
    y = lax.rem(lat, 4)
    z, x_lo, core = lax.div(lon, 4), r.ring.x_lo, r.ring.core
    x = lax.div(lat, 4) * 2 + x_lo
    other = 1 - core
    xs, ys = [lax.rem(x + d, 4) for d in range(4)], [lax.rem(y + d, 4) for d in range(4)]
    zs = [lax.rem(z + d, 8) for d in range(8)]
    r.small[...] = jnp.zeros(r.small.shape, f32)
    near_arrive()
    for i in range(2):
        for tile in range(4):
            gather_heads(r.near_in, (r.back_project, 0), (r.heads, 0), i, tile)
    field = jnp.dot(r.heads[...], r.weight_out[...], preferred_element_type=f32)
    for i in range(2):
        part = slice(i * CELLS, i * CELLS + CELLS)
        r.field[i] = (r.inner[part, :].astype(f32) + field[part]).astype(bf16)[0:valid]
    back_second = nt_dot(r.back_project[:, 0:512], r.weight_in[:, 0:512])
    last_arrive()
    for i in range(2):
        for tile in range(4):
            gather_heads(r.last_in, (r.back_project, 512), (r.back_project, 1024), i, tile)
    back_second = back_second + nt_dot(r.back_project[:, 512:1536], r.weight_in[:, 512:1536])
    gain_two = jnp.zeros((1, field.shape[1]), f32)
    for i in range(2):
        part = slice(i * CELLS, i * CELLS + CELLS)
        inner = r.inner[part, :].astype(f32)
        inverse = inverse_rms(inner)
        gain_two = gain_two + jnp.sum(back_second[part] * inner * inverse, axis=0, keepdims=True)
        scaled = back_second[part] * r.second_gain[...]
        back = (
            r.cot_pad[part, :].astype(f32)
            + inverse * scaled
            - inverse * inverse * inverse * inner * jnp.mean(scaled * inner, axis=-1, keepdims=True)
        )
        r.back_rows[i] = back.astype(bf16)
    west, east = edge_pair(r.back_rows[0].astype(f32), r.back_rows[1].astype(f32), valid - 1)
    r.back_edges[0] = west
    r.back_edges[1] = east
    halo = halo_copies(
        r.back_rows, r.back_edges, r.back_slots, r.back_sides, r.back_sends, r.back_recvs
    )
    halo_start(halo)

    def half_lanes(top, bottom):
        lane = lax.broadcasted_iota(jnp.int32, top.shape, 1)
        even = jnp.where(lane < 64, top, pltpu.roll(bottom, 64, 1))
        odd = jnp.where(lane < 64, pltpu.roll(top, 64, 1), bottom)
        return even, odd

    def cross(left, right):
        return (
            lax.dot_general(left, right, (((0,), (0,)), ((), ())), preferred_element_type=f32)
            * factor
        )

    def core_copy(mine, theirs, first, width, index):
        rows = pl.ds(first, width)
        return exchange(
            mine.at[other, rows], theirs.at[rows], r.core_sends, r.core_recvs, index, sibling
        )

    def early_x(zz):
        return core_copy(r.ex, r.ex0, zz * 2, 2, zz)

    def early_y(zz):
        return core_copy(r.ey, r.ey0, zz * 2, 2, 4 + zz)

    def late_x(pz):
        return core_copy(r.lx, r.lx0, pz, 1, 8 + pz)

    def late_y(pz):
        return core_copy(r.ly, r.ly0, pz, 1, 16 + pz)

    def early_part(zz, carry):
        columns = pl.ds(pl.multiple_of(zz * 128, 128), 128)
        own = jnp.concatenate([r.back_rows[0, :, columns], r.back_rows[1, :, columns]], axis=0)
        shrink = cross(own, r.mixed[...])
        grad_in = cross(
            r.back_project[:, pl.ds(pl.multiple_of(zz * 384, 128), 384)], r.second[...]
        )
        grad_out = cross(r.cot_pad[:, columns], r.heads[...])
        for sub in range(8):
            pz, plo, pc = zz * 2 + sub // 4, (sub // 2) % 2, sub % 2
            for plat in range(8):
                px, py = (plat // 4) * 2 + plo, plat % 4
                part = slice(sub * 16, sub * 16 + 16)
                for side in range(2):
                    column = plat * 256 + side * 128
                    r.ex[pc, pz, px, py, side * 16 : side * 16 + 16, :] = shrink[
                        part, column : column + 128
                    ].astype(bf16)
            for pair in range(4):
                tile = slice(pair * 128, pair * 128 + 128)
                top = jnp.concatenate(
                    [grad_in[sub * 48 : sub * 48 + 24, tile], grad_out[sub * 16 : sub * 16 + 8, tile]],
                    axis=0,
                )
                bottom = jnp.concatenate(
                    [
                        grad_in[sub * 48 + 24 : sub * 48 + 48, tile],
                        grad_out[sub * 16 + 8 : sub * 16 + 16, tile],
                    ],
                    axis=0,
                )
                parts = half_lanes(top, bottom)
                for odd in range(2):
                    plat = pair * 2 + odd
                    px, py = (plat // 4) * 2 + plo, plat % 4
                    r.ey[pc, pz, py, px] = parts[odd].astype(bf16)
        early_x(zz).start()
        early_y(zz).start()
        return carry

    lax.fori_loop(0, 4, early_part, 0)

    def add_pair(mine, theirs, pz):
        for q in range(4):
            mine[core, pz, q] = (mine[core, pz, q].astype(f32) + theirs[pz, q].astype(f32)).astype(bf16)

    def early_arrive(zz, carry):
        early_x(zz).wait_recv()
        early_y(zz).wait_recv()
        for step in range(2):
            add_pair(r.ex, r.ex0, zz * 2 + step)
            add_pair(r.ey, r.ey0, zz * 2 + step)
        return carry

    lax.fori_loop(0, 4, early_arrive, 0)
    count = [0]

    def copy(source, target, peer):
        index = count[0]
        count[0] += 1
        made = exchange(source, target, r.sends, r.recvs, index, peer)
        made.start()
        return made

    def stage_one(mine, slots, targets, turns):
        return [
            copy(mine.at[core, :, turns[d]], slots.at[d - 1], targets[d - 1])
            for d in (1, 2, 3)
        ]

    early_one_x = stage_one(r.ex, r.ex1, x_peers, xs)
    early_one_y = stage_one(r.ey, r.ey1, y_peers, ys)
    halo_arrive(slope_halo)
    halo_arrive(halo)
    for row in range(4):
        base = r.back_rows[row - 1] if row in (1, 2) else r.back_slots[row // 3]
        value = halo_row(row, base.astype(f32), r.back_sides, valid)
        r.wide_back[row * CELLS : row * CELLS + CELLS, :] = value.astype(bf16)
    r.back_normed[...] = jnp.zeros(r.back_normed.shape, f32)

    def chunk(pz, carry):
        start = pl.multiple_of(pz * CHUNK, CHUNK)
        lanes = pl.ds(start, CHUNK)
        product = nt_dot(r.wide_back[...], r.shrink[lanes, :])
        planes = []
        for row in range(4):
            base = r.slope[row - 1, :, lanes] if row in (1, 2) else r.slope_rows[row // 3, :, lanes]
            slope = halo_row(row, base.astype(f32), r.slope_sides, valid, lanes)
            plane = product[row * CELLS : row * CELLS + CELLS] * slope
            planes.append(plane.astype(bf16).astype(f32))
        for b in range(3):
            turned = []
            for i in range(2):
                centre = planes[i + 1]
                centre = jnp.where(inside(centre.shape, valid), centre, 0.0)
                turned.append(pltpu.roll(centre, (CELLS + b - 1) % CELLS, 0) if b != 1 else centre)
            for a in range(3):
                value = r.act[a, :, lanes].astype(f32) * turned[0]
                value = value + r.act[a + 1, :, lanes].astype(f32) * turned[1]
                r.small[a * 3 + b : a * 3 + b + 1, lanes] = (
                    jnp.sum(value, axis=0, keepdims=True) * factor
                )
        outs = []
        for i in range(2):
            sums = []
            for b in range(3):
                part = r.depth[b : b + 1, lanes] * planes[i + 2]
                for a in (1, 2):
                    part = part + r.depth[a * 3 + b : a * 3 + b + 1, lanes] * planes[i + 2 - a]
                sums.append(part)
            total = pltpu.roll(sums[0], CELLS - 1, 0) + sums[1] + pltpu.roll(sums[2], 1, 0)
            total = total * r.slope_expanded[i * CELLS : i * CELLS + CELLS, lanes].astype(f32)
            outs.append(jnp.where(inside(total.shape, valid), total, 0.0).astype(bf16))
        back = jnp.concatenate(outs, axis=0)
        r.back_normed[...] += nt_dot(back, r.expand[:, lanes])
        grad = cross(back, r.normed[...])
        for sub in range(4):
            plo, pc = sub // 2, sub % 2
            for pair in range(4):
                tile = slice(pair * 128, pair * 128 + 128)
                parts = half_lanes(
                    grad[sub * 64 : sub * 64 + 32, tile], grad[sub * 64 + 32 : sub * 64 + 64, tile]
                )
                for odd in range(2):
                    plat = pair * 2 + odd
                    px, py = (plat // 4) * 2 + plo, plat % 4
                    r.lx[pc, pz, px, py] = parts[odd][0:16].astype(bf16)
                    r.ly[pc, pz, py, px] = parts[odd][16:32].astype(bf16)
        late_x(pz).start()
        late_y(pz).start()
        return carry

    lax.fori_loop(0, 8, chunk, 0)
    gain_one = jnp.zeros((1, r.back_normed.shape[1]), f32)
    for i in range(2):
        part = slice(i * CELLS, i * CELLS + valid)
        state = r.rows[i, 0:valid, :].astype(f32)
        inverse = inverse_rms(state)
        back = r.back_normed[part, :]
        gain_one = gain_one + jnp.sum(back * state * inverse, axis=0, keepdims=True)
        scaled = back * r.first_gain[...]
        r.grad[i] = (
            r.back_rows[i, 0:valid, :].astype(f32)
            + inverse * scaled
            - inverse * inverse * inverse * state * jnp.mean(scaled * state, axis=-1, keepdims=True)
        ).astype(bf16)
    width = r.small.shape[1]
    r.small[9:10, :] = jnp.concatenate(
        [gain_one * factor, gain_two * factor, jnp.zeros((1, width - 1024), f32)], axis=1
    )
    for tile in range(16):
        for part in range(2):
            r.small_split[tile * 2 + part] = r.small[
                part * 8 : part * 8 + 8, tile * 128 : tile * 128 + 128
            ]
    sectors, bands = r.small_lon.shape[0], r.small_lat.shape[0]
    columns = [(r.ring.partner(k, 1), r.ring.partner(k, -1)) for k in range(sectors - 1)]

    def scatter(k, to, slot):
        return exchange(
            r.small_split.at[to], r.small_lon.at[slot], r.small_sends, r.small_recvs, k, (lat, to)
        )

    def spread(k, to, slot):
        return exchange(
            r.sums.at[lon], r.sums.at[slot], r.spread_sends, r.spread_recvs, k, (lat, to)
        )

    for k, (to, _) in enumerate(columns):
        scatter(k, to, lon).start()
    r.small_lon[lon] = r.small_split[lon]

    def late_arrive(pz, carry):
        late_x(pz).wait_recv()
        late_y(pz).wait_recv()
        add_pair(r.lx, r.lx0, pz)
        add_pair(r.ly, r.ly0, pz)
        return carry

    lax.fori_loop(0, 8, late_arrive, 0)
    late_one_x = stage_one(r.lx, r.lx1, x_peers, xs)
    late_one_y = stage_one(r.ly, r.ly1, y_peers, ys)

    def add_four(mine, theirs, here, total):
        def body(pz, carry):
            value = mine[core, pz, here].astype(f32)
            for d in range(3):
                value = value + theirs[d, pz].astype(f32)
            total[pz] = value.astype(bf16)
            return carry

        lax.fori_loop(0, 8, body, 0)

    def stage_two(arrivals, mine, slots, here, total, next_slots, targets, turns):
        for made in arrivals:
            made.wait_recv()
        add_four(mine, slots, here, total)
        return [
            copy(total.at[:, turns[d]], next_slots.at[d - 1], targets[d - 1])
            for d in (1, 2, 3)
        ]

    early_two_x = stage_two(early_one_x, r.ex, r.ex1, x, r.ext, r.ex2, y_peers, ys)
    early_two_y = stage_two(early_one_y, r.ey, r.ey1, y, r.eyt, r.ey2, x_peers, xs)

    def stage_three(arrivals, total, slots, here, first, count_rows):
        for made in arrivals:
            made.wait_recv()

        def body(pz, carry):
            value = total[pz, here].astype(f32)
            for d in range(3):
                value = value + slots[d, pz].astype(f32)
            r.final[pz, first : first + count_rows, :] = value.astype(bf16)
            return carry

        lax.fori_loop(0, 8, body, 0)

    def send_final(first, count_rows):
        rows = pl.ds(first, count_rows)
        return [
            copy(r.final.at[zs[d], rows], r.final_in.at[d - 1, rows], z_peers[d - 1])
            for d in range(1, 8)
        ]

    stage_three(early_two_x, r.ext, r.ex2, y, 0, 32)
    stage_three(early_two_y, r.eyt, r.ey2, x, 32, 32)
    final_early = send_final(0, 64)
    late_two_x = stage_two(late_one_x, r.lx, r.lx1, x, r.lxt, r.lx2, y_peers, ys)
    late_two_y = stage_two(late_one_y, r.ly, r.ly1, y, r.lyt, r.ly2, x_peers, xs)

    for k, (_, source) in enumerate(columns):
        scatter(k, source, source).wait_recv()
    total = r.small_lon[0]
    for index in range(1, sectors):
        total = total + r.small_lon[index]
    r.small_lat[lat] = total
    small_lat = [
        copy(r.small_lat.at[lat], r.small_lat.at[lat], (lax.rem(lat + d, bands), lon))
        for d in range(1, bands)
    ]

    stage_three(late_two_x, r.lxt, r.lx2, y, 64, 16)
    stage_three(late_two_y, r.lyt, r.ly2, x, 80, 16)
    final_late = send_final(64, 32)

    for made in small_lat:
        made.wait_recv()
    total = r.small_lat[0]
    for index in range(1, bands):
        total = total + r.small_lat[index]
    r.sums[lon] = total
    for k, (to, _) in enumerate(columns):
        spread(k, to, lon).start()

    for made in final_early + final_late:
        made.wait_recv()
    value = r.final[z].astype(f32)
    for d in range(7):
        value = value + r.final_in[d].astype(f32)
    r.block[...] = value
    for k, (to, source) in enumerate(columns):
        spread(k, source, source).wait_recv()
        spread(k, to, lon).wait_send()
        scatter(k, to, lon).wait_send()
    for made in (
        early_one_x
        + early_one_y
        + late_one_x
        + late_one_y
        + early_two_x
        + early_two_y
        + late_two_x
        + late_two_y
        + final_early
        + final_late
        + small_lat
    ):
        made.wait_send()

    def settle(pz, carry):
        late_x(pz).wait_send()
        late_y(pz).wait_send()
        return carry

    def settle_early(zz, carry):
        early_x(zz).wait_send()
        early_y(zz).wait_send()
        return carry

    lax.fori_loop(0, 8, settle, 0)
    lax.fori_loop(0, 4, settle_early, 0)
    halo_leave(halo)


def step_kernel(names, valid, scale, factor, *refs):
    r = Refs(names, refs)
    lat, lon = lax.axis_index("lat"), lax.axis_index("lon")
    sectors = lax.axis_size("lon")
    y, z, core = lax.rem(lat, 4), lax.div(lon, 4), lax.rem(lon, 2)
    x = lax.div(lat, 4) * 2 + lax.rem(lax.div(lon, 2), 2)

    def place(px, py, pz, pc):
        return (lax.div(px, 2) * 4 + py, pz * 4 + lax.rem(px, 2) * 2 + pc)

    barrier = pltpu.get_barrier_semaphore()
    peers = (
        place(x, y, z, 1 - core),
        [place(lax.rem(x + d, 4), y, z, core) for d in range(1, 4)],
        [place(x, lax.rem(y + d, 4), z, core) for d in range(1, 4)],
        [place(x, y, lax.rem(z + d, 8), core) for d in range(1, 8)],
    )
    greetings = halo_greet(barrier)
    bands = lax.axis_size("lat")
    band_peers = [(lax.rem(lat + d, bands), lon) for d in range(1, bands)]
    for peer in peers[1] + peers[2] + band_peers:
        pl.semaphore_signal(barrier, inc=1, device_id=peer, device_id_type=MESH)

    r.ring = Ring()
    for k in range(sectors - 1):
        pl.semaphore_signal(
            barrier, inc=1, device_id=(lat, r.ring.partner(k, 1)), device_id_type=MESH
        )
    greetings = greetings + len(peers[1]) + len(peers[2]) + bands - 1 + sectors - 1
    load = {}
    for index, (name, source, target) in enumerate(
        (
            ("state", r.state_hbm, r.state),
            ("cot", r.cot_hbm, r.cot),
            ("out", r.out_hbm, r.weight_out),
            ("expand", r.expand_hbm, r.expand),
            ("shrink", r.shrink_hbm, r.shrink),
            ("in", r.in_hbm, r.weight_in),
        )
    ):
        load[name] = pltpu.make_async_copy(source, target, r.loads.at[index])
        load[name].start()
    state_halo = forward_phase(r, load, valid, greetings)
    slope_halo, near_arrive, last_arrive, settle = attention_phase(r, valid, scale)
    backward_phase(r, valid, factor, slope_halo, near_arrive, last_arrive, peers)
    settle()
    halo_leave(state_halo)
    halo_leave(slope_halo)


def whole_step(factor, scale, operands, bias, depth, first_gain, second_gain):
    f32, bf16 = jnp.float32, jnp.bfloat16
    state, cot, expand, shrink, weight_in, weight_out = operands
    valid = state.shape[0]
    channels, wide = expand.shape
    cells = 2 * CELLS
    sources = lax.axis_size("lon")
    total, block = sources * CELLS, 768
    vmem, dma = pltpu.VMEM, pltpu.SemaphoreType.DMA
    message = vmem((sources, 48, 128), bf16)

    def tree(name, rows):
        return {
            name: vmem((2, 8, 4, 4, rows, 128), bf16),
            name + "0": vmem((8, 4, 4, rows, 128), bf16),
            name + "1": vmem((3, 8, 4, rows, 128), bf16),
            name + "t": vmem((8, 4, rows, 128), bf16),
            name + "2": vmem((3, 8, rows, 128), bf16),
        }

    def halo_set(prefix, width):
        return {prefix + "sends": dma((8,)), prefix + "recvs": dma((8,))}

    scratch = {
        "state": vmem(state.shape, bf16),
        "cot": vmem(cot.shape, bf16),
        "expand": vmem(expand.shape, bf16),
        "shrink": vmem(shrink.shape, bf16),
        "weight_in": vmem(weight_in.shape, bf16),
        "weight_out": vmem(weight_out.shape, bf16),
        "bias_cells": vmem((2, 16, 128), f32),
        "bias_low": vmem((32, 128), f32),
        "bias_high": vmem((32, 128), f32),
        "depth": vmem((16, wide), f32),
        "rows": vmem((2, CELLS, channels), bf16),
        "edges": vmem((2, 8, channels), f32),
        "row_slots": vmem((2, CELLS, channels), bf16),
        "edge_slots": vmem((2, 3, 8, channels), f32),
        "back_rows": vmem((2, CELLS, channels), bf16),
        "back_edges": vmem((2, 8, channels), f32),
        "back_slots": vmem((2, CELLS, channels), bf16),
        "back_sides": vmem((2, 3, 8, channels), f32),
        "slope": vmem((2, CELLS, wide), bf16),
        "slope_edges": vmem((2, 8, wide), f32),
        "slope_rows": vmem((2, CELLS, wide), bf16),
        "slope_sides": vmem((2, 3, 8, wide), f32),
        "wide_normed": vmem((2 * CELLS + 16, channels), bf16),
        "wide_back": vmem((4 * CELLS, channels), bf16),
        "total": vmem((cells, channels), f32),
        "back_normed": vmem((cells, channels), f32),
        "projected": vmem((cells, 4 * channels), bf16),
        "back_project": vmem((cells, 3 * channels), bf16),
        "heads": vmem((cells, channels), bf16),
        "cot_pad": vmem((cells, channels), bf16),
        "act": vmem((4, CELLS, wide), bf16),
        "slope_expanded": vmem((cells, wide), bf16),
        "mixed": vmem((cells, wide), bf16),
        "normed": vmem((cells, channels), bf16),
        "inner": vmem((cells, channels), bf16),
        "second": vmem((cells, channels), bf16),
        "kv_out": message,
        "kv_in": message,
        "qd_out": message,
        "qd_in": message,
        "near_out": message,
        "near_in": message,
        "last_out": message,
        "last_in": message,
        "xt": vmem((64, total), bf16),
        "kaug": vmem((total, 128), bf16),
        "vaug": vmem((total, 128), bf16),
        "scores": vmem((total, block), f32),
        "low": vmem((total, block), bf16),
        "acc": vmem((64, total), f32),
        "cell": vmem((total, 128), f32),
        "qd_cell": vmem((block, 128), f32),
        **tree("ex", 32),
        **tree("ey", 32),
        **tree("lx", 16),
        **tree("ly", 16),
        "final": vmem((8, 96, 128), bf16),
        "final_in": vmem((7, 96, 128), bf16),
        "small": vmem((16, wide), f32),
        "small_split": vmem((sources, 8, 128), f32),
        "small_lon": vmem((sources, 8, 128), f32),
        "small_lat": vmem((lax.axis_size("lat"), 8, 128), f32),
        "loads": dma((6,)),
        "core_sends": dma((24,)),
        "core_recvs": dma((24,)),
        "sends": dma((66,)),
        "recvs": dma((66,)),
    }
    for prefix in ("state_", "slope_", "back_"):
        scratch[prefix + "sends"] = dma((8,))
        scratch[prefix + "recvs"] = dma((8,))
    for prefix in ("kv_", "qd_", "near_", "last_", "small_", "spread_"):
        scratch[prefix + "sends"] = dma((sources,))
        scratch[prefix + "recvs"] = dma((sources,))
    inputs = [name + "_hbm" for name in ("state", "cot", "expand", "shrink", "in", "out")]
    inputs += ["bias", "depth_low", "first_gain", "second_gain"]
    outputs = {
        "field": ((2, valid, channels), bf16),
        "grad": ((2, valid, channels), bf16),
        "block": ((96, 128), f32),
        "sums": ((sources, 8, 128), f32),
    }
    names = inputs + list(outputs) + list(scratch)
    whole, anywhere = pl.BlockSpec(memory_space=vmem), pl.BlockSpec(memory_space=pl.ANY)
    return pl.pallas_call(
        functools.partial(step_kernel, names, valid, scale, factor),
        out_shape=tuple(jax.ShapeDtypeStruct(*kind) for kind in outputs.values()),
        in_specs=[anywhere] * 6 + [whole] * 4,
        out_specs=(whole,) * 4,
        scratch_shapes=list(scratch.values()),
        compiler_params=pltpu.CompilerParams(
            vmem_limit_bytes=VMEM_MIB * 1024 * 1024, collective_id=1, has_side_effects=True
        ),
        name="step",
    )(*operands, bias, depth, first_gain, second_gain)


def deliver_kernel(
    block_hbm,
    sums_hbm,
    field_hbm,
    grad_hbm,
    expand_ref,
    shrink_ref,
    in_ref,
    out_ref,
    depth_ref,
    one_ref,
    two_ref,
    field_out,
    grad_out,
    block_ref,
    sums_ref,
    field_ref,
    grad_ref,
    loads,
):
    pairs = (
        (block_hbm, block_ref),
        (sums_hbm, sums_ref),
        (field_hbm, field_ref),
        (grad_hbm, grad_ref),
    )
    copies = [
        pltpu.make_async_copy(source, target, loads.at[index])
        for index, (source, target) in enumerate(pairs)
    ]
    for made in copies:
        made.start()
    for made in copies:
        made.wait()
    for source, target in ((field_ref, field_out), (grad_ref, grad_out)):
        for i in range(2):
            target[:, i, :] = source[i]

    def unfold(part):
        return jnp.concatenate([part, pltpu.roll(part, 64, 1)], axis=0)

    block = block_ref[...]
    expand = unfold(block[64:96])
    expand = jnp.concatenate([expand, jnp.zeros_like(expand)], axis=0).T
    expand_ref[...] = expand[0:64, 0:64]
    shrink_ref[:, 0:128] = block[0:16]
    shrink_ref[:, 128:256] = block[16:32]
    in_ref[...] = unfold(block[32:56])[:, 0:64]
    out_ref[...] = unfold(block[56:64])[:, 0:64]
    for tile in range(16):
        lanes = slice(tile * 128, tile * 128 + 128)
        low, high = sums_ref[tile * 2], sums_ref[tile * 2 + 1]
        depth_ref[0, :, lanes] = low[0:3]
        depth_ref[1, :, lanes] = low[3:6]
        depth_ref[2, 0:2, lanes] = low[6:8]
        depth_ref[2, 2:3, lanes] = high[0:1]
        if tile < 4:
            one_ref[:, lanes] = high[1:2]
        elif tile < 8:
            two_ref[:, tile * 128 - 512 : tile * 128 - 384] = high[1:2]


def deliver(block, sums, field, grad, channels, wide):
    vmem = pl.BlockSpec(memory_space=pltpu.VMEM)
    shapes = [(64, 64), (16, 256), (48, 64), (16, 64), (3, 3, wide), (1, channels), (1, channels)]
    turned = jax.ShapeDtypeStruct((field.shape[1], 2, channels), field.dtype)
    expand, shrink, grad_in, grad_out, depth, one, two, field, grad = pl.pallas_call(
        deliver_kernel,
        out_shape=tuple(jax.ShapeDtypeStruct(shape, jnp.float32) for shape in shapes)
        + (turned, turned),
        in_specs=[pl.BlockSpec(memory_space=pl.ANY)] * 4,
        out_specs=(vmem,) * 9,
        scratch_shapes=[
            pltpu.VMEM(value.shape, value.dtype) for value in (block, sums, field, grad)
        ]
        + [pltpu.SemaphoreType.DMA((4,))],
        compiler_params=pltpu.CompilerParams(vmem_limit_bytes=54 * 1024 * 1024),
        name="deliver",
    )(block, sums, field, grad)
    field, grad = field.transpose(1, 0, 2), grad.transpose(1, 0, 2)
    one, two = one.reshape(channels), two.reshape(channels)
    return field, grad, expand, shrink.T, grad_in.T, grad_out.T, depth, one, two


def per_device(
    state_field,
    cotangent,
    key_bias,
    input_gain,
    expand_weight,
    depth_weight,
    shrink_weight,
    attention_gain,
    attention_in,
    attention_out,
):
    row_count, lon_count, channels = state_field.shape
    head_count = key_bias.shape[2]
    wide_count = expand_weight.shape[1]
    norm_factor = 1.0 / math.sqrt(
        row_count * lon_count * lax.axis_size("lat") * lax.axis_size("lon")
    )
    score_scale = 1.0 / math.sqrt(channels // head_count)
    output_field, input_grad, block, sums = whole_step(
        norm_factor,
        score_scale,
        (state_field.transpose(1, 0, 2), cotangent.transpose(1, 0, 2), expand_weight, shrink_weight, attention_in, attention_out),
        key_bias.transpose(0, 2, 1),
        depth_weight,
        input_gain.reshape(1, channels),
        attention_gain.reshape(1, channels),
    )
    return deliver(block, sums, output_field, input_grad, channels, wide_count)


def solution(mesh):
    placed = (
        P("lat", "lon", None),
        P("lat", "lon", None),
        P("lat", "lon", None),
        P(),
        P(),
        P(),
        P(),
        P(),
        P(),
        P(),
    )
    return jax.shard_map(
        per_device,
        mesh=mesh,
        in_specs=placed,
        out_specs=(
            P("lat", "lon", None),
            P("lat", "lon", None),
            P("lat", "lon"),
            P("lat", "lon"),
            P("lat", "lon"),
            P("lat", "lon"),
            P(),
            P(),
            P(),
        ),
        check_vma=False,
    )
```
